32 devices in a mesh: wide: 8 (over z, y), narrow: 4 (over x, core).
Axes of the slice: x: 2, y: 2, z: 4, core: 2. Of those that a mesh axis runs over, the one named last changes fastest.
Arguments:
- source_old: float32 [512, 1024], P(None, ('wide', 'narrow')), may hold values from -90 to 90
- reaction_old: float32 [512, 1024], P(None, ('wide', 'narrow')), may hold values from 0.5 to 4
- new_place: int32 [1024], P(('wide', 'narrow')), may hold values from 0 to 127, as said below
Outputs:
- solution: float32 [512, 1024], P(None, ('wide', 'narrow'))
- strong_residual: float32 [512, 1024], P(None, ('wide', 'narrow'))
The draws below stay inside these ranges and needn't reach their ends.
Inputs may be any that keep to these rules, and one draw needn't show every extreme that they name: Within the 128 rows of each index of wide, new_place is a permutation of 0 to 127: the row goes to the device of the same index of wide whose index of narrow is new_place // 32, as its element new_place % 32. The rows of one device send at most 16 elements to one device, and every device sends exactly 16 to some device.
All inputs are finite; a program needn't handle non-finite values.
Results may differ from the reference program's by a relative error of at most 0.0001.
Values sent between devices are 32-bit elements; how exact they have to be, the bound alone decides.
No kernel may reach another device: no remote copies, remote signals or barrier semaphores. Data moves between devices by JAX's collectives and lax.ppermute only.
A program may use at most 64 MiB of HBM per device.

```python
import math
import jax
import jax.numpy as jnp
import numpy as np
from jax import lax

NP = 8
PTS = 512
BX = 2
BY = 4
EZ = 4
ITERS = 2
LOC = 32
NELX = 16
NELY = 16
GROUP = 128
ELEMS = 1024
N_WIDE = 8
N_NARROW = 4


def group_places(subkey):
    owners = N_NARROW
    average = LOC // N_NARROW
    subkeys = jax.random.split(subkey, 5)
    owner_order = jax.random.permutation(subkeys[0], owners)
    levels = jax.random.randint(subkeys[1], (owners,), 0, average + 1)
    peak_at = jax.random.randint(subkeys[2], (), 0, owners)
    levels = levels.at[peak_at].set(average).at[(peak_at + owners - 1) % owners].set(0)
    shifts = levels - jnp.roll(levels, 1)
    counts = average + shifts[(owner_order[None, :] - owner_order[:, None]) % owners]

    def one_order(order_key):
        return jax.random.permutation(order_key, LOC)
    row_orders = jax.vmap(one_order)(jax.random.split(subkeys[3], owners))
    slot_orders = jax.vmap(one_order)(jax.random.split(subkeys[4], owners))
    seg_ends = jnp.cumsum(counts, axis=1)
    seg_starts = seg_ends - counts
    position = jnp.arange(LOC, dtype=jnp.int32)
    owner_of = jnp.sum((seg_ends[:, None, :] <= position[None, :, None]).astype(jnp.int32), axis=2)
    within = position[None, :] - jnp.take_along_axis(seg_starts, owner_of, axis=1)
    offsets = jnp.cumsum(counts, axis=0) - counts
    base_off = jnp.take_along_axis(offsets, owner_of, axis=1)
    slot_of = slot_orders[owner_of, base_off + within]
    placed = owner_of * LOC + slot_of
    places = jnp.zeros((owners, LOC), jnp.int32).at[jnp.arange(owners)[:, None], row_orders].set(placed)
    return places.reshape(-1)


def draw_new_place(key, part):
    subkeys = jax.random.split(jax.random.fold_in(key, 7), N_WIDE)
    return jax.vmap(group_places)(subkeys).reshape(-1).astype(jnp.int32)


def draw_source_old(key, part):
    subkeys = jax.random.split(jax.random.fold_in(key, 11), 3)
    rowpos = jnp.arange(ELEMS, dtype=jnp.float32) / (ELEMS - 1)
    elem_scale = 10.0 ** jax.random.uniform(subkeys[0], (ELEMS,), jnp.float32)
    point_scale = 10.0 ** jax.random.uniform(subkeys[1], (PTS, 1), jnp.float32)
    noise_part = jnp.clip(jax.random.normal(subkeys[2], (PTS, ELEMS), jnp.float32), -4.0, 4.0)
    values = noise_part * point_scale * elem_scale[None, :] * jnp.sqrt(1.0 + 2.0 * rowpos[None, :]) / 10.0
    return values.astype(jnp.float32)


def steps_of(stream_key, shape, pieces, smallest, high):
    def one(dim, blocks):
        steps = jax.random.uniform(jax.random.fold_in(jax.random.fold_in(stream_key, 6), dim), (blocks,), jnp.float32, smallest / len(pieces), high / len(pieces))
        return jnp.repeat(jnp.exp(steps), shape[dim] // blocks).reshape((-1,) + (1,) * (len(shape) - dim - 1))

    factor_of = one(*pieces[0])
    for cut in pieces[1:]:
        factor_of = factor_of * one(*cut)
    return factor_of


def setup_inputs(seed: int = 0) -> dict:
    arg_keys = jax.random.split(jax.random.key(seed), 4)
    return {
        "source_old": draw_source_old(jax.random.fold_in(arg_keys[3], 71), 0),
        "reaction_old": jnp.clip(jnp.exp(math.log(4.0) - 2.0794415 * jax.random.uniform(arg_keys[1], (PTS, ELEMS), jnp.float32) ** steps_of(arg_keys[1], (PTS, ELEMS), ((1, 32),), -0.2, 0.2)), 0.5, 4.0),
        "new_place": draw_new_place(jax.random.fold_in(arg_keys[3], 71), 0),
    }


DIFFUSION = 0.05


def legendre_values(abscissa, num_points):
    columns = [np.ones(abscissa.shape), abscissa]
    for degree in range(2, num_points):
        columns.append(((2 * degree - 1) * abscissa * columns[degree - 1] - (degree - 1) * columns[degree - 2]) / degree)
    return np.stack(columns, 1)


def gll_tables(num_points):
    poly_order = num_points - 1
    abscissa = np.cos(np.pi * np.arange(num_points) / poly_order)
    for newton_step in range(60):
        legendre = legendre_values(abscissa, num_points)
        abscissa = abscissa - (abscissa * legendre[:, poly_order] - legendre[:, poly_order - 1]) / (num_points * legendre[:, poly_order])
    legendre = legendre_values(abscissa, num_points)
    top_values = legendre[:, poly_order][::-1]
    abscissa = abscissa[::-1]
    weights = 2.0 / (poly_order * num_points * top_values ** 2)
    identity = np.eye(num_points)
    differ = np.where(identity > 0, 1.0, abscissa[:, None] - abscissa[None, :])
    deriv_table = np.where(identity > 0, 0.0, top_values[:, None] / (top_values[None, :] * differ))
    quarter = poly_order * num_points / 4.0
    edge_fix = np.concatenate([np.array([-quarter]), np.zeros(num_points - 2), np.array([quarter])])
    deriv_table = deriv_table + identity * edge_fix[:, None]
    return weights, deriv_table


def local_tables():
    weights, deriv_table = gll_tables(NP)
    mass_table = weights[:, None, None] * weights[None, :, None] * weights[None, None, :]
    return jnp.asarray(deriv_table, jnp.float32), jnp.asarray(mass_table, jnp.float32)


def apply_local(values, reaction, deriv_table, mass_table):
    highest = lax.Precision.HIGHEST
    slope_x = jnp.einsum("ai,ijke->ajke", deriv_table, values, precision=highest)
    slope_y = jnp.einsum("bj,ijke->ibke", deriv_table, values, precision=highest)
    slope_z = jnp.einsum("ck,ijke->ijce", deriv_table, values, precision=highest)
    scaled = DIFFUSION * mass_table[..., None]
    result = jnp.einsum("ai,ajke->ijke", deriv_table, scaled * slope_x, precision=highest)
    result = result + jnp.einsum("bj,ibke->ijke", deriv_table, scaled * slope_y, precision=highest)
    result = result + jnp.einsum("ck,ijce->ijke", deriv_table, scaled * slope_z, precision=highest)
    return result + reaction * mass_table[..., None] * values


def share_axis(values, point_axis, elem_axis):
    last_axis = values.ndim - 1
    turned = jnp.moveaxis(values, (point_axis, elem_axis), (0, last_axis))
    upper_face = turned[-1]
    lower_face = turned[0]
    shared = upper_face[..., :-1] + lower_face[..., 1:]
    upper_new = jnp.concatenate([shared, upper_face[..., -1:]], axis=-1)
    lower_new = jnp.concatenate([lower_face[..., :1], shared], axis=-1)
    turned = turned.at[-1].set(upper_new).at[0].set(lower_new)
    return jnp.moveaxis(turned, (0, last_axis), (point_axis, elem_axis))


def assemble(values):
    eight_dims = values.reshape(NP, NP, NP, N_WIDE, N_NARROW, BX, BY, EZ)
    box = jnp.transpose(eight_dims, (0, 1, 2, 3, 5, 4, 6, 7)).reshape(NP, NP, NP, NELX, NELY, EZ)
    box = share_axis(box, 0, 3)
    box = share_axis(box, 1, 4)
    box = share_axis(box, 2, 5)
    eight_dims = box.reshape(NP, NP, NP, N_WIDE, BX, N_NARROW, BY, EZ)
    return jnp.transpose(eight_dims, (0, 1, 2, 3, 5, 4, 6, 7)).reshape(NP, NP, NP, ELEMS)


def reference(source_old, reaction_old, new_place):
    group_len = GROUP
    row_ids = jnp.arange(ELEMS, dtype=jnp.int32)
    target = (row_ids // group_len) * group_len + new_place
    source = jnp.zeros_like(source_old).at[:, target].set(source_old)
    reaction = jnp.zeros_like(reaction_old).at[:, target].set(reaction_old)
    deriv_table, mass_table = local_tables()
    grid_shape = (NP, NP, NP, ELEMS)
    source4 = source.reshape(grid_shape)
    reaction4 = reaction.reshape(grid_shape)
    mass_four = mass_table[..., None]
    weight = 1.0 / assemble(jnp.ones(grid_shape, jnp.float32))
    rhs = assemble(mass_four * source4)
    solution = jnp.zeros(grid_shape, jnp.float32)
    residual = rhs
    direction = rhs
    norm_now = jnp.sum(weight * residual * residual)
    for iteration in range(ITERS):
        applied = assemble(apply_local(direction, reaction4, deriv_table, mass_table))
        step_len = norm_now / jnp.sum(weight * direction * applied)
        solution = solution + step_len * direction
        residual = residual - step_len * applied
        if iteration + 1 < ITERS:
            norm_next = jnp.sum(weight * residual * residual)
            direction = residual + (norm_next / norm_now) * direction
            norm_now = norm_next
    strong = residual * weight / mass_four
    return solution.reshape(PTS, ELEMS), strong.reshape(PTS, ELEMS)
```

```python
import functools

import jax
import jax.numpy as jnp
import numpy as np
from jax import lax
from jax.experimental import pallas as pl
from jax.experimental.pallas import tpu as pltpu
from jax.sharding import PartitionSpec as P

NP = 8
BX = 2
BY = 4
EZ = 4
PTS = NP**3
PLANE = NP * NP
LANES = 128
HALF = PLANE // 2
XSTEP = BY * EZ

DIFFUSION = 0.05


def legendre_values(abscissa, num_points):
    columns = [np.ones(abscissa.shape), abscissa]
    for degree in range(2, num_points):
        columns.append(
            ((2 * degree - 1) * abscissa * columns[degree - 1] - (degree - 1) * columns[degree - 2])
            / degree
        )
    return np.stack(columns, 1)


def gll_tables(num_points):
    poly_order = num_points - 1
    abscissa = np.cos(np.pi * np.arange(num_points) / poly_order)
    for newton_step in range(60):
        legendre = legendre_values(abscissa, num_points)
        abscissa = abscissa - (abscissa * legendre[:, poly_order] - legendre[:, poly_order - 1]) / (
            num_points * legendre[:, poly_order]
        )
    legendre = legendre_values(abscissa, num_points)
    top_values = legendre[:, poly_order][::-1]
    abscissa = abscissa[::-1]
    weights = 2.0 / (poly_order * num_points * top_values**2)
    identity = np.eye(num_points)
    differ = np.where(identity > 0, 1.0, abscissa[:, None] - abscissa[None, :])
    deriv_table = np.where(identity > 0, 0.0, top_values[:, None] / (top_values[None, :] * differ))
    quarter = poly_order * num_points / 4.0
    edge_fix = np.concatenate([np.array([-quarter]), np.zeros(num_points - 2), np.array([quarter])])
    deriv_table = deriv_table + identity * edge_fix[:, None]
    return (weights, deriv_table)


def stiffness():
    weights, deriv = gll_tables(NP)
    stiff = DIFFUSION * deriv.T @ np.diag(weights) @ deriv
    return weights, 0.5 * (stiff + stiff.T)


WEIGHTS, STIFF = stiffness()
EVEN = 0.5 * (STIFF[:4, :4] + STIFF[:4, 7:3:-1])
ODD = 0.5 * (STIFF[:4, :4] - STIFF[:4, 7:3:-1])


def apply_stiff(f):
    even = [f[j] + f[7 - j] for j in range(4)]
    odd = [f[j] - f[7 - j] for j in range(4)]
    out = [None] * NP
    for i in range(4):
        e = sum_of([float(EVEN[i, j]) * even[j] for j in range(4)])
        o = sum_of([float(ODD[i, j]) * odd[j] for j in range(4)])
        out[i] = e + o
        out[7 - i] = e - o
    return out


def sum_of(terms):
    while len(terms) > 1:
        terms = [
            terms[k] + terms[k + 1] if k + 1 < len(terms) else terms[k]
            for k in range(0, len(terms), 2)
        ]
    return terms[0]


class Grid:
    def __init__(self, lanes, wide):
        self.lanes = lanes
        self.wide = wide
        self.lane = lax.broadcasted_iota(jnp.int32, (NP, lanes), 1)
        self.row = lax.broadcasted_iota(jnp.int32, (NP, lanes), 0)
        self.s = self.lane & (EZ - 1)
        self.j = (self.lane // EZ) & (BY - 1)
        self.i = (self.lane // XSTEP) & (BX - 1)
        self.lower = self.i == 0
        w = jnp.full((NP, lanes), float(WEIGHTS[0]), jnp.float32)
        for c in range(1, NP):
            w = jnp.where(self.row == c, float(WEIGHTS[c]), w)
        self.w = w

    def has_neighbour(self):
        u = lax.axis_index("wide")
        low = jnp.where(u > 0, 1, 0)
        high = jnp.where(u < self.wide - 1, 1, 0)
        return jnp.where(self.lower, low, high) > 0

    def roll(self, x, shift):
        return pltpu.roll(x, shift % self.lanes, axis=x.ndim - 1)

    def share(self, lo, hi, axis):
        if axis == "x":
            new_lo = lo + jnp.where(self.lower, 0.0, self.roll(hi, XSTEP))
            new_hi = hi + jnp.where(self.lower, self.roll(lo, -XSTEP), 0.0)
        elif axis == "y":
            block = BX * XSTEP
            jump = block - (BY - 1) * EZ
            from_hi = jnp.where(self.j > 0, self.roll(hi, EZ), self.roll(hi, jump))
            from_lo = jnp.where(self.j < BY - 1, self.roll(lo, -EZ), self.roll(lo, -jump))
            first = (self.j == 0) & (self.lane < block)
            last = (self.j == BY - 1) & (self.lane >= self.lanes - block)
            new_lo = lo + jnp.where(first, 0.0, from_hi)
            new_hi = hi + jnp.where(last, 0.0, from_lo)
        else:
            new_lo = lo + jnp.where(self.s > 0, self.roll(hi, 1), 0.0)
            new_hi = hi + jnp.where(self.s < EZ - 1, self.roll(lo, -1), 0.0)
        return new_lo, new_hi

    def assemble(self, ref):
        for b in range(NP):
            lo, hi = rows(0, b), rows(NP - 1, b)
            ref[lo, :], ref[hi, :] = self.share(ref[lo, :], ref[hi, :], "x")
        for a in range(NP):
            lo, hi = rows(a, 0), rows(a, NP - 1)
            ref[lo, :], ref[hi, :] = self.share(ref[lo, :], ref[hi, :], "y")
        for a in range(NP):
            lo, hi = self.share(column(ref, PLANE * a), column(ref, PLANE * a + NP - 1), "z")
            put_column(ref, PLANE * a, lo)
            put_column(ref, PLANE * a + NP - 1, hi)

    def plane_product(self, f_ref, base, out_ref):
        z = apply_stiff([column(f_ref, base + c) for c in range(NP)])
        for c in range(NP):
            put_column(out_ref, c, self.w * z[c])
        y = apply_stiff([f_ref[pl.ds(base + NP * b, NP), :] for b in range(NP)])
        return [self.w * y[b] + out_ref[pl.ds(NP * b, NP), :] for b in range(NP)]

    def local(self, f_ref, reaction_ref, out_ref, tmp_ref):
        for a in range(NP):
            flat = self.plane_product(f_ref, PLANE * a, tmp_ref)
            wa = float(WEIGHTS[a])
            for b in range(NP):
                r = rows(a, b)
                mass = (wa * float(WEIGHTS[b])) * self.w
                out_ref[r, :] = wa * flat[b] + (reaction_ref[r, :] * mass) * f_ref[r, :]
        for b in range(NP):
            x = apply_stiff([f_ref[rows(a, b), :] for a in range(NP)])
            wb = float(WEIGHTS[b]) * self.w
            for a in range(NP):
                r = rows(a, b)
                out_ref[r, :] = out_ref[r, :] + wb * x[a]

    def count_weights(self):
        nb = self.has_neighbour()
        one = jnp.ones((NP, self.lanes), jnp.float32)
        x0 = jnp.where(~self.lower | nb, 0.5, one)
        x7 = jnp.where(self.lower | nb, 0.5, one)
        block = BX * XSTEP
        first = (self.j == 0) & (self.lane < block)
        last = (self.j == BY - 1) & (self.lane >= self.lanes - block)
        y0 = jnp.where(first, one, 0.5)
        y7 = jnp.where(last, one, 0.5)
        z = jnp.where((self.row == 0) & (self.s > 0), 0.5, one)
        z = jnp.where((self.row == NP - 1) & (self.s < EZ - 1), 0.5, z)
        zx = [z * x0, z, z * x7]
        return [[m * y0, m, m * y7] for m in zx]


def place(a):
    return 0 if a == 0 else (2 if a == NP - 1 else 1)


def rows(a, b):
    return pl.ds(PLANE * a + NP * b, NP)


def column(ref, start):
    if ref.shape[1] == LANES:
        return ref[pl.ds(start, NP, stride=NP), :]
    return jnp.concatenate([ref[pl.ds(start + NP * b, 1), :] for b in range(NP)], axis=0)


def put_column(ref, start, value):
    if ref.shape[1] == LANES:
        ref[pl.ds(start, NP, stride=NP), :] = value
    else:
        for b in range(NP):
            ref[pl.ds(start + NP * b, 1), :] = value[b : b + 1, :]


def pack_face(grid, face, write):
    u = lax.axis_index("wide")
    even = (u % 2) == 0
    for b in range(NP // 2):
        top, bottom = face[b], face[b + NP // 2]
        up = jnp.where(grid.lower, grid.roll(bottom, -XSTEP), top)
        down = jnp.where(grid.lower, top, grid.roll(bottom, XSTEP))
        write(b, jnp.where(even, up, down), jnp.where(even, down, up))


def unpack_face(grid, read_a, read_b, nb):
    u = lax.axis_index("wide")
    even = (u % 2) == 0
    tops, bottoms = [], []
    for b in range(NP // 2):
        first, second = read_a(b), read_b(b)
        from_up = jnp.where(even, first, second)
        from_down = jnp.where(even, second, first)
        top = jnp.where(grid.lower, grid.roll(from_down, -XSTEP), grid.roll(from_up, XSTEP))
        bottom = jnp.where(grid.lower, from_down, from_up)
        tops.append(jnp.where(nb, top, 0.0))
        bottoms.append(jnp.where(nb, bottom, 0.0))
    return tops + bottoms


def pack_kernel(source_ref, reaction_ref, place_ref, out_ref):
    v = lax.axis_index("narrow")
    per = source_ref.shape[1]
    groups = LANES // per
    block = PTS // groups
    shift = (v % groups) * per
    for k, ref in enumerate((source_ref, reaction_ref)):
        dense = jnp.concatenate([ref[block * g : block * (g + 1), :] for g in range(groups)], axis=1)
        out_ref[block * k : block * (k + 1), :] = pltpu.roll(dense, shift, axis=1)
    row = lax.broadcasted_iota(jnp.int32, (NP, LANES), 0)
    lane = lax.broadcasted_iota(jnp.int32, (NP, LANES), 1)
    position = row * LANES + lane
    owner = jnp.zeros((NP, LANES), jnp.int32)
    for col in range(per):
        owner = jnp.where(position == place_ref[col], v * per + (col + 1), owner)
    out_ref[2 * block : 2 * block + NP, :] = owner.astype(jnp.float32)


def first_kernel(per, narrow, wide, got_ref, rhs_ref, reaction_ref, msg_a_ref, msg_b_ref, owner_ref):
    groups = LANES // per
    block = PTS // groups
    lanes = per * narrow
    grid = Grid(lanes, wide)
    total = got_ref[0, 2 * block : 2 * block + NP, :]
    for v in range(1, narrow):
        total = total + got_ref[v, 2 * block : 2 * block + NP, :]
    owner_ref[...] = total.astype(jnp.int32) - 1
    lane = lax.broadcasted_iota(jnp.int32, (NP, LANES), 1)
    tiles = []
    for t in range(lanes // LANES):
        owner = jnp.broadcast_to(owner_ref[t : t + 1, :], (NP, LANES))
        tiles.append((owner // per, owner % per))
    spot = lane // per
    for m in range(groups):
        idx = [per * ((v + m) % groups) + col for v, col in tiles]
        for k, ref in enumerate((rhs_ref, reaction_ref)):
            for r in range(block // NP):
                where_in = pl.ds(block * k + NP * r, NP)
                picks = []
                for h in range(narrow // groups):
                    pick = got_ref[groups * h + (0 - m) % groups, where_in, :]
                    for g in range(1, groups):
                        pick = jnp.where(
                            spot == g, got_ref[groups * h + (g - m) % groups, where_in, :], pick
                        )
                    picks.append(pick)
                at = block * m + NP * r
                a, b = at // PLANE, (at % PLANE) // NP
                for t, (v, col) in enumerate(tiles):
                    value = jnp.take_along_axis(picks[0], idx[t], axis=1)
                    for h in range(1, narrow // groups):
                        other = jnp.take_along_axis(picks[h], idx[t], axis=1)
                        value = jnp.where(v // groups == h, other, value)
                    if k == 0:
                        mass = float(WEIGHTS[a]) * float(WEIGHTS[b])
                        value = value * (mass * grid.w[:, t * LANES : (t + 1) * LANES])
                    ref[pl.ds(at, NP), t * LANES : (t + 1) * LANES] = value
    grid.assemble(rhs_ref)

    def write(part):
        def put(b, first, second):
            msg_a_ref[pl.ds(part * HALF + NP * b, NP), :] = first
            msg_b_ref[pl.ds(part * HALF + NP * b, NP), :] = second

        return put

    last = NP - 1
    pack_face(
        grid,
        [jnp.where(grid.lower, rhs_ref[rows(0, b), :], rhs_ref[rows(last, b), :]) for b in range(NP)],
        write(0),
    )
    part = []
    for b in range(NP):
        f = [rhs_ref[rows(a, b), :] for a in range(NP)]
        low = sum_of([float(STIFF[0, a]) * f[a] for a in range(1, NP)])
        high = sum_of([float(STIFF[last, a]) * f[a] for a in range(last)])
        part.append((float(WEIGHTS[b]) * grid.w) * jnp.where(grid.lower, low, high))
    pack_face(grid, part, write(1))
    pack_face(
        grid,
        [
            jnp.where(grid.lower, reaction_ref[rows(0, b), :], reaction_ref[rows(last, b), :])
            for b in range(NP)
        ],
        write(2),
    )


def second_kernel(
    wide,
    rhs_ref,
    reaction_ref,
    got_a_ref,
    got_b_ref,
    v0_ref,
    v1_ref,
    v2_ref,
    msg_a_ref,
    msg_b_ref,
    sums_ref,
    face_ref,
    tmp_ref,
):
    lanes = rhs_ref.shape[1]
    grid = Grid(lanes, wide)
    nb = grid.has_neighbour()
    last = NP - 1

    def reader(part):
        def first(b):
            return got_a_ref[pl.ds(part * HALF + NP * b, NP), :]

        def second(b):
            return got_b_ref[pl.ds(part * HALF + NP * b, NP), :]

        return first, second

    extra = unpack_face(grid, *reader(0), nb)
    v0_ref[...] = rhs_ref[...]
    for b in range(NP):
        low = rhs_ref[rows(0, b), :] + jnp.where(grid.lower, extra[b], 0.0)
        high = rhs_ref[rows(last, b), :] + jnp.where(grid.lower, 0.0, extra[b])
        v0_ref[rows(0, b), :] = low
        v0_ref[rows(last, b), :] = high
        face_ref[pl.ds(NP * b, NP), :] = jnp.where(grid.lower, low, high)
    grid.local(v0_ref, reaction_ref, v1_ref, tmp_ref)
    flat = grid.plane_product(face_ref, 0, tmp_ref)
    slopes = unpack_face(grid, *reader(1), nb)
    reactions = unpack_face(grid, *reader(2), nb)
    for b in range(NP):
        wb = float(WEIGHTS[b]) * grid.w
        face = face_ref[pl.ds(NP * b, NP), :]
        own = float(WEIGHTS[0]) * flat[b] + wb * (
            float(STIFF[0, 0]) * face + (float(WEIGHTS[0]) * reactions[b]) * face
        )
        more = jnp.where(nb, slopes[b] + own, 0.0)
        low, high = rows(0, b), rows(last, b)
        v1_ref[low, :] = v1_ref[low, :] + jnp.where(grid.lower, more, 0.0)
        v1_ref[high, :] = v1_ref[high, :] + jnp.where(grid.lower, 0.0, more)
    grid.assemble(v1_ref)
    grid.local(v1_ref, reaction_ref, v2_ref, tmp_ref)
    weight = grid.count_weights()
    parts = [[], [], [], []]
    for a in range(NP):
        terms = [[], [], [], []]
        for b in range(NP):
            r = rows(a, b)
            v0, v1, v2 = v0_ref[r, :], v1_ref[r, :], v2_ref[r, :]
            wt = weight[place(a)][place(b)]
            w1 = wt * v1
            for t, value in zip(terms, ((wt * v0) * v0, w1 * v0, w1 * v1, v1 * v2)):
                t.append(value)
        for p, t in zip(parts, terms):
            p.append(sum_of(t))
    row = grid.row
    out = jnp.zeros((NP, lanes), jnp.float32)
    for k, p in enumerate(parts):
        total = jnp.sum(sum_of(p), axis=0, keepdims=True)
        out = jnp.where(row == k, jnp.broadcast_to(total, (NP, lanes)), out)
    sums_ref[...] = out
    grid.assemble(v2_ref)

    def write(b, first, second):
        msg_a_ref[pl.ds(NP * b, NP), :] = first
        msg_b_ref[pl.ds(NP * b, NP), :] = second

    pack_face(
        grid,
        [jnp.where(grid.lower, v2_ref[rows(0, b), :], v2_ref[rows(last, b), :]) for b in range(NP)],
        write,
    )


def last_kernel(
    per, wide, v0_ref, v1_ref, v2_ref, got_a_ref, got_b_ref, sums_ref, solution_ref, strong_ref
):
    lanes = v0_ref.shape[1]
    grid = Grid(lanes, wide)
    nb = grid.has_neighbour()
    last = NP - 1
    v = lax.axis_index("narrow")
    shift = (lanes - v * per) % lanes
    extra = unpack_face(
        grid,
        lambda b: got_a_ref[pl.ds(NP * b, NP), :],
        lambda b: got_b_ref[pl.ds(NP * b, NP), :],
        nb,
    )
    g = [jnp.sum(sums_ref[k : k + 1, :], axis=1, keepdims=True) for k in range(4)]
    alpha = g[0] / g[1]
    norm = g[0] - 2.0 * alpha * g[1] + (alpha * alpha) * g[2]
    beta = norm / g[0]
    one = 1.0 + beta
    curve = one * one * g[1] - 2.0 * one * alpha * g[2] + (alpha * alpha) * g[3]
    step = norm / curve
    first = jnp.broadcast_to(alpha + step * one, (NP, lanes))
    second = jnp.broadcast_to(alpha * step, (NP, lanes))
    weight = grid.count_weights()
    inverse = 1.0 / grid.w
    weight = [[w * inverse for w in line] for line in weight]
    for a in range(NP):
        for b in range(NP):
            r = rows(a, b)
            v0, v1, v2 = v0_ref[r, :], v1_ref[r, :], v2_ref[r, :]
            if a == 0:
                v2 = v2 + jnp.where(grid.lower, extra[b], 0.0)
            if a == last:
                v2 = v2 + jnp.where(grid.lower, 0.0, extra[b])
            out = first * v0 - second * v1
            left = v0 - first * v1 + second * v2
            scale = float(1.0 / (WEIGHTS[a] * WEIGHTS[b]))
            left = left * (scale * weight[place(a)][place(b)])
            solution_ref[r, :] = pltpu.roll(out, shift, axis=1)[:, :per]
            strong_ref[r, :] = pltpu.roll(left, shift, axis=1)[:, :per]


VM = pl.BlockSpec(memory_space=pltpu.VMEM)
SM = pl.BlockSpec(memory_space=pltpu.SMEM)


def call(kernel, out_shapes, in_specs, scratch=(), name=None):
    return pl.pallas_call(
        kernel,
        out_shape=[jax.ShapeDtypeStruct(s, jnp.float32) for s in out_shapes],
        in_specs=in_specs,
        out_specs=[VM] * len(out_shapes),
        scratch_shapes=list(scratch),
        compiler_params=pltpu.CompilerParams(vmem_limit_bytes=16 * 1024 * 1024),
        name=name,
    )


def exchange(first, second, wide):
    pairs = [(u, u ^ 1) for u in range(wide)]
    across = [(u, min(max(u + 1 if u % 2 else u - 1, 0), wide - 1)) for u in range(wide)]
    return lax.ppermute(first, "wide", pairs), lax.ppermute(second, "wide", across)


def reduce_wide(sums, wide):
    if wide & (wide - 1):
        return lax.psum(sums, "wide")
    hop = 1
    while hop < wide:
        sums = sums + lax.ppermute(sums, "wide", [(u, u ^ hop) for u in range(wide)])
        hop *= 2
    return sums


def local(wide, narrow, source_old, reaction_old, new_place):
    per = source_old.shape[1]
    lanes = per * narrow
    packed = call(pack_kernel, [(2 * PTS * per // LANES + NP, LANES)], [VM, VM, SM], name="pack")(
        source_old, reaction_old, new_place
    )[0]
    got = lax.all_gather(packed, "narrow")
    full = (PTS, lanes)
    rhs, reaction, msg_a, msg_b = call(
        functools.partial(first_kernel, per, narrow, wide),
        [full, full, (3 * HALF, lanes), (3 * HALF, lanes)],
        [VM],
        [pltpu.VMEM((NP, LANES), jnp.int32)],
        name="first",
    )(got)
    got_a, got_b = exchange(msg_a, msg_b, wide)
    v0, v1, v2, msg_a, msg_b, sums = call(
        functools.partial(second_kernel, wide),
        [full, full, full, (HALF, lanes), (HALF, lanes), (NP, lanes)],
        [VM] * 4,
        [pltpu.VMEM((PLANE, lanes), jnp.float32), pltpu.VMEM((PLANE, lanes), jnp.float32)],
        name="second",
    )(rhs, reaction, got_a, got_b)
    got_a, got_b = exchange(msg_a, msg_b, wide)
    sums = reduce_wide(sums, wide)
    return tuple(
        call(
            functools.partial(last_kernel, per, wide),
            [(PTS, per), (PTS, per)],
            [VM] * 6,
            name="last",
        )(v0, v1, v2, got_a, got_b, sums)
    )


def solution(mesh):
    placed = (P(None, ("wide", "narrow")), P(None, ("wide", "narrow")), P(("wide", "narrow")))
    return jax.shard_map(
        functools.partial(local, mesh.shape["wide"], mesh.shape["narrow"]),
        mesh=mesh,
        in_specs=placed,
        out_specs=(P(None, ("wide", "narrow")), P(None, ("wide", "narrow"))),
        check_vma=False,
    )
```

```python
import functools

import jax
import jax.numpy as jnp
import numpy as np
from jax import lax
from jax.experimental import pallas as pl
from jax.experimental.pallas import tpu as pltpu
from jax.sharding import PartitionSpec as P

NP = 8
BX = 2
BY = 4
EZ = 4
PTS = NP**3
PLANE = NP * NP
LANES = 128
HALF = PLANE // 2
XSTEP = BY * EZ

DIFFUSION = 0.05


def legendre_values(abscissa, num_points):
    columns = [np.ones(abscissa.shape), abscissa]
    for degree in range(2, num_points):
        columns.append(
            ((2 * degree - 1) * abscissa * columns[degree - 1] - (degree - 1) * columns[degree - 2])
            / degree
        )
    return np.stack(columns, 1)


def gll_tables(num_points):
    poly_order = num_points - 1
    abscissa = np.cos(np.pi * np.arange(num_points) / poly_order)
    for newton_step in range(60):
        legendre = legendre_values(abscissa, num_points)
        abscissa = abscissa - (abscissa * legendre[:, poly_order] - legendre[:, poly_order - 1]) / (
            num_points * legendre[:, poly_order]
        )
    legendre = legendre_values(abscissa, num_points)
    top_values = legendre[:, poly_order][::-1]
    abscissa = abscissa[::-1]
    weights = 2.0 / (poly_order * num_points * top_values**2)
    identity = np.eye(num_points)
    differ = np.where(identity > 0, 1.0, abscissa[:, None] - abscissa[None, :])
    deriv_table = np.where(identity > 0, 0.0, top_values[:, None] / (top_values[None, :] * differ))
    quarter = poly_order * num_points / 4.0
    edge_fix = np.concatenate([np.array([-quarter]), np.zeros(num_points - 2), np.array([quarter])])
    deriv_table = deriv_table + identity * edge_fix[:, None]
    return (weights, deriv_table)


def stiffness():
    weights, deriv = gll_tables(NP)
    stiff = DIFFUSION * deriv.T @ np.diag(weights) @ deriv
    return weights, 0.5 * (stiff + stiff.T)


WEIGHTS, STIFF = stiffness()
EVEN = 0.5 * (STIFF[:4, :4] + STIFF[:4, 7:3:-1])
ODD = 0.5 * (STIFF[:4, :4] - STIFF[:4, 7:3:-1])


def apply_stiff(f):
    even = [f[j] + f[7 - j] for j in range(4)]
    odd = [f[j] - f[7 - j] for j in range(4)]
    out = [None] * NP
    for i in range(4):
        e = sum_of([float(EVEN[i, j]) * even[j] for j in range(4)])
        o = sum_of([float(ODD[i, j]) * odd[j] for j in range(4)])
        out[i] = e + o
        out[7 - i] = e - o
    return out


def sum_of(terms):
    while len(terms) > 1:
        terms = [
            terms[k] + terms[k + 1] if k + 1 < len(terms) else terms[k]
            for k in range(0, len(terms), 2)
        ]
    return terms[0]


class Grid:
    def __init__(self, lanes, wide):
        self.lanes = lanes
        self.wide = wide
        self.lane = lax.broadcasted_iota(jnp.int32, (NP, lanes), 1)
        self.row = lax.broadcasted_iota(jnp.int32, (NP, lanes), 0)
        self.s = self.lane & (EZ - 1)
        self.j = (self.lane // EZ) & (BY - 1)
        self.i = (self.lane // XSTEP) & (BX - 1)
        self.lower = self.i == 0
        w = jnp.full((NP, lanes), float(WEIGHTS[0]), jnp.float32)
        for c in range(1, NP):
            w = jnp.where(self.row == c, float(WEIGHTS[c]), w)
        self.w = w

    def has_neighbour(self):
        u = lax.axis_index("wide")
        low = jnp.where(u > 0, 1, 0)
        high = jnp.where(u < self.wide - 1, 1, 0)
        return jnp.where(self.lower, low, high) > 0

    def roll(self, x, shift):
        return pltpu.roll(x, shift % self.lanes, axis=x.ndim - 1)

    def share(self, lo, hi, axis):
        if axis == "x":
            new_lo = lo + jnp.where(self.lower, 0.0, self.roll(hi, XSTEP))
            new_hi = hi + jnp.where(self.lower, self.roll(lo, -XSTEP), 0.0)
        elif axis == "y":
            block = BX * XSTEP
            jump = block - (BY - 1) * EZ
            from_hi = jnp.where(self.j > 0, self.roll(hi, EZ), self.roll(hi, jump))
            from_lo = jnp.where(self.j < BY - 1, self.roll(lo, -EZ), self.roll(lo, -jump))
            first = (self.j == 0) & (self.lane < block)
            last = (self.j == BY - 1) & (self.lane >= self.lanes - block)
            new_lo = lo + jnp.where(first, 0.0, from_hi)
            new_hi = hi + jnp.where(last, 0.0, from_lo)
        else:
            new_lo = lo + jnp.where(self.s > 0, self.roll(hi, 1), 0.0)
            new_hi = hi + jnp.where(self.s < EZ - 1, self.roll(lo, -1), 0.0)
        return new_lo, new_hi

    def assemble(self, ref):
        for b in range(NP):
            lo, hi = rows(0, b), rows(NP - 1, b)
            ref[lo, :], ref[hi, :] = self.share(ref[lo, :], ref[hi, :], "x")
        for a in range(NP):
            lo, hi = rows(a, 0), rows(a, NP - 1)
            ref[lo, :], ref[hi, :] = self.share(ref[lo, :], ref[hi, :], "y")
        for a in range(NP):
            lo, hi = self.share(column(ref, PLANE * a), column(ref, PLANE * a + NP - 1), "z")
            put_column(ref, PLANE * a, lo)
            put_column(ref, PLANE * a + NP - 1, hi)

    def plane_product(self, f_ref, base, out_ref):
        z = apply_stiff([column(f_ref, base + c) for c in range(NP)])
        for c in range(NP):
            put_column(out_ref, c, self.w * z[c])
        y = apply_stiff([f_ref[pl.ds(base + NP * b, NP), :] for b in range(NP)])
        return [self.w * y[b] + out_ref[pl.ds(NP * b, NP), :] for b in range(NP)]

    def local(self, f_ref, reaction_ref, out_ref, tmp_ref):
        for a in range(NP):
            flat = self.plane_product(f_ref, PLANE * a, tmp_ref)
            wa = float(WEIGHTS[a])
            for b in range(NP):
                r = rows(a, b)
                mass = (wa * float(WEIGHTS[b])) * self.w
                out_ref[r, :] = wa * flat[b] + (reaction_ref[r, :] * mass) * f_ref[r, :]
        for b in range(NP):
            x = apply_stiff([f_ref[rows(a, b), :] for a in range(NP)])
            wb = float(WEIGHTS[b]) * self.w
            for a in range(NP):
                r = rows(a, b)
                out_ref[r, :] = out_ref[r, :] + wb * x[a]

    def count_weights(self):
        nb = self.has_neighbour()
        one = jnp.ones((NP, self.lanes), jnp.float32)
        x0 = jnp.where(~self.lower | nb, 0.5, one)
        x7 = jnp.where(self.lower | nb, 0.5, one)
        block = BX * XSTEP
        first = (self.j == 0) & (self.lane < block)
        last = (self.j == BY - 1) & (self.lane >= self.lanes - block)
        y0 = jnp.where(first, one, 0.5)
        y7 = jnp.where(last, one, 0.5)
        z = jnp.where((self.row == 0) & (self.s > 0), 0.5, one)
        z = jnp.where((self.row == NP - 1) & (self.s < EZ - 1), 0.5, z)
        zx = [z * x0, z, z * x7]
        return [[m * y0, m, m * y7] for m in zx]


def place(a):
    return 0 if a == 0 else (2 if a == NP - 1 else 1)


def rows(a, b):
    return pl.ds(PLANE * a + NP * b, NP)


def column(ref, start):
    if ref.shape[1] == LANES:
        return ref[pl.ds(start, NP, stride=NP), :]
    return jnp.concatenate([ref[pl.ds(start + NP * b, 1), :] for b in range(NP)], axis=0)


def put_column(ref, start, value):
    if ref.shape[1] == LANES:
        ref[pl.ds(start, NP, stride=NP), :] = value
    else:
        for b in range(NP):
            ref[pl.ds(start + NP * b, 1), :] = value[b : b + 1, :]


def pack_face(grid, face, write):
    u = lax.axis_index("wide")
    even = (u % 2) == 0
    for b in range(NP // 2):
        top, bottom = face[b], face[b + NP // 2]
        up = jnp.where(grid.lower, grid.roll(bottom, -XSTEP), top)
        down = jnp.where(grid.lower, top, grid.roll(bottom, XSTEP))
        write(b, jnp.where(even, up, down), jnp.where(even, down, up))


def unpack_face(grid, read_a, read_b, nb):
    u = lax.axis_index("wide")
    even = (u % 2) == 0
    tops, bottoms = [], []
    for b in range(NP // 2):
        first, second = read_a(b), read_b(b)
        from_up = jnp.where(even, first, second)
        from_down = jnp.where(even, second, first)
        top = jnp.where(grid.lower, grid.roll(from_down, -XSTEP), grid.roll(from_up, XSTEP))
        bottom = jnp.where(grid.lower, from_down, from_up)
        tops.append(jnp.where(nb, top, 0.0))
        bottoms.append(jnp.where(nb, bottom, 0.0))
    return tops + bottoms


def pack_kernel(source_ref, reaction_ref, place_ref, out_ref, near_ref, sems):
    per = source_ref.shape[0]
    blocks = 2 * (PTS // LANES)
    places = pltpu.make_async_copy(place_ref, near_ref, sems.at[blocks])
    places.start()
    copies = []
    for k, ref in enumerate((source_ref, reaction_ref)):
        for q in range(PTS // LANES):
            n = len(copies)
            copy = pltpu.make_async_copy(
                ref.at[:, pl.ds(q * LANES, LANES)], out_ref.at[pl.ds(per * n, per), :], sems.at[n]
            )
            copy.start()
            copies.append(copy)
    v = lax.axis_index("narrow")
    groups = LANES // per
    row = lax.broadcasted_iota(jnp.int32, (NP, LANES), 0)
    lane = lax.broadcasted_iota(jnp.int32, (NP, LANES), 1)
    mine = (row == v // groups) & (lane // per == v % groups)
    places.wait()
    places = jnp.concatenate([near_ref[...].astype(jnp.float32)] * groups, axis=1)
    out_ref[per * blocks :, :] = jnp.where(mine, jnp.broadcast_to(places, (NP, LANES)), 0.0)
    for copy in copies:
        copy.wait()


def first_kernel(per, narrow, wide, got_ref, rhs_ref, reaction_ref, msg_a_ref, msg_b_ref):
    lanes = per * narrow
    tiles = lanes // LANES
    groups = LANES // per
    blocks = PTS // LANES
    grid = Grid(lanes, wide)
    spot = lax.broadcasted_iota(jnp.int32, (LANES, lanes), 1).astype(jnp.float32)
    row = lax.broadcasted_iota(jnp.int32, (LANES, lanes), 0)
    places = sum_of([got_ref[v, 2 * blocks * per :, :] for v in range(narrow)])
    came = jnp.zeros((1, lanes), jnp.float32)
    for t in range(tiles):
        new = jnp.transpose(jnp.broadcast_to(places[t : t + 1, :], (LANES, LANES)))
        new = jnp.concatenate([new] * tiles, axis=1)
        old = (row + t * LANES).astype(jnp.float32)
        came = came + jnp.sum(jnp.where(new == spot, old, 0.0), axis=0, keepdims=True)
    came = jnp.broadcast_to(came.astype(jnp.int32), (NP, lanes))
    for k, out_ref in enumerate((rhs_ref, reaction_ref)):
        for q in range(blocks):
            block = pl.ds(per * (blocks * k + q), per)
            old = [
                jnp.transpose(
                    jnp.concatenate([got_ref[groups * t + g, block, :] for g in range(groups)], axis=0)
                )
                for t in range(tiles)
            ]
            for r in range(LANES // NP):
                at = q * LANES + NP * r
                a, b = at // PLANE, (at % PLANE) // NP
                for t in range(tiles):
                    owner = came[:, t * LANES : (t + 1) * LANES]
                    value = None
                    for h in range(tiles):
                        pick = jnp.take_along_axis(
                            old[h][NP * r : NP * (r + 1), :], owner % LANES, axis=1
                        )
                        value = pick if value is None else jnp.where(owner // LANES == h, pick, value)
                    if k == 0:
                        mass = float(WEIGHTS[a]) * float(WEIGHTS[b])
                        value = value * (mass * grid.w[:, t * LANES : (t + 1) * LANES])
                    out_ref[pl.ds(at, NP), t * LANES : (t + 1) * LANES] = value
    grid.assemble(rhs_ref)

    def write(part):
        def put(b, first, second):
            msg_a_ref[pl.ds(part * HALF + NP * b, NP), :] = first
            msg_b_ref[pl.ds(part * HALF + NP * b, NP), :] = second

        return put

    last = NP - 1
    pack_face(
        grid,
        [jnp.where(grid.lower, rhs_ref[rows(0, b), :], rhs_ref[rows(last, b), :]) for b in range(NP)],
        write(0),
    )
    part = []
    for b in range(NP):
        f = [rhs_ref[rows(a, b), :] for a in range(NP)]
        low = sum_of([float(STIFF[0, a]) * f[a] for a in range(1, NP)])
        high = sum_of([float(STIFF[last, a]) * f[a] for a in range(last)])
        part.append((float(WEIGHTS[b]) * grid.w) * jnp.where(grid.lower, low, high))
    pack_face(grid, part, write(1))
    pack_face(
        grid,
        [
            jnp.where(grid.lower, reaction_ref[rows(0, b), :], reaction_ref[rows(last, b), :])
            for b in range(NP)
        ],
        write(2),
    )


def second_kernel(
    wide,
    rhs_ref,
    reaction_ref,
    got_a_ref,
    got_b_ref,
    v0_ref,
    v1_ref,
    v2_ref,
    msg_a_ref,
    msg_b_ref,
    face_ref,
    tmp_ref,
):
    lanes = rhs_ref.shape[1]
    grid = Grid(lanes, wide)
    nb = grid.has_neighbour()
    last = NP - 1

    def reader(part):
        def first(b):
            return got_a_ref[pl.ds(part * HALF + NP * b, NP), :]

        def second(b):
            return got_b_ref[pl.ds(part * HALF + NP * b, NP), :]

        return first, second

    extra = unpack_face(grid, *reader(0), nb)
    v0_ref[...] = rhs_ref[...]
    for b in range(NP):
        low = rhs_ref[rows(0, b), :] + jnp.where(grid.lower, extra[b], 0.0)
        high = rhs_ref[rows(last, b), :] + jnp.where(grid.lower, 0.0, extra[b])
        v0_ref[rows(0, b), :] = low
        v0_ref[rows(last, b), :] = high
        face_ref[pl.ds(NP * b, NP), :] = jnp.where(grid.lower, low, high)
    grid.local(v0_ref, reaction_ref, v1_ref, tmp_ref)
    flat = grid.plane_product(face_ref, 0, tmp_ref)
    slopes = unpack_face(grid, *reader(1), nb)
    reactions = unpack_face(grid, *reader(2), nb)
    for b in range(NP):
        wb = float(WEIGHTS[b]) * grid.w
        face = face_ref[pl.ds(NP * b, NP), :]
        own = float(WEIGHTS[0]) * flat[b] + wb * (
            float(STIFF[0, 0]) * face + (float(WEIGHTS[0]) * reactions[b]) * face
        )
        more = jnp.where(nb, slopes[b] + own, 0.0)
        low, high = rows(0, b), rows(last, b)
        v1_ref[low, :] = v1_ref[low, :] + jnp.where(grid.lower, more, 0.0)
        v1_ref[high, :] = v1_ref[high, :] + jnp.where(grid.lower, 0.0, more)
    grid.assemble(v1_ref)
    grid.local(v1_ref, reaction_ref, v2_ref, tmp_ref)
    weight = grid.count_weights()
    parts = [[], [], [], []]
    for a in range(NP):
        terms = [[], [], [], []]
        for b in range(NP):
            r = rows(a, b)
            v0, v1, v2 = v0_ref[r, :], v1_ref[r, :], v2_ref[r, :]
            wt = weight[place(a)][place(b)]
            w1 = wt * v1
            for t, value in zip(terms, ((wt * v0) * v0, w1 * v0, w1 * v1, v1 * v2)):
                t.append(value)
        for p, t in zip(parts, terms):
            p.append(sum_of(t))
    row = grid.row
    out = jnp.zeros((NP, lanes), jnp.float32)
    for k, p in enumerate(parts):
        total = jnp.sum(sum_of(p), axis=0, keepdims=True)
        out = jnp.where(row == k, jnp.broadcast_to(total, (NP, lanes)), out)
    msg_a_ref[HALF : HALF + NP, :] = out
    msg_b_ref[HALF : HALF + NP, :] = out
    grid.assemble(v2_ref)

    def write(b, first, second):
        msg_a_ref[pl.ds(NP * b, NP), :] = first
        msg_b_ref[pl.ds(NP * b, NP), :] = second

    pack_face(
        grid,
        [jnp.where(grid.lower, v2_ref[rows(0, b), :], v2_ref[rows(last, b), :]) for b in range(NP)],
        write,
    )


def own_kernel(per, wide, *refs):
    *in_refs, scratch_ref = refs
    vector_refs, out_refs = in_refs[:3], in_refs[3:]
    lanes = vector_refs[0].shape[1]
    grid = Grid(lanes, wide)
    mine = pl.ds(pl.multiple_of(lax.axis_index("narrow") * per, per), per)
    weight = grid.count_weights()
    inverse = 1.0 / grid.w
    weight = [[w * inverse for w in line] for line in weight]
    for q in range(PTS // LANES):
        lines = []
        for r in range(LANES // NP):
            at = q * LANES + NP * r
            a, b = at // PLANE, (at % PLANE) // NP
            lines.append(float(1.0 / (WEIGHTS[a] * WEIGHTS[b])) * weight[place(a)][place(b)])
        scale = jnp.concatenate(lines, axis=0)
        fields = [ref[q * LANES : (q + 1) * LANES, :] for ref in vector_refs] + [scale]
        for k, (field, ref) in enumerate(zip(fields, out_refs)):
            for t in range(lanes // LANES):
                scratch_ref[k, t * LANES : (t + 1) * LANES, :] = jnp.transpose(
                    field[:, t * LANES : (t + 1) * LANES]
                )
            ref[:, q * LANES : (q + 1) * LANES] = scratch_ref[k, mine, :]


def last_kernel(
    wide,
    v0_ref,
    v1_ref,
    v2_ref,
    scale_ref,
    got_a_ref,
    got_b_ref,
    twin_b_ref,
    sums_ref,
    twin_sums_ref,
    solution_ref,
    strong_ref,
    face_ref,
    turned_ref,
):
    per = v0_ref.shape[0]
    lanes = got_a_ref.shape[1]
    grid = Grid(lanes, wide)
    nb = grid.has_neighbour()
    v = lax.axis_index("narrow")
    core = v % 2
    extra = unpack_face(
        grid,
        lambda b: got_a_ref[pl.ds(NP * b, NP), :],
        lambda b: jnp.where(
            core == 0, twin_b_ref[pl.ds(NP * b, NP), :], got_b_ref[pl.ds(NP * b, NP), :]
        ),
        nb,
    )
    for b in range(NP):
        face_ref[pl.ds(NP * b, NP), :] = extra[b]
        face_ref[pl.ds(PLANE + NP * b, NP), :] = extra[b]
    for t in range(lanes // LANES):
        turned_ref[t * LANES : (t + 1) * LANES, :] = jnp.transpose(
            face_ref[:, t * LANES : (t + 1) * LANES]
        )
    face = turned_ref[pl.ds(pl.multiple_of(v * per, per), per), :]
    spot = lax.broadcasted_iota(jnp.int32, (per, LANES), 1)
    layer = lax.broadcasted_iota(jnp.int32, (per, LANES), 0) // XSTEP
    ends = {
        0: jnp.where((spot < PLANE) & (layer == 0), face, 0.0),
        PTS // LANES - 1: jnp.where((spot >= PLANE) & (layer == BX - 1), face, 0.0),
    }
    total = sums_ref[...] + twin_sums_ref[...]
    g = [jnp.sum(total[k : k + 1, :], axis=1, keepdims=True) for k in range(4)]
    alpha = g[0] / g[1]
    norm = g[0] - 2.0 * alpha * g[1] + (alpha * alpha) * g[2]
    beta = norm / g[0]
    one = 1.0 + beta
    curve = one * one * g[1] - 2.0 * one * alpha * g[2] + (alpha * alpha) * g[3]
    step = norm / curve
    first = jnp.broadcast_to(alpha + step * one, (per, LANES))
    second = jnp.broadcast_to(alpha * step, (per, LANES))
    for q in range(PTS // LANES):
        at = (slice(None), slice(q * LANES, (q + 1) * LANES))
        v0, v1, v2 = v0_ref[at], v1_ref[at], v2_ref[at]
        if q in ends:
            v2 = v2 + ends[q]
        solution_ref[at] = first * v0 - second * v1
        strong_ref[at] = (v0 - first * v1 + second * v2) * scale_ref[at]


VM = pl.BlockSpec(memory_space=pltpu.VMEM)


def call(kernel, out_shapes, in_specs, scratch=(), name=None, grant=16 * 1024 * 1024):
    return pl.pallas_call(
        kernel,
        out_shape=[jax.ShapeDtypeStruct(s, jnp.float32) for s in out_shapes],
        in_specs=in_specs,
        out_specs=[VM] * len(out_shapes),
        scratch_shapes=list(scratch),
        compiler_params=pltpu.CompilerParams(vmem_limit_bytes=grant),
        name=name,
    )


def swap(x, wide, narrow, *partner_of):
    pairs = []
    for u in range(wide):
        to = [partner(u) for partner in partner_of]
        idle = [not 0 <= t < wide for t in to]
        for v in range(narrow):
            k = v % len(to)
            away = v ^ 1 if all(idle) else v ^ 2
            target = u * narrow + away if idle[k] else to[k] * narrow + v
            pairs.append((u * narrow + v, target))
    return lax.ppermute(x, ("wide", "narrow"), pairs)


def same_pair(u):
    return u ^ 1


def next_pair(u):
    return u + 1 if u % 2 else u - 1


def twin(x, narrow):
    return lax.ppermute(x, "narrow", [(v, v ^ 1) for v in range(narrow)])


def finish(msg_a, msg_b, wide, narrow):
    got_a = swap(msg_a, wide, narrow, same_pair)
    if wide == 8:
        pair = msg_a[HALF:] + got_a[HALF:]
        got_b = swap(
            jnp.concatenate([msg_b[:HALF], pair], axis=0), wide, narrow, lambda u: u ^ 4, next_pair
        )
        more = swap(pair, wide, narrow, lambda u: u ^ 2, lambda u: u ^ 6)
        even = lax.axis_index("narrow") % 2 == 0
        sums = more + jnp.where(even, pair + got_b[HALF:], 0.0)
        return got_a[:HALF], got_b[:HALF], twin(got_b[:HALF], narrow), sums, twin(sums, narrow)
    got_b = swap(msg_b, wide, narrow, next_pair)[:HALF]
    sums = lax.psum(msg_a[HALF:], "wide")
    return got_a[:HALF], got_b, got_b, sums, jnp.zeros_like(sums)


def local(wide, narrow, source_old, reaction_old, new_place):
    per = source_old.shape[1]
    lanes = per * narrow
    blocks = 2 * (PTS // LANES)
    packed = call(
        pack_kernel,
        [(blocks * per + NP, LANES)],
        [pl.BlockSpec(memory_space=pltpu.HBM)] * 3,
        [pltpu.VMEM((1, per), jnp.int32), pltpu.SemaphoreType.DMA((blocks + 1,))],
        name="pack",
        grant=None,
    )(source_old.T, reaction_old.T, new_place.reshape(1, per))[0]
    full = (PTS, lanes)
    rhs, reaction, msg_a, msg_b = call(
        functools.partial(first_kernel, per, narrow, wide),
        [full, full, (3 * HALF, lanes), (3 * HALF, lanes)],
        [VM],
        name="first",
    )(lax.all_gather(packed, "narrow"))
    got_a = swap(msg_a, wide, narrow, same_pair)
    got_b = swap(msg_b, wide, narrow, next_pair)
    v0, v1, v2, msg_a, msg_b = call(
        functools.partial(second_kernel, wide),
        [full, full, full, (HALF + NP, lanes), (HALF + NP, lanes)],
        [VM] * 4,
        [pltpu.VMEM((PLANE, lanes), jnp.float32), pltpu.VMEM((PLANE, lanes), jnp.float32)],
        name="second",
    )(rhs, reaction, got_a, got_b)
    arrived = finish(msg_a, msg_b, wide, narrow)
    own = call(
        functools.partial(own_kernel, per, wide),
        [(per, PTS)] * 4,
        [VM] * 3,
        [pltpu.VMEM((4, lanes, LANES), jnp.float32)],
        name="own",
    )(v0, v1, v2)
    out = call(
        functools.partial(last_kernel, wide),
        [(per, PTS), (per, PTS)],
        [VM] * 9,
        [pltpu.VMEM((LANES, lanes), jnp.float32), pltpu.VMEM((lanes, LANES), jnp.float32)],
        name="last",
    )(*own, *arrived)
    return tuple(x.T for x in out)


def solution(mesh):
    placed = (P(None, ("wide", "narrow")), P(None, ("wide", "narrow")), P(("wide", "narrow")))
    return jax.shard_map(
        functools.partial(local, mesh.shape["wide"], mesh.shape["narrow"]),
        mesh=mesh,
        in_specs=placed,
        out_specs=(P(None, ("wide", "narrow")), P(None, ("wide", "narrow"))),
        check_vma=False,
    )
```

```python
import functools

import jax
import jax.numpy as jnp
import numpy as np
from jax import lax
from jax.experimental import pallas as pl
from jax.experimental.pallas import tpu as pltpu
from jax.sharding import PartitionSpec as P

NP = 8
BX = 2
BY = 4
EZ = 4
PTS = NP**3
PLANE = NP * NP
LANES = 128
HALF = PLANE // 2
XSTEP = BY * EZ

DIFFUSION = 0.05


def legendre_values(abscissa, num_points):
    columns = [np.ones(abscissa.shape), abscissa]
    for degree in range(2, num_points):
        columns.append(
            ((2 * degree - 1) * abscissa * columns[degree - 1] - (degree - 1) * columns[degree - 2])
            / degree
        )
    return np.stack(columns, 1)


def gll_tables(num_points):
    poly_order = num_points - 1
    abscissa = np.cos(np.pi * np.arange(num_points) / poly_order)
    for newton_step in range(60):
        legendre = legendre_values(abscissa, num_points)
        abscissa = abscissa - (abscissa * legendre[:, poly_order] - legendre[:, poly_order - 1]) / (
            num_points * legendre[:, poly_order]
        )
    legendre = legendre_values(abscissa, num_points)
    top_values = legendre[:, poly_order][::-1]
    abscissa = abscissa[::-1]
    weights = 2.0 / (poly_order * num_points * top_values**2)
    identity = np.eye(num_points)
    differ = np.where(identity > 0, 1.0, abscissa[:, None] - abscissa[None, :])
    deriv_table = np.where(identity > 0, 0.0, top_values[:, None] / (top_values[None, :] * differ))
    quarter = poly_order * num_points / 4.0
    edge_fix = np.concatenate([np.array([-quarter]), np.zeros(num_points - 2), np.array([quarter])])
    deriv_table = deriv_table + identity * edge_fix[:, None]
    return (weights, deriv_table)


def stiffness():
    weights, deriv = gll_tables(NP)
    stiff = DIFFUSION * deriv.T @ np.diag(weights) @ deriv
    return weights, 0.5 * (stiff + stiff.T)


WEIGHTS, STIFF = stiffness()
EVEN = 0.5 * (STIFF[:4, :4] + STIFF[:4, 7:3:-1])
ODD = 0.5 * (STIFF[:4, :4] - STIFF[:4, 7:3:-1])


def apply_stiff(f):
    even = [f[j] + f[7 - j] for j in range(4)]
    odd = [f[j] - f[7 - j] for j in range(4)]
    out = [None] * NP
    for i in range(4):
        e = sum_of([float(EVEN[i, j]) * even[j] for j in range(4)])
        o = sum_of([float(ODD[i, j]) * odd[j] for j in range(4)])
        out[i] = e + o
        out[7 - i] = e - o
    return out


def sum_of(terms):
    while len(terms) > 1:
        terms = [
            terms[k] + terms[k + 1] if k + 1 < len(terms) else terms[k]
            for k in range(0, len(terms), 2)
        ]
    return terms[0]


class Grid:
    def __init__(self, lanes, wide):
        self.lanes = lanes
        self.wide = wide
        self.lane = lax.broadcasted_iota(jnp.int32, (NP, lanes), 1)
        self.row = lax.broadcasted_iota(jnp.int32, (NP, lanes), 0)
        self.s = self.lane & (EZ - 1)
        self.j = (self.lane // EZ) & (BY - 1)
        self.i = (self.lane // XSTEP) & (BX - 1)
        self.lower = self.i == 0
        w = jnp.full((NP, lanes), float(WEIGHTS[0]), jnp.float32)
        for c in range(1, NP):
            w = jnp.where(self.row == c, float(WEIGHTS[c]), w)
        self.w = w

    def has_neighbour(self):
        u = lax.axis_index("wide")
        low = jnp.where(u > 0, 1, 0)
        high = jnp.where(u < self.wide - 1, 1, 0)
        return jnp.where(self.lower, low, high) > 0

    def roll(self, x, shift):
        return pltpu.roll(x, shift % self.lanes, axis=x.ndim - 1)

    def share(self, lo, hi, axis):
        if axis == "x":
            new_lo = lo + jnp.where(self.lower, 0.0, self.roll(hi, XSTEP))
            new_hi = hi + jnp.where(self.lower, self.roll(lo, -XSTEP), 0.0)
        elif axis == "y":
            block = BX * XSTEP
            jump = block - (BY - 1) * EZ
            from_hi = jnp.where(self.j > 0, self.roll(hi, EZ), self.roll(hi, jump))
            from_lo = jnp.where(self.j < BY - 1, self.roll(lo, -EZ), self.roll(lo, -jump))
            first = (self.j == 0) & (self.lane < block)
            last = (self.j == BY - 1) & (self.lane >= self.lanes - block)
            new_lo = lo + jnp.where(first, 0.0, from_hi)
            new_hi = hi + jnp.where(last, 0.0, from_lo)
        else:
            new_lo = lo + jnp.where(self.s > 0, self.roll(hi, 1), 0.0)
            new_hi = hi + jnp.where(self.s < EZ - 1, self.roll(lo, -1), 0.0)
        return new_lo, new_hi

    def assemble(self, ref):
        for b in range(NP):
            lo, hi = rows(0, b), rows(NP - 1, b)
            ref[lo, :], ref[hi, :] = self.share(ref[lo, :], ref[hi, :], "x")
        for a in range(NP):
            lo, hi = rows(a, 0), rows(a, NP - 1)
            ref[lo, :], ref[hi, :] = self.share(ref[lo, :], ref[hi, :], "y")
        for a in range(NP):
            lo, hi = self.share(column(ref, PLANE * a), column(ref, PLANE * a + NP - 1), "z")
            put_column(ref, PLANE * a, lo)
            put_column(ref, PLANE * a + NP - 1, hi)

    def plane_product(self, f_ref, base, out_ref):
        z = apply_stiff([column(f_ref, base + c) for c in range(NP)])
        for c in range(NP):
            put_column(out_ref, c, self.w * z[c])
        y = apply_stiff([f_ref[pl.ds(base + NP * b, NP), :] for b in range(NP)])
        return [self.w * y[b] + out_ref[pl.ds(NP * b, NP), :] for b in range(NP)]

    def local(self, f_ref, reaction_ref, out_ref, tmp_ref):
        for a in range(NP):
            flat = self.plane_product(f_ref, PLANE * a, tmp_ref)
            wa = float(WEIGHTS[a])
            for b in range(NP):
                r = rows(a, b)
                mass = (wa * float(WEIGHTS[b])) * self.w
                out_ref[r, :] = wa * flat[b] + (reaction_ref[r, :] * mass) * f_ref[r, :]
        for b in range(NP):
            x = apply_stiff([f_ref[rows(a, b), :] for a in range(NP)])
            wb = float(WEIGHTS[b]) * self.w
            for a in range(NP):
                r = rows(a, b)
                out_ref[r, :] = out_ref[r, :] + wb * x[a]

    def count_weights(self):
        nb = self.has_neighbour()
        one = jnp.ones((NP, self.lanes), jnp.float32)
        x0 = jnp.where(~self.lower | nb, 0.5, one)
        x7 = jnp.where(self.lower | nb, 0.5, one)
        block = BX * XSTEP
        first = (self.j == 0) & (self.lane < block)
        last = (self.j == BY - 1) & (self.lane >= self.lanes - block)
        y0 = jnp.where(first, one, 0.5)
        y7 = jnp.where(last, one, 0.5)
        z = jnp.where((self.row == 0) & (self.s > 0), 0.5, one)
        z = jnp.where((self.row == NP - 1) & (self.s < EZ - 1), 0.5, z)
        zx = [z * x0, z, z * x7]
        return [[m * y0, m, m * y7] for m in zx]


def place(a):
    return 0 if a == 0 else (2 if a == NP - 1 else 1)


def rows(a, b):
    return pl.ds(PLANE * a + NP * b, NP)


def column(ref, start):
    if ref.shape[1] == LANES:
        return ref[pl.ds(start, NP, stride=NP), :]
    return jnp.concatenate([ref[pl.ds(start + NP * b, 1), :] for b in range(NP)], axis=0)


def put_column(ref, start, value):
    if ref.shape[1] == LANES:
        ref[pl.ds(start, NP, stride=NP), :] = value
    else:
        for b in range(NP):
            ref[pl.ds(start + NP * b, 1), :] = value[b : b + 1, :]


def pack_face(grid, face, write):
    u = lax.axis_index("wide")
    even = (u % 2) == 0
    for b in range(NP // 2):
        top, bottom = face[b], face[b + NP // 2]
        up = jnp.where(grid.lower, grid.roll(bottom, -XSTEP), top)
        down = jnp.where(grid.lower, top, grid.roll(bottom, XSTEP))
        write(b, jnp.where(even, up, down), jnp.where(even, down, up))


def unpack_face(grid, read_a, read_b, nb):
    u = lax.axis_index("wide")
    even = (u % 2) == 0
    tops, bottoms = [], []
    for b in range(NP // 2):
        first, second = read_a(b), read_b(b)
        from_up = jnp.where(even, first, second)
        from_down = jnp.where(even, second, first)
        top = jnp.where(grid.lower, grid.roll(from_down, -XSTEP), grid.roll(from_up, XSTEP))
        bottom = jnp.where(grid.lower, from_down, from_up)
        tops.append(jnp.where(nb, top, 0.0))
        bottoms.append(jnp.where(nb, bottom, 0.0))
    return tops + bottoms


def pack_kernel(source_ref, reaction_ref, place_ref, out_ref, near_ref, sems):
    per = source_ref.shape[0]
    blocks = 2 * (PTS // LANES)
    places = pltpu.make_async_copy(place_ref, near_ref, sems.at[blocks])
    places.start()
    copies = []
    for k, ref in enumerate((source_ref, reaction_ref)):
        for q in range(PTS // LANES):
            n = len(copies)
            copy = pltpu.make_async_copy(
                ref.at[:, pl.ds(q * LANES, LANES)], out_ref.at[pl.ds(per * n, per), :], sems.at[n]
            )
            copy.start()
            copies.append(copy)
    v = lax.axis_index("narrow")
    groups = LANES // per
    row = lax.broadcasted_iota(jnp.int32, (NP, LANES), 0)
    lane = lax.broadcasted_iota(jnp.int32, (NP, LANES), 1)
    mine = (row == v // groups) & (lane // per == v % groups)
    places.wait()
    places = jnp.concatenate([near_ref[...].astype(jnp.float32)] * groups, axis=1)
    out_ref[per * blocks :, :] = jnp.where(mine, jnp.broadcast_to(places, (NP, LANES)), 0.0)
    for copy in copies:
        copy.wait()


class Arrived:
    def __init__(self, per, narrow, got_ref):
        self.per = per
        self.got = got_ref
        self.tiles = per * narrow // LANES
        self.groups = LANES // per
        self.blocks = PTS // LANES
        lanes = per * narrow
        spot = lax.broadcasted_iota(jnp.int32, (LANES, lanes), 1).astype(jnp.float32)
        row = lax.broadcasted_iota(jnp.int32, (LANES, lanes), 0)
        places = sum_of([got_ref[v, 2 * self.blocks * per :, :] for v in range(narrow)])
        came = jnp.zeros((1, lanes), jnp.float32)
        for t in range(self.tiles):
            new = jnp.transpose(jnp.broadcast_to(places[t : t + 1, :], (LANES, LANES)))
            new = jnp.concatenate([new] * self.tiles, axis=1)
            old = (row + t * LANES).astype(jnp.float32)
            came = came + jnp.sum(jnp.where(new == spot, old, 0.0), axis=0, keepdims=True)
        came = jnp.broadcast_to(came.astype(jnp.int32), (NP, lanes))
        owners = [came[:, t * LANES : (t + 1) * LANES] for t in range(self.tiles)]
        self.source = [(owner // LANES, owner % LANES) for owner in owners]

    def block(self, field, q, t):
        rows_of = pl.ds(self.per * (self.blocks * field + q), self.per)
        return jnp.concatenate(
            [self.got[self.groups * t + g, rows_of, :] for g in range(self.groups)], axis=0
        )

    def turned(self, old):
        old = [jnp.transpose(x) for x in old]
        for r in range(LANES // NP):
            for t, (home, lane) in enumerate(self.source):
                value = None
                for h in range(self.tiles):
                    pick = jnp.take_along_axis(old[h][NP * r : NP * (r + 1), :], lane, axis=1)
                    value = pick if value is None else jnp.where(home == h, pick, value)
                yield r, slice(t * LANES, (t + 1) * LANES), value


def first_kernel(per, narrow, wide, got_ref, rhs_ref, msg_a_ref, msg_b_ref, ends_ref):
    lanes = per * narrow
    grid = Grid(lanes, wide)
    arrived = Arrived(per, narrow, got_ref)
    tiles = range(arrived.tiles)
    for q in range(arrived.blocks):
        for r, cols, value in arrived.turned([arrived.block(0, q, t) for t in tiles]):
            at = q * LANES + NP * r
            a, b = at // PLANE, (at % PLANE) // NP
            mass = float(WEIGHTS[a]) * float(WEIGHTS[b])
            rhs_ref[pl.ds(at, NP), cols] = value * (mass * grid.w[:, cols])
    low = lax.broadcasted_iota(jnp.int32, (LANES, LANES), 1) < PLANE
    ends = [
        jnp.where(low, arrived.block(1, 0, t), arrived.block(1, arrived.blocks - 1, t)) for t in tiles
    ]
    for r, cols, value in arrived.turned(ends):
        ends_ref[pl.ds(NP * r, NP), cols] = value
    grid.assemble(rhs_ref)

    def write(part):
        def put(b, first, second):
            msg_a_ref[pl.ds(part * HALF + NP * b, NP), :] = first
            msg_b_ref[pl.ds(part * HALF + NP * b, NP), :] = second

        return put

    last = NP - 1
    pack_face(
        grid,
        [jnp.where(grid.lower, rhs_ref[rows(0, b), :], rhs_ref[rows(last, b), :]) for b in range(NP)],
        write(0),
    )
    part = []
    for b in range(NP):
        f = [rhs_ref[rows(a, b), :] for a in range(NP)]
        low = sum_of([float(STIFF[0, a]) * f[a] for a in range(1, NP)])
        high = sum_of([float(STIFF[last, a]) * f[a] for a in range(last)])
        part.append((float(WEIGHTS[b]) * grid.w) * jnp.where(grid.lower, low, high))
    pack_face(grid, part, write(1))
    pack_face(
        grid,
        [
            jnp.where(
                grid.lower, ends_ref[pl.ds(NP * b, NP), :], ends_ref[pl.ds(PLANE + NP * b, NP), :]
            )
            for b in range(NP)
        ],
        write(2),
    )


def middle_kernel(per, narrow, wide, got_ref, rhs_ref, reaction_ref, part_ref, flat_ref, tmp_ref):
    grid = Grid(per * narrow, wide)
    arrived = Arrived(per, narrow, got_ref)
    for q in range(arrived.blocks):
        blocks = [arrived.block(1, q, t) for t in range(arrived.tiles)]
        for r, cols, value in arrived.turned(blocks):
            reaction_ref[pl.ds(q * LANES + NP * r, NP), cols] = value
    grid.local(rhs_ref, reaction_ref, part_ref, tmp_ref)
    for b in range(NP):
        low, high = rhs_ref[rows(0, b), :], rhs_ref[rows(NP - 1, b), :]
        flat_ref[pl.ds(NP * b, NP), :] = jnp.where(grid.lower, low, high)
    flat = grid.plane_product(flat_ref, 0, tmp_ref)
    for b in range(NP):
        flat_ref[pl.ds(NP * b, NP), :] = flat[b]


def second_kernel(
    wide,
    rhs_ref,
    reaction_ref,
    part_ref,
    flat0_ref,
    got_a_ref,
    got_b_ref,
    v0_ref,
    v1_ref,
    v2_ref,
    msg_a_ref,
    msg_b_ref,
    face_ref,
    tmp_ref,
):
    lanes = rhs_ref.shape[1]
    grid = Grid(lanes, wide)
    nb = grid.has_neighbour()
    last = NP - 1

    def reader(part):
        def first(b):
            return got_a_ref[pl.ds(part * HALF + NP * b, NP), :]

        def second(b):
            return got_b_ref[pl.ds(part * HALF + NP * b, NP), :]

        return first, second

    extra = unpack_face(grid, *reader(0), nb)
    slopes = unpack_face(grid, *reader(1), nb)
    reactions = unpack_face(grid, *reader(2), nb)
    for b in range(NP):
        face_ref[pl.ds(NP * b, NP), :] = extra[b]
    flat = grid.plane_product(face_ref, 0, tmp_ref)
    pull = [jnp.where(grid.lower, float(STIFF[a, 0]), float(STIFF[a, last])) for a in range(NP)]
    w0 = float(WEIGHTS[0])
    for b in range(NP):
        wb = float(WEIGHTS[b]) * grid.w
        more = wb * extra[b]
        for a in range(1, last):
            r = rows(a, b)
            v0_ref[r, :] = rhs_ref[r, :]
            v1_ref[r, :] = part_ref[r, :] + pull[a] * more
        r_low, r_high = rows(0, b), rows(last, b)
        low = rhs_ref[r_low, :] + jnp.where(grid.lower, extra[b], 0.0)
        high = rhs_ref[r_high, :] + jnp.where(grid.lower, 0.0, extra[b])
        v0_ref[r_low, :] = low
        v0_ref[r_high, :] = high
        face = jnp.where(grid.lower, low, high)
        own = jnp.where(grid.lower, reaction_ref[r_low, :], reaction_ref[r_high, :])
        theirs = slopes[b] + w0 * (flat0_ref[pl.ds(NP * b, NP), :] + flat[b])
        theirs = theirs + wb * ((float(STIFF[0, 0]) + w0 * reactions[b]) * face)
        more_face = w0 * (flat[b] + own * more) + jnp.where(nb, theirs, 0.0)
        v1_ref[r_low, :] = part_ref[r_low, :] + pull[0] * more + jnp.where(grid.lower, more_face, 0.0)
        v1_ref[r_high, :] = (
            part_ref[r_high, :] + pull[last] * more + jnp.where(grid.lower, 0.0, more_face)
        )
    grid.assemble(v1_ref)
    grid.local(v1_ref, reaction_ref, v2_ref, tmp_ref)
    weight = grid.count_weights()
    parts = [[], [], [], []]
    for a in range(NP):
        terms = [[], [], [], []]
        for b in range(NP):
            r = rows(a, b)
            v0, v1, v2 = v0_ref[r, :], v1_ref[r, :], v2_ref[r, :]
            wt = weight[place(a)][place(b)]
            w1 = wt * v1
            for t, value in zip(terms, ((wt * v0) * v0, w1 * v0, w1 * v1, v1 * v2)):
                t.append(value)
        for p, t in zip(parts, terms):
            p.append(sum_of(t))
    row = grid.row
    out = jnp.zeros((NP, lanes), jnp.float32)
    for k, p in enumerate(parts):
        total = jnp.sum(sum_of(p), axis=0, keepdims=True)
        out = jnp.where(row == k, jnp.broadcast_to(total, (NP, lanes)), out)
    msg_a_ref[HALF : HALF + NP, :] = out
    msg_b_ref[HALF : HALF + NP, :] = out
    grid.assemble(v2_ref)

    def write(b, first, second):
        msg_a_ref[pl.ds(NP * b, NP), :] = first
        msg_b_ref[pl.ds(NP * b, NP), :] = second

    pack_face(
        grid,
        [jnp.where(grid.lower, v2_ref[rows(0, b), :], v2_ref[rows(last, b), :]) for b in range(NP)],
        write,
    )


def own_kernel(per, wide, *refs):
    *in_refs, scratch_ref = refs
    vector_refs, out_refs = in_refs[:3], in_refs[3:]
    lanes = vector_refs[0].shape[1]
    grid = Grid(lanes, wide)
    mine = pl.ds(pl.multiple_of(lax.axis_index("narrow") * per, per), per)
    weight = grid.count_weights()
    inverse = 1.0 / grid.w
    weight = [[w * inverse for w in line] for line in weight]
    for q in range(PTS // LANES):
        lines = []
        for r in range(LANES // NP):
            at = q * LANES + NP * r
            a, b = at // PLANE, (at % PLANE) // NP
            lines.append(float(1.0 / (WEIGHTS[a] * WEIGHTS[b])) * weight[place(a)][place(b)])
        scale = jnp.concatenate(lines, axis=0)
        fields = [ref[q * LANES : (q + 1) * LANES, :] for ref in vector_refs] + [scale]
        for k, (field, ref) in enumerate(zip(fields, out_refs)):
            for t in range(lanes // LANES):
                scratch_ref[k, t * LANES : (t + 1) * LANES, :] = jnp.transpose(
                    field[:, t * LANES : (t + 1) * LANES]
                )
            ref[:, q * LANES : (q + 1) * LANES] = scratch_ref[k, mine, :]


def last_kernel(
    wide,
    v0_ref,
    v1_ref,
    v2_ref,
    scale_ref,
    got_a_ref,
    got_b_ref,
    twin_b_ref,
    sums_ref,
    twin_sums_ref,
    solution_ref,
    strong_ref,
    face_ref,
    turned_ref,
):
    per = v0_ref.shape[0]
    lanes = got_a_ref.shape[1]
    grid = Grid(lanes, wide)
    nb = grid.has_neighbour()
    v = lax.axis_index("narrow")
    core = v % 2
    extra = unpack_face(
        grid,
        lambda b: got_a_ref[pl.ds(NP * b, NP), :],
        lambda b: jnp.where(
            core == 0, twin_b_ref[pl.ds(NP * b, NP), :], got_b_ref[pl.ds(NP * b, NP), :]
        ),
        nb,
    )
    for b in range(NP):
        face_ref[pl.ds(NP * b, NP), :] = extra[b]
        face_ref[pl.ds(PLANE + NP * b, NP), :] = extra[b]
    for t in range(lanes // LANES):
        turned_ref[t * LANES : (t + 1) * LANES, :] = jnp.transpose(
            face_ref[:, t * LANES : (t + 1) * LANES]
        )
    face = turned_ref[pl.ds(pl.multiple_of(v * per, per), per), :]
    spot = lax.broadcasted_iota(jnp.int32, (per, LANES), 1)
    layer = lax.broadcasted_iota(jnp.int32, (per, LANES), 0) // XSTEP
    ends = {
        0: jnp.where((spot < PLANE) & (layer == 0), face, 0.0),
        PTS // LANES - 1: jnp.where((spot >= PLANE) & (layer == BX - 1), face, 0.0),
    }
    total = sums_ref[...] + twin_sums_ref[...]
    g = [jnp.sum(total[k : k + 1, :], axis=1, keepdims=True) for k in range(4)]
    alpha = g[0] / g[1]
    norm = g[0] - 2.0 * alpha * g[1] + (alpha * alpha) * g[2]
    beta = norm / g[0]
    one = 1.0 + beta
    curve = one * one * g[1] - 2.0 * one * alpha * g[2] + (alpha * alpha) * g[3]
    step = norm / curve
    first = jnp.broadcast_to(alpha + step * one, (per, LANES))
    second = jnp.broadcast_to(alpha * step, (per, LANES))
    for q in range(PTS // LANES):
        at = (slice(None), slice(q * LANES, (q + 1) * LANES))
        v0, v1, v2 = v0_ref[at], v1_ref[at], v2_ref[at]
        if q in ends:
            v2 = v2 + ends[q]
        solution_ref[at] = first * v0 - second * v1
        strong_ref[at] = (v0 - first * v1 + second * v2) * scale_ref[at]


VM = pl.BlockSpec(memory_space=pltpu.VMEM)


def call(kernel, out_shapes, in_specs, scratch=(), name=None):
    return pl.pallas_call(
        kernel,
        out_shape=[jax.ShapeDtypeStruct(s, jnp.float32) for s in out_shapes],
        in_specs=in_specs,
        out_specs=[VM] * len(out_shapes),
        scratch_shapes=list(scratch),
        compiler_params=pltpu.CompilerParams(vmem_limit_bytes=16 * 1024 * 1024),
        name=name,
    )


def in_hbm(*arrays):
    return [pltpu.with_memory_space_constraint(x, pltpu.HBM) for x in arrays]


def swap(x, wide, narrow, *partner_of):
    pairs = []
    for u in range(wide):
        to = [partner(u) for partner in partner_of]
        idle = [not 0 <= t < wide for t in to]
        for v in range(narrow):
            k = v % len(to)
            away = v ^ 1 if all(idle) else v ^ 2
            target = u * narrow + away if idle[k] else to[k] * narrow + v
            pairs.append((u * narrow + v, target))
    return lax.ppermute(x, ("wide", "narrow"), pairs)


def same_pair(u):
    return u ^ 1


def next_pair(u):
    return u + 1 if u % 2 else u - 1


def twin(x, narrow):
    return lax.ppermute(x, "narrow", [(v, v ^ 1) for v in range(narrow)])


def finish(msg_a, msg_b, wide, narrow):
    got_a = swap(msg_a, wide, narrow, same_pair)
    if wide == 8:
        pair = msg_a[HALF:] + got_a[HALF:]
        got_b = swap(
            jnp.concatenate([msg_b[:HALF], pair], axis=0), wide, narrow, lambda u: u ^ 4, next_pair
        )
        more = swap(pair, wide, narrow, lambda u: u ^ 2, lambda u: u ^ 6)
        even = lax.axis_index("narrow") % 2 == 0
        sums = more + jnp.where(even, pair + got_b[HALF:], 0.0)
        return got_a[:HALF], got_b[:HALF], twin(got_b[:HALF], narrow), sums, twin(sums, narrow)
    got_b = swap(msg_b, wide, narrow, next_pair)[:HALF]
    sums = lax.psum(msg_a[HALF:], "wide")
    return got_a[:HALF], got_b, got_b, sums, jnp.zeros_like(sums)


def local(wide, narrow, source_old, reaction_old, new_place):
    per = source_old.shape[1]
    lanes = per * narrow
    blocks = 2 * (PTS // LANES)
    packed = call(
        pack_kernel,
        [(blocks * per + NP, LANES)],
        [pl.BlockSpec(memory_space=pltpu.HBM)] * 3,
        [pltpu.VMEM((1, per), jnp.int32), pltpu.SemaphoreType.DMA((blocks + 1,))],
        name="pack",
    )(*in_hbm(source_old.T, reaction_old.T, new_place.reshape(1, per)))[0]
    full = (PTS, lanes)
    got = lax.all_gather(packed, "narrow")
    rhs, msg_a, msg_b = call(
        functools.partial(first_kernel, per, narrow, wide),
        [full, (3 * HALF, lanes), (3 * HALF, lanes)],
        [VM],
        [pltpu.VMEM((2 * PLANE, lanes), jnp.float32)],
        name="first",
    )(got)
    got_a = swap(msg_a, wide, narrow, same_pair)
    got_b = swap(msg_b, wide, narrow, next_pair)
    reaction, part, flat = call(
        functools.partial(middle_kernel, per, narrow, wide),
        [full, full, (PLANE, lanes)],
        [VM] * 2,
        [pltpu.VMEM((PLANE, lanes), jnp.float32)],
        name="middle",
    )(got, rhs)
    v0, v1, v2, msg_a, msg_b = call(
        functools.partial(second_kernel, wide),
        [full, full, full, (HALF + NP, lanes), (HALF + NP, lanes)],
        [VM] * 6,
        [pltpu.VMEM((PLANE, lanes), jnp.float32), pltpu.VMEM((PLANE, lanes), jnp.float32)],
        name="second",
    )(rhs, reaction, part, flat, got_a, got_b)
    arrived = finish(msg_a, msg_b, wide, narrow)
    own = call(
        functools.partial(own_kernel, per, wide),
        [(per, PTS)] * 4,
        [VM] * 3,
        [pltpu.VMEM((4, lanes, LANES), jnp.float32)],
        name="own",
    )(v0, v1, v2)
    out = call(
        functools.partial(last_kernel, wide),
        [(per, PTS), (per, PTS)],
        [VM] * 9,
        [pltpu.VMEM((LANES, lanes), jnp.float32), pltpu.VMEM((lanes, LANES), jnp.float32)],
        name="last",
    )(*own, *arrived)
    return tuple(x.T for x in out)


def solution(mesh):
    placed = (P(None, ("wide", "narrow")), P(None, ("wide", "narrow")), P(("wide", "narrow")))
    return jax.shard_map(
        functools.partial(local, mesh.shape["wide"], mesh.shape["narrow"]),
        mesh=mesh,
        in_specs=placed,
        out_specs=(P(None, ("wide", "narrow")), P(None, ("wide", "narrow"))),
        check_vma=False,
    )
```

```python
import functools

import jax
import jax.numpy as jnp
import numpy as np
from jax import lax
from jax.experimental import pallas as pl
from jax.experimental.pallas import tpu as pltpu
from jax.sharding import PartitionSpec as P

NP = 8
BX = 2
BY = 4
EZ = 4
PTS = NP**3
PLANE = NP * NP
LANES = 128
HALF = PLANE // 2
XSTEP = BY * EZ

DIFFUSION = 0.05


def legendre_values(abscissa, num_points):
    columns = [np.ones(abscissa.shape), abscissa]
    for degree in range(2, num_points):
        columns.append(
            ((2 * degree - 1) * abscissa * columns[degree - 1] - (degree - 1) * columns[degree - 2])
            / degree
        )
    return np.stack(columns, 1)


def gll_tables(num_points):
    poly_order = num_points - 1
    abscissa = np.cos(np.pi * np.arange(num_points) / poly_order)
    for newton_step in range(60):
        legendre = legendre_values(abscissa, num_points)
        abscissa = abscissa - (abscissa * legendre[:, poly_order] - legendre[:, poly_order - 1]) / (
            num_points * legendre[:, poly_order]
        )
    legendre = legendre_values(abscissa, num_points)
    top_values = legendre[:, poly_order][::-1]
    abscissa = abscissa[::-1]
    weights = 2.0 / (poly_order * num_points * top_values**2)
    identity = np.eye(num_points)
    differ = np.where(identity > 0, 1.0, abscissa[:, None] - abscissa[None, :])
    deriv_table = np.where(identity > 0, 0.0, top_values[:, None] / (top_values[None, :] * differ))
    quarter = poly_order * num_points / 4.0
    edge_fix = np.concatenate([np.array([-quarter]), np.zeros(num_points - 2), np.array([quarter])])
    deriv_table = deriv_table + identity * edge_fix[:, None]
    return (weights, deriv_table)


def stiffness():
    weights, deriv = gll_tables(NP)
    stiff = DIFFUSION * deriv.T @ np.diag(weights) @ deriv
    return weights, 0.5 * (stiff + stiff.T)


WEIGHTS, STIFF = stiffness()
EVEN = 0.5 * (STIFF[:4, :4] + STIFF[:4, 7:3:-1])
ODD = 0.5 * (STIFF[:4, :4] - STIFF[:4, 7:3:-1])


def apply_stiff(f):
    even = [f[j] + f[7 - j] for j in range(4)]
    odd = [f[j] - f[7 - j] for j in range(4)]
    out = [None] * NP
    for i in range(4):
        e = sum_of([float(EVEN[i, j]) * even[j] for j in range(4)])
        o = sum_of([float(ODD[i, j]) * odd[j] for j in range(4)])
        out[i] = e + o
        out[7 - i] = e - o
    return out


def sum_of(terms):
    while len(terms) > 1:
        terms = [
            terms[k] + terms[k + 1] if k + 1 < len(terms) else terms[k]
            for k in range(0, len(terms), 2)
        ]
    return terms[0]


class Grid:
    def __init__(self, lanes, wide):
        self.lanes = lanes
        self.wide = wide
        self.lane = lax.broadcasted_iota(jnp.int32, (NP, lanes), 1)
        self.row = lax.broadcasted_iota(jnp.int32, (NP, lanes), 0)
        self.s = self.lane & (EZ - 1)
        self.j = (self.lane // EZ) & (BY - 1)
        self.i = (self.lane // XSTEP) & (BX - 1)
        self.lower = self.i == 0
        w = jnp.full((NP, lanes), float(WEIGHTS[0]), jnp.float32)
        for c in range(1, NP):
            w = jnp.where(self.row == c, float(WEIGHTS[c]), w)
        self.w = w

    def has_neighbour(self):
        u = lax.axis_index("wide")
        low = jnp.where(u > 0, 1, 0)
        high = jnp.where(u < self.wide - 1, 1, 0)
        return jnp.where(self.lower, low, high) > 0

    def roll(self, x, shift):
        return pltpu.roll(x, shift % self.lanes, axis=x.ndim - 1)

    def share(self, lo, hi, axis):
        if axis == "x":
            new_lo = lo + jnp.where(self.lower, 0.0, self.roll(hi, XSTEP))
            new_hi = hi + jnp.where(self.lower, self.roll(lo, -XSTEP), 0.0)
        elif axis == "y":
            block = BX * XSTEP
            jump = block - (BY - 1) * EZ
            from_hi = jnp.where(self.j > 0, self.roll(hi, EZ), self.roll(hi, jump))
            from_lo = jnp.where(self.j < BY - 1, self.roll(lo, -EZ), self.roll(lo, -jump))
            first = (self.j == 0) & (self.lane < block)
            last = (self.j == BY - 1) & (self.lane >= self.lanes - block)
            new_lo = lo + jnp.where(first, 0.0, from_hi)
            new_hi = hi + jnp.where(last, 0.0, from_lo)
        else:
            new_lo = lo + jnp.where(self.s > 0, self.roll(hi, 1), 0.0)
            new_hi = hi + jnp.where(self.s < EZ - 1, self.roll(lo, -1), 0.0)
        return new_lo, new_hi

    def assemble(self, ref):
        for b in range(NP):
            lo, hi = rows(0, b), rows(NP - 1, b)
            ref[lo, :], ref[hi, :] = self.share(ref[lo, :], ref[hi, :], "x")
        for a in range(NP):
            lo, hi = rows(a, 0), rows(a, NP - 1)
            ref[lo, :], ref[hi, :] = self.share(ref[lo, :], ref[hi, :], "y")
        for a in range(NP):
            lo, hi = self.share(column(ref, PLANE * a), column(ref, PLANE * a + NP - 1), "z")
            put_column(ref, PLANE * a, lo)
            put_column(ref, PLANE * a + NP - 1, hi)

    def plane_product(self, f_ref, base, out_ref):
        z = apply_stiff([column(f_ref, base + c) for c in range(NP)])
        for c in range(NP):
            put_column(out_ref, c, self.w * z[c])
        y = apply_stiff([f_ref[pl.ds(base + NP * b, NP), :] for b in range(NP)])
        return [self.w * y[b] + out_ref[pl.ds(NP * b, NP), :] for b in range(NP)]

    def local(self, f_ref, reaction_ref, out_ref, tmp_ref):
        for a in range(NP):
            flat = self.plane_product(f_ref, PLANE * a, tmp_ref)
            wa = float(WEIGHTS[a])
            for b in range(NP):
                r = rows(a, b)
                mass = (wa * float(WEIGHTS[b])) * self.w
                out_ref[r, :] = wa * flat[b] + (reaction_ref[r, :] * mass) * f_ref[r, :]
        for b in range(NP):
            x = apply_stiff([f_ref[rows(a, b), :] for a in range(NP)])
            wb = float(WEIGHTS[b]) * self.w
            for a in range(NP):
                r = rows(a, b)
                out_ref[r, :] = out_ref[r, :] + wb * x[a]

    def count_weights(self):
        nb = self.has_neighbour()
        one = jnp.ones((NP, self.lanes), jnp.float32)
        x0 = jnp.where(~self.lower | nb, 0.5, one)
        x7 = jnp.where(self.lower | nb, 0.5, one)
        block = BX * XSTEP
        first = (self.j == 0) & (self.lane < block)
        last = (self.j == BY - 1) & (self.lane >= self.lanes - block)
        y0 = jnp.where(first, one, 0.5)
        y7 = jnp.where(last, one, 0.5)
        z = jnp.where((self.row == 0) & (self.s > 0), 0.5, one)
        z = jnp.where((self.row == NP - 1) & (self.s < EZ - 1), 0.5, z)
        zx = [z * x0, z, z * x7]
        return [[m * y0, m, m * y7] for m in zx]


def place(a):
    return 0 if a == 0 else (2 if a == NP - 1 else 1)


def rows(a, b):
    return pl.ds(PLANE * a + NP * b, NP)


def column(ref, start):
    if ref.shape[1] == LANES:
        return ref[pl.ds(start, NP, stride=NP), :]
    return jnp.concatenate([ref[pl.ds(start + NP * b, 1), :] for b in range(NP)], axis=0)


def put_column(ref, start, value):
    if ref.shape[1] == LANES:
        ref[pl.ds(start, NP, stride=NP), :] = value
    else:
        for b in range(NP):
            ref[pl.ds(start + NP * b, 1), :] = value[b : b + 1, :]


def pack_face(grid, face, write):
    u = lax.axis_index("wide")
    even = (u % 2) == 0
    for b in range(NP // 2):
        top, bottom = face[b], face[b + NP // 2]
        up = jnp.where(grid.lower, grid.roll(bottom, -XSTEP), top)
        down = jnp.where(grid.lower, top, grid.roll(bottom, XSTEP))
        write(b, jnp.where(even, up, down), jnp.where(even, down, up))


def unpack_face(grid, read_a, read_b, nb):
    u = lax.axis_index("wide")
    even = (u % 2) == 0
    tops, bottoms = [], []
    for b in range(NP // 2):
        first, second = read_a(b), read_b(b)
        from_up = jnp.where(even, first, second)
        from_down = jnp.where(even, second, first)
        top = jnp.where(grid.lower, grid.roll(from_down, -XSTEP), grid.roll(from_up, XSTEP))
        bottom = jnp.where(grid.lower, from_down, from_up)
        tops.append(jnp.where(nb, top, 0.0))
        bottoms.append(jnp.where(nb, bottom, 0.0))
    return tops + bottoms


def pack_kernel(source_ref, reaction_ref, place_ref, out_ref, near_ref, sems):
    per = source_ref.shape[0]
    blocks = 2 * (PTS // LANES)
    places = pltpu.make_async_copy(place_ref, near_ref, sems.at[blocks])
    places.start()
    copies = []
    for k, ref in enumerate((source_ref, reaction_ref)):
        for q in range(PTS // LANES):
            n = len(copies)
            copy = pltpu.make_async_copy(
                ref.at[:, pl.ds(q * LANES, LANES)], out_ref.at[pl.ds(per * n, per), :], sems.at[n]
            )
            copy.start()
            copies.append(copy)
    v = lax.axis_index("narrow")
    groups = LANES // per
    row = lax.broadcasted_iota(jnp.int32, (NP, LANES), 0)
    lane = lax.broadcasted_iota(jnp.int32, (NP, LANES), 1)
    mine = (row == v // groups) & (lane // per == v % groups)
    places.wait()
    places = jnp.concatenate([near_ref[...].astype(jnp.float32)] * groups, axis=1)
    out_ref[per * blocks :, :] = jnp.where(mine, jnp.broadcast_to(places, (NP, LANES)), 0.0)
    for copy in copies:
        copy.wait()


class Arrived:
    def __init__(self, per, narrow, got_ref):
        self.per = per
        self.got = got_ref
        self.tiles = per * narrow // LANES
        self.groups = LANES // per
        self.blocks = PTS // LANES
        lanes = per * narrow
        spot = lax.broadcasted_iota(jnp.int32, (LANES, lanes), 1).astype(jnp.float32)
        row = lax.broadcasted_iota(jnp.int32, (LANES, lanes), 0)
        places = sum_of([got_ref[v, 2 * self.blocks * per :, :] for v in range(narrow)])
        came = jnp.zeros((1, lanes), jnp.float32)
        for t in range(self.tiles):
            new = jnp.transpose(jnp.broadcast_to(places[t : t + 1, :], (LANES, LANES)))
            new = jnp.concatenate([new] * self.tiles, axis=1)
            old = (row + t * LANES).astype(jnp.float32)
            came = came + jnp.sum(jnp.where(new == spot, old, 0.0), axis=0, keepdims=True)
        came = jnp.broadcast_to(came.astype(jnp.int32), (NP, lanes))
        owners = [came[:, t * LANES : (t + 1) * LANES] for t in range(self.tiles)]
        self.source = [(owner // LANES, owner % LANES) for owner in owners]

    def block(self, field, q, t):
        rows_of = pl.ds(self.per * (self.blocks * field + q), self.per)
        return jnp.concatenate(
            [self.got[self.groups * t + g, rows_of, :] for g in range(self.groups)], axis=0
        )

    def turned(self, old):
        old = [jnp.transpose(x) for x in old]
        for r in range(LANES // NP):
            for t, (home, lane) in enumerate(self.source):
                value = None
                for h in range(self.tiles):
                    pick = jnp.take_along_axis(old[h][NP * r : NP * (r + 1), :], lane, axis=1)
                    value = pick if value is None else jnp.where(home == h, pick, value)
                yield r, slice(t * LANES, (t + 1) * LANES), value


def first_kernel(per, narrow, wide, got_ref, rhs_ref, msg_a_ref, msg_b_ref, ends_ref):
    lanes = per * narrow
    grid = Grid(lanes, wide)
    arrived = Arrived(per, narrow, got_ref)
    tiles = range(arrived.tiles)
    for q in range(arrived.blocks):
        for r, cols, value in arrived.turned([arrived.block(0, q, t) for t in tiles]):
            at = q * LANES + NP * r
            a, b = at // PLANE, (at % PLANE) // NP
            mass = float(WEIGHTS[a]) * float(WEIGHTS[b])
            rhs_ref[pl.ds(at, NP), cols] = value * (mass * grid.w[:, cols])
    low = lax.broadcasted_iota(jnp.int32, (LANES, LANES), 1) < PLANE
    ends = [
        jnp.where(low, arrived.block(1, 0, t), arrived.block(1, arrived.blocks - 1, t)) for t in tiles
    ]
    for r, cols, value in arrived.turned(ends):
        ends_ref[pl.ds(NP * r, NP), cols] = value
    grid.assemble(rhs_ref)

    def write(part):
        def put(b, first, second):
            msg_a_ref[pl.ds(part * HALF + NP * b, NP), :] = first
            msg_b_ref[pl.ds(part * HALF + NP * b, NP), :] = second

        return put

    last = NP - 1
    pack_face(
        grid,
        [jnp.where(grid.lower, rhs_ref[rows(0, b), :], rhs_ref[rows(last, b), :]) for b in range(NP)],
        write(0),
    )
    part = []
    for b in range(NP):
        f = [rhs_ref[rows(a, b), :] for a in range(NP)]
        low = sum_of([float(STIFF[0, a]) * f[a] for a in range(1, NP)])
        high = sum_of([float(STIFF[last, a]) * f[a] for a in range(last)])
        part.append((float(WEIGHTS[b]) * grid.w) * jnp.where(grid.lower, low, high))
    pack_face(grid, part, write(1))
    pack_face(
        grid,
        [
            jnp.where(
                grid.lower, ends_ref[pl.ds(NP * b, NP), :], ends_ref[pl.ds(PLANE + NP * b, NP), :]
            )
            for b in range(NP)
        ],
        write(2),
    )


def middle_kernel(per, narrow, wide, got_ref, rhs_ref, reaction_ref, part_ref, flat_ref, tmp_ref):
    grid = Grid(per * narrow, wide)
    arrived = Arrived(per, narrow, got_ref)
    for q in range(arrived.blocks):
        blocks = [arrived.block(1, q, t) for t in range(arrived.tiles)]
        for r, cols, value in arrived.turned(blocks):
            reaction_ref[pl.ds(q * LANES + NP * r, NP), cols] = value
    grid.local(rhs_ref, reaction_ref, part_ref, tmp_ref)
    for b in range(NP):
        low, high = rhs_ref[rows(0, b), :], rhs_ref[rows(NP - 1, b), :]
        flat_ref[pl.ds(NP * b, NP), :] = jnp.where(grid.lower, low, high)
    flat = grid.plane_product(flat_ref, 0, tmp_ref)
    for b in range(NP):
        flat_ref[pl.ds(NP * b, NP), :] = flat[b]


def second_kernel(
    wide,
    rhs_ref,
    reaction_ref,
    part_ref,
    flat0_ref,
    got_a_ref,
    got_b_ref,
    v0_ref,
    v1_ref,
    v2_ref,
    msg_a_ref,
    msg_b_ref,
    face_ref,
    tmp_ref,
):
    lanes = rhs_ref.shape[1]
    grid = Grid(lanes, wide)
    nb = grid.has_neighbour()
    last = NP - 1

    def reader(part):
        def first(b):
            return got_a_ref[pl.ds(part * HALF + NP * b, NP), :]

        def second(b):
            return got_b_ref[pl.ds(part * HALF + NP * b, NP), :]

        return first, second

    extra = unpack_face(grid, *reader(0), nb)
    slopes = unpack_face(grid, *reader(1), nb)
    reactions = unpack_face(grid, *reader(2), nb)
    for b in range(NP):
        face_ref[pl.ds(NP * b, NP), :] = extra[b]
    flat = grid.plane_product(face_ref, 0, tmp_ref)
    pull = [jnp.where(grid.lower, float(STIFF[a, 0]), float(STIFF[a, last])) for a in range(NP)]
    w0 = float(WEIGHTS[0])
    for b in range(NP):
        wb = float(WEIGHTS[b]) * grid.w
        more = wb * extra[b]
        for a in range(1, last):
            r = rows(a, b)
            v0_ref[r, :] = rhs_ref[r, :]
            v1_ref[r, :] = part_ref[r, :] + pull[a] * more
        r_low, r_high = rows(0, b), rows(last, b)
        low = rhs_ref[r_low, :] + jnp.where(grid.lower, extra[b], 0.0)
        high = rhs_ref[r_high, :] + jnp.where(grid.lower, 0.0, extra[b])
        v0_ref[r_low, :] = low
        v0_ref[r_high, :] = high
        face = jnp.where(grid.lower, low, high)
        own = jnp.where(grid.lower, reaction_ref[r_low, :], reaction_ref[r_high, :])
        theirs = slopes[b] + w0 * (flat0_ref[pl.ds(NP * b, NP), :] + flat[b])
        theirs = theirs + wb * ((float(STIFF[0, 0]) + w0 * reactions[b]) * face)
        more_face = w0 * (flat[b] + own * more) + jnp.where(nb, theirs, 0.0)
        v1_ref[r_low, :] = part_ref[r_low, :] + pull[0] * more + jnp.where(grid.lower, more_face, 0.0)
        v1_ref[r_high, :] = (
            part_ref[r_high, :] + pull[last] * more + jnp.where(grid.lower, 0.0, more_face)
        )
    grid.assemble(v1_ref)
    grid.local(v1_ref, reaction_ref, v2_ref, tmp_ref)
    weight = grid.count_weights()
    parts = [[], [], [], []]
    for a in range(NP):
        terms = [[], [], [], []]
        for b in range(NP):
            r = rows(a, b)
            v0, v1, v2 = v0_ref[r, :], v1_ref[r, :], v2_ref[r, :]
            wt = weight[place(a)][place(b)]
            w1 = wt * v1
            for t, value in zip(terms, ((wt * v0) * v0, w1 * v0, w1 * v1, v1 * v2)):
                t.append(value)
        for p, t in zip(parts, terms):
            p.append(sum_of(t))
    row = grid.row
    out = jnp.zeros((NP, lanes), jnp.float32)
    for k, p in enumerate(parts):
        total = jnp.sum(sum_of(p), axis=0, keepdims=True)
        out = jnp.where(row == k, jnp.broadcast_to(total, (NP, lanes)), out)
    msg_a_ref[HALF : HALF + NP, :] = out
    msg_b_ref[HALF : HALF + NP, :] = out
    grid.assemble(v2_ref)

    def write(b, first, second):
        msg_a_ref[pl.ds(NP * b, NP), :] = first
        msg_b_ref[pl.ds(NP * b, NP), :] = second

    pack_face(
        grid,
        [jnp.where(grid.lower, v2_ref[rows(0, b), :], v2_ref[rows(last, b), :]) for b in range(NP)],
        write,
    )


def own_kernel(per, wide, *refs):
    *in_refs, scratch_ref = refs
    vector_refs, out_refs = in_refs[:3], in_refs[3:]
    lanes = vector_refs[0].shape[1]
    grid = Grid(lanes, wide)
    mine = pl.ds(pl.multiple_of(lax.axis_index("narrow") * per, per), per)
    weight = grid.count_weights()
    inverse = 1.0 / grid.w
    weight = [[w * inverse for w in line] for line in weight]
    for q in range(PTS // LANES):
        lines = []
        for r in range(LANES // NP):
            at = q * LANES + NP * r
            a, b = at // PLANE, (at % PLANE) // NP
            lines.append(float(1.0 / (WEIGHTS[a] * WEIGHTS[b])) * weight[place(a)][place(b)])
        scale = jnp.concatenate(lines, axis=0)
        fields = [ref[q * LANES : (q + 1) * LANES, :] for ref in vector_refs] + [scale]
        for k, (field, ref) in enumerate(zip(fields, out_refs)):
            for t in range(lanes // LANES):
                scratch_ref[k, t * LANES : (t + 1) * LANES, :] = jnp.transpose(
                    field[:, t * LANES : (t + 1) * LANES]
                )
            ref[:, q * LANES : (q + 1) * LANES] = scratch_ref[k, mine, :]


def last_kernel(
    wide,
    v0_ref,
    v1_ref,
    v2_ref,
    scale_ref,
    got_a_ref,
    got_b_ref,
    twin_b_ref,
    sums_ref,
    solution_ref,
    strong_ref,
    face_ref,
    turned_ref,
):
    per = v0_ref.shape[0]
    lanes = got_a_ref.shape[1]
    grid = Grid(lanes, wide)
    nb = grid.has_neighbour()
    v = lax.axis_index("narrow")
    core = v % 2
    extra = unpack_face(
        grid,
        lambda b: got_a_ref[pl.ds(NP * b, NP), :],
        lambda b: jnp.where(
            core == 0, twin_b_ref[pl.ds(NP * b, NP), :], got_b_ref[pl.ds(NP * b, NP), :]
        ),
        nb,
    )
    for b in range(NP):
        face_ref[pl.ds(NP * b, NP), :] = extra[b]
        face_ref[pl.ds(PLANE + NP * b, NP), :] = extra[b]
    for t in range(lanes // LANES):
        turned_ref[t * LANES : (t + 1) * LANES, :] = jnp.transpose(
            face_ref[:, t * LANES : (t + 1) * LANES]
        )
    face = turned_ref[pl.ds(pl.multiple_of(v * per, per), per), :]
    spot = lax.broadcasted_iota(jnp.int32, (per, LANES), 1)
    layer = lax.broadcasted_iota(jnp.int32, (per, LANES), 0) // XSTEP
    ends = {
        0: jnp.where((spot < PLANE) & (layer == 0), face, 0.0),
        PTS // LANES - 1: jnp.where((spot >= PLANE) & (layer == BX - 1), face, 0.0),
    }
    g = [jnp.sum(sums_ref[k : k + 1, :], axis=1, keepdims=True) for k in range(4)]
    alpha = g[0] / g[1]
    norm = g[0] - 2.0 * alpha * g[1] + (alpha * alpha) * g[2]
    beta = norm / g[0]
    one = 1.0 + beta
    curve = one * one * g[1] - 2.0 * one * alpha * g[2] + (alpha * alpha) * g[3]
    step = norm / curve
    first = jnp.broadcast_to(alpha + step * one, (per, LANES))
    second = jnp.broadcast_to(alpha * step, (per, LANES))
    for q in range(PTS // LANES):
        at = (slice(None), slice(q * LANES, (q + 1) * LANES))
        v0, v1, v2 = v0_ref[at], v1_ref[at], v2_ref[at]
        if q in ends:
            v2 = v2 + ends[q]
        solution_ref[at] = first * v0 - second * v1
        strong_ref[at] = (v0 - first * v1 + second * v2) * scale_ref[at]


VM = pl.BlockSpec(memory_space=pltpu.VMEM)


def call(kernel, out_shapes, in_specs, scratch=(), name=None):
    return pl.pallas_call(
        kernel,
        out_shape=[jax.ShapeDtypeStruct(s, jnp.float32) for s in out_shapes],
        in_specs=in_specs,
        out_specs=[VM] * len(out_shapes),
        scratch_shapes=list(scratch),
        compiler_params=pltpu.CompilerParams(vmem_limit_bytes=16 * 1024 * 1024),
        name=name,
    )


def in_hbm(*arrays):
    return [pltpu.with_memory_space_constraint(x, pltpu.HBM) for x in arrays]


def swap(x, wide, narrow, *partner_of):
    pairs = []
    for u in range(wide):
        to = [partner(u) for partner in partner_of]
        idle = [not 0 <= t < wide for t in to]
        for v in range(narrow):
            k = v % len(to)
            away = v ^ 1 if all(idle) else v ^ 2
            target = u * narrow + away if idle[k] else to[k] * narrow + v
            pairs.append((u * narrow + v, target))
    return lax.ppermute(x, ("wide", "narrow"), pairs)


def same_pair(u):
    return u ^ 1


def next_pair(u):
    return u + 1 if u % 2 else u - 1


def twin(x, narrow):
    return lax.ppermute(x, "narrow", [(v, v ^ 1) for v in range(narrow)])


def finish(msg_a, msg_b, wide, narrow):
    sums = msg_a[HALF:]
    if wide == 8:
        got_b = swap(msg_b, wide, narrow, lambda u: u ^ 4, next_pair)
        more = swap(sums, wide, narrow, lambda u: u ^ 2, lambda u: u ^ 6)
        twin_b = twin(got_b[:HALF], narrow)
        even = lax.axis_index("narrow") % 2 == 0
        part = more + jnp.where(even, sums + got_b[HALF:], 0.0)
        got_a = swap(jnp.concatenate([msg_a[:HALF], part], axis=0), wide, narrow, same_pair)
        cross = [
            (u * narrow + v, (u ^ 1) * narrow + (v ^ 1)) for u in range(wide) for v in range(narrow)
        ]
        theirs = got_a[HALF:] + lax.ppermute(part, ("wide", "narrow"), cross)
        total = (part + twin(part, narrow)) + theirs
        return got_a[:HALF], got_b[:HALF], twin_b, total
    got_a = swap(msg_a, wide, narrow, same_pair)
    got_b = swap(msg_b, wide, narrow, next_pair)[:HALF]
    return got_a[:HALF], got_b, got_b, lax.psum(sums, "wide")


def local(wide, narrow, source_old, reaction_old, new_place):
    per = source_old.shape[1]
    lanes = per * narrow
    blocks = 2 * (PTS // LANES)
    packed = call(
        pack_kernel,
        [(blocks * per + NP, LANES)],
        [pl.BlockSpec(memory_space=pltpu.HBM)] * 3,
        [pltpu.VMEM((1, per), jnp.int32), pltpu.SemaphoreType.DMA((blocks + 1,))],
        name="pack",
    )(*in_hbm(source_old.T, reaction_old.T, new_place.reshape(1, per)))[0]
    full = (PTS, lanes)
    got = lax.all_gather(packed, "narrow")
    rhs, msg_a, msg_b = call(
        functools.partial(first_kernel, per, narrow, wide),
        [full, (3 * HALF, lanes), (3 * HALF, lanes)],
        [VM],
        [pltpu.VMEM((2 * PLANE, lanes), jnp.float32)],
        name="first",
    )(got)
    got_a = swap(msg_a, wide, narrow, same_pair)
    got_b = swap(msg_b, wide, narrow, next_pair)
    reaction, part, flat = call(
        functools.partial(middle_kernel, per, narrow, wide),
        [full, full, (PLANE, lanes)],
        [VM] * 2,
        [pltpu.VMEM((PLANE, lanes), jnp.float32)],
        name="middle",
    )(got, rhs)
    v0, v1, v2, msg_a, msg_b = call(
        functools.partial(second_kernel, wide),
        [full, full, full, (HALF + NP, lanes), (HALF + NP, lanes)],
        [VM] * 6,
        [pltpu.VMEM((PLANE, lanes), jnp.float32), pltpu.VMEM((PLANE, lanes), jnp.float32)],
        name="second",
    )(rhs, reaction, part, flat, got_a, got_b)
    arrived = finish(msg_a, msg_b, wide, narrow)
    own = call(
        functools.partial(own_kernel, per, wide),
        [(per, PTS)] * 4,
        [VM] * 3,
        [pltpu.VMEM((4, lanes, LANES), jnp.float32)],
        name="own",
    )(v0, v1, v2)
    out = call(
        functools.partial(last_kernel, wide),
        [(per, PTS), (per, PTS)],
        [VM] * 8,
        [pltpu.VMEM((LANES, lanes), jnp.float32), pltpu.VMEM((lanes, LANES), jnp.float32)],
        name="last",
    )(*own, *arrived)
    return tuple(x.T for x in out)


def solution(mesh):
    placed = (P(None, ("wide", "narrow")), P(None, ("wide", "narrow")), P(("wide", "narrow")))
    return jax.shard_map(
        functools.partial(local, mesh.shape["wide"], mesh.shape["narrow"]),
        mesh=mesh,
        in_specs=placed,
        out_specs=(P(None, ("wide", "narrow")), P(None, ("wide", "narrow"))),
        check_vma=False,
    )
```

```python
import functools

import jax
import jax.numpy as jnp
import numpy as np
from jax import lax
from jax.experimental import pallas as pl
from jax.experimental.pallas import tpu as pltpu
from jax.sharding import PartitionSpec as P


NP = 8
BX = 2
BY = 4
EZ = 4
PTS = NP**3
PLANE = NP * NP
LANES = 128
HALF = PLANE // 2
XSTEP = BY * EZ

DIFFUSION = 0.05


def legendre_values(abscissa, num_points):
    columns = [np.ones(abscissa.shape), abscissa]
    for degree in range(2, num_points):
        columns.append(
            ((2 * degree - 1) * abscissa * columns[degree - 1] - (degree - 1) * columns[degree - 2])
            / degree
        )
    return np.stack(columns, 1)


def gll_tables(num_points):
    poly_order = num_points - 1
    abscissa = np.cos(np.pi * np.arange(num_points) / poly_order)
    for _ in range(60):
        legendre = legendre_values(abscissa, num_points)
        abscissa = abscissa - (abscissa * legendre[:, poly_order] - legendre[:, poly_order - 1]) / (
            num_points * legendre[:, poly_order]
        )
    legendre = legendre_values(abscissa, num_points)
    top_values = legendre[:, poly_order][::-1]
    abscissa = abscissa[::-1]
    weights = 2.0 / (poly_order * num_points * top_values**2)
    identity = np.eye(num_points)
    differ = np.where(identity > 0, 1.0, abscissa[:, None] - abscissa[None, :])
    deriv_table = np.where(identity > 0, 0.0, top_values[:, None] / (top_values[None, :] * differ))
    quarter = poly_order * num_points / 4.0
    edge_fix = np.concatenate([np.array([-quarter]), np.zeros(num_points - 2), np.array([quarter])])
    deriv_table = deriv_table + identity * edge_fix[:, None]
    return (weights, deriv_table)


def stiffness():
    weights, deriv = gll_tables(NP)
    stiff = DIFFUSION * deriv.T @ np.diag(weights) @ deriv
    return weights, 0.5 * (stiff + stiff.T)


WEIGHTS, STIFF = stiffness()
EVEN = 0.5 * (STIFF[:4, :4] + STIFF[:4, 7:3:-1])
ODD = 0.5 * (STIFF[:4, :4] - STIFF[:4, 7:3:-1])


def apply_stiff(f):
    even = [f[j] + f[7 - j] for j in range(4)]
    odd = [f[j] - f[7 - j] for j in range(4)]
    out = [None] * NP
    for i in range(4):
        e = sum_of([float(EVEN[i, j]) * even[j] for j in range(4)])
        o = sum_of([float(ODD[i, j]) * odd[j] for j in range(4)])
        out[i] = e + o
        out[7 - i] = e - o
    return out


def sum_of(terms):
    while len(terms) > 1:
        terms = [
            terms[k] + terms[k + 1] if k + 1 < len(terms) else terms[k]
            for k in range(0, len(terms), 2)
        ]
    return terms[0]


class Grid:
    def __init__(self, lanes, wide):
        self.lanes = lanes
        self.wide = wide
        self.lane = lax.broadcasted_iota(jnp.int32, (NP, lanes), 1)
        self.row = lax.broadcasted_iota(jnp.int32, (NP, lanes), 0)
        self.s = self.lane & (EZ - 1)
        self.j = (self.lane // EZ) & (BY - 1)
        self.i = (self.lane // XSTEP) & (BX - 1)
        self.lower = self.i == 0
        w = jnp.full((NP, lanes), float(WEIGHTS[0]), jnp.float32)
        for c in range(1, NP):
            w = jnp.where(self.row == c, float(WEIGHTS[c]), w)
        self.w = w

    def has_neighbour(self):
        u = lax.axis_index("wide")
        low = jnp.where(u > 0, 1, 0)
        high = jnp.where(u < self.wide - 1, 1, 0)
        return jnp.where(self.lower, low, high) > 0

    def roll(self, x, shift):
        return pltpu.roll(x, shift % self.lanes, axis=x.ndim - 1)

    def share(self, lo, hi, axis):
        if axis == "x":
            new_lo = lo + jnp.where(self.lower, 0.0, self.roll(hi, XSTEP))
            new_hi = hi + jnp.where(self.lower, self.roll(lo, -XSTEP), 0.0)
        elif axis == "y":
            block = BX * XSTEP
            jump = block - (BY - 1) * EZ
            from_hi = jnp.where(self.j > 0, self.roll(hi, EZ), self.roll(hi, jump))
            from_lo = jnp.where(self.j < BY - 1, self.roll(lo, -EZ), self.roll(lo, -jump))
            first = (self.j == 0) & (self.lane < block)
            last = (self.j == BY - 1) & (self.lane >= self.lanes - block)
            new_lo = lo + jnp.where(first, 0.0, from_hi)
            new_hi = hi + jnp.where(last, 0.0, from_lo)
        else:
            new_lo = lo + jnp.where(self.s > 0, self.roll(hi, 1), 0.0)
            new_hi = hi + jnp.where(self.s < EZ - 1, self.roll(lo, -1), 0.0)
        return new_lo, new_hi

    def assemble(self, ref):
        for b in range(NP):
            lo, hi = rows(0, b), rows(NP - 1, b)
            ref[lo, :], ref[hi, :] = self.share(ref[lo, :], ref[hi, :], "x")
        for a in range(NP):
            lo, hi = rows(a, 0), rows(a, NP - 1)
            ref[lo, :], ref[hi, :] = self.share(ref[lo, :], ref[hi, :], "y")
        for a in range(NP):
            lo, hi = self.share(column(ref, PLANE * a), column(ref, PLANE * a + NP - 1), "z")
            put_column(ref, PLANE * a, lo)
            put_column(ref, PLANE * a + NP - 1, hi)

    def plane_product(self, f_ref, base, out_ref):
        z = apply_stiff([column(f_ref, base + c) for c in range(NP)])
        for c in range(NP):
            put_column(out_ref, c, self.w * z[c])
        y = apply_stiff([f_ref[pl.ds(base + NP * b, NP), :] for b in range(NP)])
        return [self.w * y[b] + out_ref[pl.ds(NP * b, NP), :] for b in range(NP)]

    def local(self, f_ref, massed_ref, out_ref, tmp_ref):
        for a in range(NP):
            flat = self.plane_product(f_ref, PLANE * a, tmp_ref)
            wa = float(WEIGHTS[a])
            for b in range(NP):
                r = rows(a, b)
                value = wa * flat[b]
                if massed_ref is not None:
                    value = value + massed_ref[r, :] * f_ref[r, :]
                out_ref[r, :] = value
        for b in range(NP):
            x = apply_stiff([f_ref[rows(a, b), :] for a in range(NP)])
            wb = float(WEIGHTS[b]) * self.w
            for a in range(NP):
                r = rows(a, b)
                out_ref[r, :] = out_ref[r, :] + wb * x[a]

    def count_weights(self):
        nb = self.has_neighbour()
        one = jnp.ones((NP, self.lanes), jnp.float32)
        x0 = jnp.where(~self.lower | nb, 0.5, one)
        x7 = jnp.where(self.lower | nb, 0.5, one)
        block = BX * XSTEP
        first = (self.j == 0) & (self.lane < block)
        last = (self.j == BY - 1) & (self.lane >= self.lanes - block)
        y0 = jnp.where(first, one, 0.5)
        y7 = jnp.where(last, one, 0.5)
        z = jnp.where((self.row == 0) & (self.s > 0), 0.5, one)
        z = jnp.where((self.row == NP - 1) & (self.s < EZ - 1), 0.5, z)
        zx = [z * x0, z, z * x7]
        return [[m * y0, m, m * y7] for m in zx]


def place(a):
    return 0 if a == 0 else (2 if a == NP - 1 else 1)


def rows(a, b):
    return pl.ds(PLANE * a + NP * b, NP)


def column(ref, start):
    if ref.shape[1] == LANES:
        return ref[pl.ds(start, NP, stride=NP), :]
    return jnp.concatenate([ref[pl.ds(start + NP * b, 1), :] for b in range(NP)], axis=0)


def put_column(ref, start, value):
    if ref.shape[1] == LANES:
        ref[pl.ds(start, NP, stride=NP), :] = value
    else:
        for b in range(NP):
            ref[pl.ds(start + NP * b, 1), :] = value[b : b + 1, :]


def pack_face(grid, face, write):
    u = lax.axis_index("wide")
    even = (u % 2) == 0
    for b in range(NP // 2):
        top, bottom = face[b], face[b + NP // 2]
        up = jnp.where(grid.lower, grid.roll(bottom, -XSTEP), top)
        down = jnp.where(grid.lower, top, grid.roll(bottom, XSTEP))
        write(b, jnp.where(even, up, down), jnp.where(even, down, up))


def unpack_face(grid, read_a, read_b, nb):
    u = lax.axis_index("wide")
    even = (u % 2) == 0
    tops, bottoms = [], []
    for b in range(NP // 2):
        first, second = read_a(b), read_b(b)
        from_up = jnp.where(even, first, second)
        from_down = jnp.where(even, second, first)
        top = jnp.where(grid.lower, grid.roll(from_down, -XSTEP), grid.roll(from_up, XSTEP))
        bottom = jnp.where(grid.lower, from_down, from_up)
        tops.append(jnp.where(nb, top, 0.0))
        bottoms.append(jnp.where(nb, bottom, 0.0))
    return tops + bottoms


def pack_kernel(source_ref, reaction_ref, place_ref, early_ref, late_ref, near_ref, sems):
    per = source_ref.shape[0]
    blocks = PTS // LANES
    places = pltpu.make_async_copy(place_ref, near_ref, sems.at[2 * blocks])
    places.start()
    copies = []
    for ref, out_ref in ((reaction_ref, late_ref), (source_ref, early_ref)):
        for q in range(blocks):
            copy = pltpu.make_async_copy(
                ref.at[:, pl.ds(q * LANES, LANES)],
                out_ref.at[pl.ds(per * q, per), :],
                sems.at[len(copies)],
            )
            copy.start()
            copies.append(copy)
    places.wait()
    near = jnp.concatenate([near_ref[...].astype(jnp.float32)] * (LANES // per), axis=1)
    early_ref[per * (blocks + 1) :, :] = jnp.broadcast_to(near, (NP, LANES))
    for copy in copies:
        copy.wait()
    low = lax.broadcasted_iota(jnp.int32, (per, LANES), 1) < PLANE
    early_ref[per * blocks : per * (blocks + 1), :] = jnp.where(
        low, late_ref[:per, :], late_ref[per * (blocks - 1) :, :]
    )


def came_from(per, refs):
    lanes = per * len(refs)
    tiles, groups = lanes // LANES, LANES // per
    at = pl.ds(per * (PTS // LANES + 1), NP)
    group = lax.broadcasted_iota(jnp.int32, (NP, LANES), 1) // per
    spot = lax.broadcasted_iota(jnp.int32, (LANES, lanes), 1).astype(jnp.float32)
    row = lax.broadcasted_iota(jnp.int32, (LANES, lanes), 0)
    came = jnp.zeros((1, lanes), jnp.float32)
    for t in range(tiles):
        new = refs[groups * t][at, :]
        for g in range(1, groups):
            new = jnp.where(group == g, refs[groups * t + g][at, :], new)
        new = jnp.transpose(jnp.concatenate([new] * (LANES // NP), axis=0))
        new = jnp.concatenate([new] * tiles, axis=1)
        old = (row + t * LANES).astype(jnp.float32)
        came = came + jnp.sum(jnp.where(new == spot, old, 0.0), axis=0, keepdims=True)
    return jnp.broadcast_to(came.astype(jnp.int32), (NP, lanes))


def turned(per, refs, start, came):
    tiles, groups = per * len(refs) // LANES, LANES // per
    old = [
        jnp.transpose(
            jnp.concatenate([refs[groups * t + g][pl.ds(start, per), :] for g in range(groups)], axis=0)
        )
        for t in range(tiles)
    ]
    for r in range(LANES // NP):
        for t in range(tiles):
            cols = slice(t * LANES, (t + 1) * LANES)
            home, lane = came[:, cols] // LANES, came[:, cols] % LANES
            value = None
            for h in range(tiles):
                pick = jnp.take_along_axis(old[h][NP * r : NP * (r + 1), :], lane, axis=1)
                value = pick if value is None else jnp.where(home == h, pick, value)
            yield r, cols, value


def first_kernel(per, narrow, wide, *refs):
    got, (rhs_ref, came_ref, msg_a_ref, msg_b_ref, ends_ref) = refs[:narrow], refs[narrow:]
    grid = Grid(per * narrow, wide)
    blocks = PTS // LANES
    came = came_from(per, got)
    came_ref[...] = came
    for q in range(blocks):
        for r, cols, value in turned(per, got, per * q, came):
            at = q * LANES + NP * r
            a, b = at // PLANE, (at % PLANE) // NP
            mass = float(WEIGHTS[a]) * float(WEIGHTS[b])
            rhs_ref[pl.ds(at, NP), cols] = value * (mass * grid.w[:, cols])
    for r, cols, value in turned(per, got, per * blocks, came):
        ends_ref[pl.ds(NP * r, NP), cols] = value
    grid.assemble(rhs_ref)

    def write(part):
        def put(b, first, second):
            msg_a_ref[pl.ds(part * HALF + NP * b, NP), :] = first
            msg_b_ref[pl.ds(part * HALF + NP * b, NP), :] = second

        return put

    last = NP - 1
    pack_face(
        grid,
        [jnp.where(grid.lower, rhs_ref[rows(0, b), :], rhs_ref[rows(last, b), :]) for b in range(NP)],
        write(0),
    )
    part = []
    for b in range(NP):
        f = [rhs_ref[rows(a, b), :] for a in range(NP)]
        low = sum_of([float(STIFF[0, a]) * f[a] for a in range(1, NP)])
        high = sum_of([float(STIFF[last, a]) * f[a] for a in range(last)])
        part.append((float(WEIGHTS[b]) * grid.w) * jnp.where(grid.lower, low, high))
    pack_face(grid, part, write(1))
    pack_face(
        grid,
        [
            jnp.where(
                grid.lower, ends_ref[pl.ds(NP * b, NP), :], ends_ref[pl.ds(PLANE + NP * b, NP), :]
            )
            for b in range(NP)
        ],
        write(2),
    )


def reaction_kernel(per, narrow, wide, *refs):
    got, (came_ref, massed_ref) = refs[:narrow], refs[narrow:]
    grid = Grid(per * narrow, wide)
    came = came_ref[...]
    for q in range(PTS // LANES):
        for r, cols, value in turned(per, got, per * q, came):
            at = q * LANES + NP * r
            a, b = at // PLANE, (at % PLANE) // NP
            mass = float(WEIGHTS[a]) * float(WEIGHTS[b])
            massed_ref[pl.ds(at, NP), cols] = value * (mass * grid.w[:, cols])


def middle_kernel(wide, rhs_ref, part_ref, flat_ref, tmp_ref):
    grid = Grid(rhs_ref.shape[1], wide)
    grid.local(rhs_ref, None, part_ref, tmp_ref)
    for b in range(NP):
        low, high = rhs_ref[rows(0, b), :], rhs_ref[rows(NP - 1, b), :]
        flat_ref[pl.ds(NP * b, NP), :] = jnp.where(grid.lower, low, high)
    flat = grid.plane_product(flat_ref, 0, tmp_ref)
    for b in range(NP):
        flat_ref[pl.ds(NP * b, NP), :] = flat[b]


def second_kernel(
    wide,
    rhs_ref,
    massed_ref,
    part_ref,
    flat0_ref,
    got_a_ref,
    got_b_ref,
    v0_ref,
    v1_ref,
    v2_ref,
    msg_a_ref,
    msg_b_ref,
    face_ref,
    tmp_ref,
):
    lanes = rhs_ref.shape[1]
    grid = Grid(lanes, wide)
    nb = grid.has_neighbour()
    last = NP - 1

    def reader(part):
        def first(b):
            return got_a_ref[pl.ds(part * HALF + NP * b, NP), :]

        def second(b):
            return got_b_ref[pl.ds(part * HALF + NP * b, NP), :]

        return first, second

    extra = unpack_face(grid, *reader(0), nb)
    slopes = unpack_face(grid, *reader(1), nb)
    reactions = unpack_face(grid, *reader(2), nb)
    for b in range(NP):
        face_ref[pl.ds(NP * b, NP), :] = extra[b]
    flat = grid.plane_product(face_ref, 0, tmp_ref)
    pull = [jnp.where(grid.lower, float(STIFF[a, 0]), float(STIFF[a, last])) for a in range(NP)]
    w0 = float(WEIGHTS[0])
    for b in range(NP):
        wb = float(WEIGHTS[b]) * grid.w
        more = wb * extra[b]
        for a in range(1, last):
            r = rows(a, b)
            value = rhs_ref[r, :]
            v0_ref[r, :] = value
            v1_ref[r, :] = part_ref[r, :] + pull[a] * more + massed_ref[r, :] * value
        r_low, r_high = rows(0, b), rows(last, b)
        low = rhs_ref[r_low, :] + jnp.where(grid.lower, extra[b], 0.0)
        high = rhs_ref[r_high, :] + jnp.where(grid.lower, 0.0, extra[b])
        v0_ref[r_low, :] = low
        v0_ref[r_high, :] = high
        face = jnp.where(grid.lower, low, high)
        theirs = slopes[b] + w0 * (flat0_ref[pl.ds(NP * b, NP), :] + flat[b])
        theirs = theirs + wb * ((float(STIFF[0, 0]) + w0 * reactions[b]) * face)
        end = w0 * flat[b] + jnp.where(nb, theirs, 0.0)
        v1_low = part_ref[r_low, :] + pull[0] * more + massed_ref[r_low, :] * low
        v1_high = part_ref[r_high, :] + pull[last] * more + massed_ref[r_high, :] * high
        v1_ref[r_low, :] = v1_low + jnp.where(grid.lower, end, 0.0)
        v1_ref[r_high, :] = v1_high + jnp.where(grid.lower, 0.0, end)
    grid.assemble(v1_ref)
    grid.local(v1_ref, massed_ref, v2_ref, tmp_ref)
    weight = grid.count_weights()
    parts = [[], [], [], []]
    for a in range(NP):
        terms = [[], [], [], []]
        for b in range(NP):
            r = rows(a, b)
            v0, v1, v2 = v0_ref[r, :], v1_ref[r, :], v2_ref[r, :]
            wt = weight[place(a)][place(b)]
            w1 = wt * v1
            for t, value in zip(terms, ((wt * v0) * v0, w1 * v0, w1 * v1, v1 * v2)):
                t.append(value)
        for p, t in zip(parts, terms):
            p.append(sum_of(t))
    row = grid.row
    out = jnp.zeros((NP, lanes), jnp.float32)
    for k, p in enumerate(parts):
        total = jnp.sum(sum_of(p), axis=0, keepdims=True)
        out = jnp.where(row == k, jnp.broadcast_to(total, (NP, lanes)), out)
    msg_a_ref[HALF : HALF + NP, :] = out
    msg_b_ref[HALF : HALF + NP, :] = out
    grid.assemble(v2_ref)

    def write(b, first, second):
        msg_a_ref[pl.ds(NP * b, NP), :] = first
        msg_b_ref[pl.ds(NP * b, NP), :] = second

    pack_face(
        grid,
        [jnp.where(grid.lower, v2_ref[rows(0, b), :], v2_ref[rows(last, b), :]) for b in range(NP)],
        write,
    )


def own_kernel(per, wide, *refs):
    *in_refs, scratch_ref = refs
    vector_refs, out_refs = in_refs[:3], in_refs[3:]
    lanes = vector_refs[0].shape[1]
    grid = Grid(lanes, wide)
    mine = pl.ds(pl.multiple_of(lax.axis_index("narrow") * per, per), per)
    weight = grid.count_weights()
    inverse = 1.0 / grid.w
    weight = [[w * inverse for w in line] for line in weight]
    for q in range(PTS // LANES):
        lines = []
        for r in range(LANES // NP):
            at = q * LANES + NP * r
            a, b = at // PLANE, (at % PLANE) // NP
            lines.append(float(1.0 / (WEIGHTS[a] * WEIGHTS[b])) * weight[place(a)][place(b)])
        scale = jnp.concatenate(lines, axis=0)
        fields = [ref[q * LANES : (q + 1) * LANES, :] for ref in vector_refs] + [scale]
        for k, (field, ref) in enumerate(zip(fields, out_refs)):
            for t in range(lanes // LANES):
                scratch_ref[k, t * LANES : (t + 1) * LANES, :] = jnp.transpose(
                    field[:, t * LANES : (t + 1) * LANES]
                )
            ref[:, q * LANES : (q + 1) * LANES] = scratch_ref[k, mine, :]


def last_kernel(
    wide,
    v0_ref,
    v1_ref,
    v2_ref,
    scale_ref,
    got_a_ref,
    got_b_ref,
    twin_b_ref,
    sums_ref,
    solution_ref,
    strong_ref,
    face_ref,
    turned_ref,
):
    per = v0_ref.shape[0]
    lanes = got_a_ref.shape[1]
    grid = Grid(lanes, wide)
    nb = grid.has_neighbour()
    v = lax.axis_index("narrow")
    core = v % 2
    extra = unpack_face(
        grid,
        lambda b: got_a_ref[pl.ds(NP * b, NP), :],
        lambda b: jnp.where(
            core == 0, twin_b_ref[pl.ds(NP * b, NP), :], got_b_ref[pl.ds(NP * b, NP), :]
        ),
        nb,
    )
    for b in range(NP):
        face_ref[pl.ds(NP * b, NP), :] = extra[b]
        face_ref[pl.ds(PLANE + NP * b, NP), :] = extra[b]
    for t in range(lanes // LANES):
        turned_ref[t * LANES : (t + 1) * LANES, :] = jnp.transpose(
            face_ref[:, t * LANES : (t + 1) * LANES]
        )
    face = turned_ref[pl.ds(pl.multiple_of(v * per, per), per), :]
    spot = lax.broadcasted_iota(jnp.int32, (per, LANES), 1)
    layer = lax.broadcasted_iota(jnp.int32, (per, LANES), 0) // XSTEP
    ends = {
        0: jnp.where((spot < PLANE) & (layer == 0), face, 0.0),
        PTS // LANES - 1: jnp.where((spot >= PLANE) & (layer == BX - 1), face, 0.0),
    }
    g = [jnp.sum(sums_ref[k : k + 1, :], axis=1, keepdims=True) for k in range(4)]
    alpha = g[0] / g[1]
    norm = g[0] - 2.0 * alpha * g[1] + (alpha * alpha) * g[2]
    beta = norm / g[0]
    one = 1.0 + beta
    curve = one * one * g[1] - 2.0 * one * alpha * g[2] + (alpha * alpha) * g[3]
    step = norm / curve
    first = jnp.broadcast_to(alpha + step * one, (per, LANES))
    second = jnp.broadcast_to(alpha * step, (per, LANES))
    for q in range(PTS // LANES):
        at = (slice(None), slice(q * LANES, (q + 1) * LANES))
        v0, v1, v2 = v0_ref[at], v1_ref[at], v2_ref[at]
        if q in ends:
            v2 = v2 + ends[q]
        solution_ref[at] = first * v0 - second * v1
        strong_ref[at] = (v0 - first * v1 + second * v2) * scale_ref[at]


VM = pl.BlockSpec(memory_space=pltpu.VMEM)


def call(kernel, out_shapes, in_specs, scratch=()):
    return pl.pallas_call(
        kernel,
        out_shape=[
            jax.ShapeDtypeStruct(*(s if isinstance(s[0], tuple) else (s, jnp.float32)))
            for s in out_shapes
        ],
        in_specs=in_specs,
        out_specs=[VM] * len(out_shapes),
        scratch_shapes=list(scratch),
        compiler_params=pltpu.CompilerParams(vmem_limit_bytes=16 * 1024 * 1024),
    )


def in_hbm(*arrays):
    return [pltpu.with_memory_space_constraint(x, pltpu.HBM) for x in arrays]


def swap(x, wide, narrow, *partner_of):
    pairs = []
    for u in range(wide):
        to = [partner(u) for partner in partner_of]
        idle = [not 0 <= t < wide for t in to]
        for v in range(narrow):
            k = v % len(to)
            away = v ^ 1 if all(idle) else v ^ 2
            target = u * narrow + away if idle[k] else to[k] * narrow + v
            pairs.append((u * narrow + v, target))
    return lax.ppermute(x, ("wide", "narrow"), pairs)


def same_pair(u):
    return u ^ 1


def next_pair(u):
    return u + 1 if u % 2 else u - 1


def far_copy(x, narrow):
    if narrow != 4:
        return list(lax.all_gather(x, "narrow"))
    return [x, lax.ppermute(x, "narrow", [(v, v ^ 2) for v in range(narrow)])]


def near_copies(blocks, narrow):
    if narrow != 4:
        return blocks
    return blocks + [twin(x, narrow) for x in blocks]


def twin(x, narrow):
    return lax.ppermute(x, "narrow", [(v, v ^ 1) for v in range(narrow)])


def finish(msg_a, msg_b, wide, narrow):
    sums = msg_a[HALF:]
    if wide == 8:
        got_b = swap(msg_b, wide, narrow, lambda u: u ^ 4, next_pair)
        more = swap(sums, wide, narrow, lambda u: u ^ 2, lambda u: u ^ 6)
        twin_b = twin(got_b[:HALF], narrow)
        even = lax.axis_index("narrow") % 2 == 0
        part = more + jnp.where(even, sums + got_b[HALF:], 0.0)
        got_a = swap(jnp.concatenate([msg_a[:HALF], part], axis=0), wide, narrow, same_pair)
        cross = [
            (u * narrow + v, (u ^ 1) * narrow + (v ^ 1)) for u in range(wide) for v in range(narrow)
        ]
        theirs = got_a[HALF:] + lax.ppermute(part, ("wide", "narrow"), cross)
        total = (part + twin(part, narrow)) + theirs
        return got_a[:HALF], got_b[:HALF], twin_b, total
    got_a = swap(msg_a, wide, narrow, same_pair)
    got_b = swap(msg_b, wide, narrow, next_pair)[:HALF]
    return got_a[:HALF], got_b, got_b, lax.psum(sums, "wide")


def local(wide, narrow, source_old, reaction_old, new_place):
    per = source_old.shape[1]
    lanes = per * narrow
    blocks = PTS // LANES
    early, late = call(
        pack_kernel,
        [(per * (blocks + 1) + NP, LANES), (per * blocks, LANES)],
        [pl.BlockSpec(memory_space=pltpu.HBM)] * 3,
        [pltpu.VMEM((1, per), jnp.int32), pltpu.SemaphoreType.DMA((2 * blocks + 1,))],
    )(*in_hbm(source_old.T, reaction_old.T, new_place.reshape(1, per)))
    full = (PTS, lanes)
    late = far_copy(late, narrow)
    early = near_copies(far_copy(early, narrow), narrow)
    rhs, came, msg_a, msg_b = call(
        functools.partial(first_kernel, per, narrow, wide),
        [full, ((NP, lanes), jnp.int32), (3 * HALF, lanes), (3 * HALF, lanes)],
        [VM] * narrow,
        [pltpu.VMEM((2 * PLANE, lanes), jnp.float32)],
    )(*early)
    got_a = swap(msg_a, wide, narrow, same_pair)
    got_b = swap(msg_b, wide, narrow, next_pair)
    part, flat = call(
        functools.partial(middle_kernel, wide),
        [full, (PLANE, lanes)],
        [VM],
        [pltpu.VMEM((PLANE, lanes), jnp.float32)],
    )(rhs)
    late, came = lax.optimization_barrier((late, came))
    late = near_copies(late, narrow)
    massed = call(
        functools.partial(reaction_kernel, per, narrow, wide), [full], [VM] * (narrow + 1)
    )(*late, came)[0]
    v0, v1, v2, msg_a, msg_b = call(
        functools.partial(second_kernel, wide),
        [full, full, full, (HALF + NP, lanes), (HALF + NP, lanes)],
        [VM] * 6,
        [pltpu.VMEM((PLANE, lanes), jnp.float32), pltpu.VMEM((PLANE, lanes), jnp.float32)],
    )(rhs, massed, part, flat, got_a, got_b)
    arrived = finish(msg_a, msg_b, wide, narrow)
    own = call(
        functools.partial(own_kernel, per, wide),
        [(per, PTS)] * 4,
        [VM] * 3,
        [pltpu.VMEM((4, lanes, LANES), jnp.float32)],
    )(v0, v1, v2)
    out = call(
        functools.partial(last_kernel, wide),
        [(per, PTS), (per, PTS)],
        [VM] * 8,
        [pltpu.VMEM((LANES, lanes), jnp.float32), pltpu.VMEM((lanes, LANES), jnp.float32)],
    )(*own, *arrived)
    return tuple(x.T for x in out)


def solution(mesh):
    placed = (P(None, ("wide", "narrow")), P(None, ("wide", "narrow")), P(("wide", "narrow")))
    return jax.shard_map(
        functools.partial(local, mesh.shape["wide"], mesh.shape["narrow"]),
        mesh=mesh,
        in_specs=placed,
        out_specs=(P(None, ("wide", "narrow")), P(None, ("wide", "narrow"))),
        check_vma=False,
    )
```

```python
import functools

import jax
import jax.numpy as jnp
import numpy as np
from jax import lax
from jax.experimental import pallas as pl
from jax.experimental.pallas import tpu as pltpu
from jax.sharding import PartitionSpec as P


NP = 8
BX = 2
BY = 4
EZ = 4
PTS = NP**3
PLANE = NP * NP
LANES = 128
HALF = PLANE // 2
XSTEP = BY * EZ

DIFFUSION = 0.05


def legendre_values(abscissa, num_points):
    columns = [np.ones(abscissa.shape), abscissa]
    for degree in range(2, num_points):
        columns.append(
            ((2 * degree - 1) * abscissa * columns[degree - 1] - (degree - 1) * columns[degree - 2])
            / degree
        )
    return np.stack(columns, 1)


def gll_tables(num_points):
    poly_order = num_points - 1
    abscissa = np.cos(np.pi * np.arange(num_points) / poly_order)
    for _ in range(60):
        legendre = legendre_values(abscissa, num_points)
        abscissa = abscissa - (abscissa * legendre[:, poly_order] - legendre[:, poly_order - 1]) / (
            num_points * legendre[:, poly_order]
        )
    legendre = legendre_values(abscissa, num_points)
    top_values = legendre[:, poly_order][::-1]
    abscissa = abscissa[::-1]
    weights = 2.0 / (poly_order * num_points * top_values**2)
    identity = np.eye(num_points)
    differ = np.where(identity > 0, 1.0, abscissa[:, None] - abscissa[None, :])
    deriv_table = np.where(identity > 0, 0.0, top_values[:, None] / (top_values[None, :] * differ))
    quarter = poly_order * num_points / 4.0
    edge_fix = np.concatenate([np.array([-quarter]), np.zeros(num_points - 2), np.array([quarter])])
    deriv_table = deriv_table + identity * edge_fix[:, None]
    return (weights, deriv_table)


def stiffness():
    weights, deriv = gll_tables(NP)
    stiff = DIFFUSION * deriv.T @ np.diag(weights) @ deriv
    return weights, 0.5 * (stiff + stiff.T)


WEIGHTS, STIFF = stiffness()
EVEN = 0.5 * (STIFF[:4, :4] + STIFF[:4, 7:3:-1])
ODD = 0.5 * (STIFF[:4, :4] - STIFF[:4, 7:3:-1])
EVEN = 0.5 * (EVEN + EVEN.T)
ODD = 0.5 * (ODD + ODD.T)


def apply_stiff(f):
    even = [f[j] + f[7 - j] for j in range(4)]
    odd = [f[j] - f[7 - j] for j in range(4)]
    flux = {(i, j): float(EVEN[i, j]) * (even[j] - even[i]) for i in range(4) for j in range(i + 1, 4)}
    e = [
        (flux[0, 1] + flux[0, 2]) + flux[0, 3],
        (flux[1, 2] + flux[1, 3]) - flux[0, 1],
        (flux[2, 3] - flux[0, 2]) - flux[1, 2],
        None,
    ]
    e[3] = -((flux[0, 3] + flux[1, 3]) + flux[2, 3])
    out = [None] * NP
    for i in range(4):
        o = sum_of([float(ODD[min(i, j), max(i, j)]) * odd[j] for j in range(4)])
        out[i] = e[i] + o
        out[7 - i] = e[i] - o
    return out


def sum_of(terms):
    while len(terms) > 1:
        terms = [
            terms[k] + terms[k + 1] if k + 1 < len(terms) else terms[k]
            for k in range(0, len(terms), 2)
        ]
    return terms[0]


class Grid:
    def __init__(self, lanes, wide):
        self.lanes = lanes
        self.wide = wide
        self.lane = lax.broadcasted_iota(jnp.int32, (NP, lanes), 1)
        self.row = lax.broadcasted_iota(jnp.int32, (NP, lanes), 0)
        self.s = self.lane & (EZ - 1)
        self.j = (self.lane // EZ) & (BY - 1)
        self.i = (self.lane // XSTEP) & (BX - 1)
        self.lower = self.i == 0
        w = jnp.full((NP, lanes), float(WEIGHTS[0]), jnp.float32)
        for c in range(1, NP):
            w = jnp.where(self.row == c, float(WEIGHTS[c]), w)
        self.w = w

    def has_neighbour(self):
        u = lax.axis_index("wide")
        low = jnp.where(u > 0, 1, 0)
        high = jnp.where(u < self.wide - 1, 1, 0)
        return jnp.where(self.lower, low, high) > 0

    def roll(self, x, shift):
        return pltpu.roll(x, shift % self.lanes, axis=x.ndim - 1)

    def share(self, lo, hi, axis):
        if axis == "x":
            new_lo = lo + jnp.where(self.lower, 0.0, self.roll(hi, XSTEP))
            new_hi = hi + jnp.where(self.lower, self.roll(lo, -XSTEP), 0.0)
        elif axis == "y":
            block = BX * XSTEP
            jump = block - (BY - 1) * EZ
            from_hi = jnp.where(self.j > 0, self.roll(hi, EZ), self.roll(hi, jump))
            from_lo = jnp.where(self.j < BY - 1, self.roll(lo, -EZ), self.roll(lo, -jump))
            first = (self.j == 0) & (self.lane < block)
            last = (self.j == BY - 1) & (self.lane >= self.lanes - block)
            new_lo = lo + jnp.where(first, 0.0, from_hi)
            new_hi = hi + jnp.where(last, 0.0, from_lo)
        else:
            new_lo = lo + jnp.where(self.s > 0, self.roll(hi, 1), 0.0)
            new_hi = hi + jnp.where(self.s < EZ - 1, self.roll(lo, -1), 0.0)
        return new_lo, new_hi

    def assemble(self, ref):
        for b in range(NP):
            lo, hi = rows(0, b), rows(NP - 1, b)
            ref[lo, :], ref[hi, :] = self.share(ref[lo, :], ref[hi, :], "x")
        for a in range(NP):
            lo, hi = rows(a, 0), rows(a, NP - 1)
            ref[lo, :], ref[hi, :] = self.share(ref[lo, :], ref[hi, :], "y")
        for a in range(NP):
            lo, hi = self.share(column(ref, PLANE * a), column(ref, PLANE * a + NP - 1), "z")
            put_column(ref, PLANE * a, lo)
            put_column(ref, PLANE * a + NP - 1, hi)

    def plane_product(self, f_ref, base, out_ref, wa=1.0):
        scale = wa * self.w
        z = apply_stiff([column(f_ref, base + c) for c in range(NP)])
        for c in range(NP):
            put_column(out_ref, c, scale * z[c])
        y = apply_stiff([f_ref[pl.ds(base + NP * b, NP), :] for b in range(NP)])
        return [scale * y[b] + out_ref[pl.ds(NP * b, NP), :] for b in range(NP)]

    def local(self, f_ref, massed_ref, out_ref, tmp_ref):
        for a in range(NP):
            flat = self.plane_product(f_ref, PLANE * a, tmp_ref, float(WEIGHTS[a]))
            for b in range(NP):
                r = rows(a, b)
                value = flat[b]
                if massed_ref is not None:
                    value = value + massed_ref[r, :] * f_ref[r, :]
                out_ref[r, :] = value
        for b in range(NP):
            x = apply_stiff([f_ref[rows(a, b), :] for a in range(NP)])
            wb = float(WEIGHTS[b]) * self.w
            for a in range(NP):
                r = rows(a, b)
                out_ref[r, :] = out_ref[r, :] + wb * x[a]

    def count_weights(self):
        nb = self.has_neighbour()
        one = jnp.ones((NP, self.lanes), jnp.float32)
        x0 = jnp.where(~self.lower | nb, 0.5, one)
        x7 = jnp.where(self.lower | nb, 0.5, one)
        block = BX * XSTEP
        first = (self.j == 0) & (self.lane < block)
        last = (self.j == BY - 1) & (self.lane >= self.lanes - block)
        y0 = jnp.where(first, one, 0.5)
        y7 = jnp.where(last, one, 0.5)
        z = jnp.where((self.row == 0) & (self.s > 0), 0.5, one)
        z = jnp.where((self.row == NP - 1) & (self.s < EZ - 1), 0.5, z)
        zx = [z * x0, z, z * x7]
        return [[m * y0, m, m * y7] for m in zx]


def place(a):
    return 0 if a == 0 else (2 if a == NP - 1 else 1)


def rows(a, b):
    return pl.ds(PLANE * a + NP * b, NP)


def column(ref, start):
    if ref.shape[1] == LANES:
        return ref[pl.ds(start, NP, stride=NP), :]
    return jnp.concatenate([ref[pl.ds(start + NP * b, 1), :] for b in range(NP)], axis=0)


def put_column(ref, start, value):
    if ref.shape[1] == LANES:
        ref[pl.ds(start, NP, stride=NP), :] = value
    else:
        for b in range(NP):
            ref[pl.ds(start + NP * b, 1), :] = value[b : b + 1, :]


def pack_face(grid, face, write):
    u = lax.axis_index("wide")
    even = (u % 2) == 0
    for b in range(NP // 2):
        top, bottom = face[b], face[b + NP // 2]
        up = jnp.where(grid.lower, grid.roll(bottom, -XSTEP), top)
        down = jnp.where(grid.lower, top, grid.roll(bottom, XSTEP))
        write(b, jnp.where(even, up, down), jnp.where(even, down, up))


def unpack_face(grid, read_a, read_b, nb):
    u = lax.axis_index("wide")
    even = (u % 2) == 0
    tops, bottoms = [], []
    for b in range(NP // 2):
        first, second = read_a(b), read_b(b)
        from_up = jnp.where(even, first, second)
        from_down = jnp.where(even, second, first)
        top = jnp.where(grid.lower, grid.roll(from_down, -XSTEP), grid.roll(from_up, XSTEP))
        bottom = jnp.where(grid.lower, from_down, from_up)
        tops.append(jnp.where(nb, top, 0.0))
        bottoms.append(jnp.where(nb, bottom, 0.0))
    return tops + bottoms


def pack_kernel(source_ref, reaction_ref, place_ref, early_ref, late_ref, near_ref, sems):
    per = source_ref.shape[0]
    blocks = PTS // LANES
    places = pltpu.make_async_copy(place_ref, near_ref, sems.at[2 * blocks])
    places.start()
    copies = []
    for ref, out_ref in ((reaction_ref, late_ref), (source_ref, early_ref)):
        for q in range(blocks):
            copy = pltpu.make_async_copy(
                ref.at[:, pl.ds(q * LANES, LANES)],
                out_ref.at[pl.ds(per * q, per), :],
                sems.at[len(copies)],
            )
            copy.start()
            copies.append(copy)
    places.wait()
    near = jnp.concatenate([near_ref[...].astype(jnp.float32)] * (LANES // per), axis=1)
    early_ref[per * (blocks + 1) :, :] = jnp.broadcast_to(near, (NP, LANES))
    for copy in copies:
        copy.wait()
    low = lax.broadcasted_iota(jnp.int32, (per, LANES), 1) < PLANE
    early_ref[per * blocks : per * (blocks + 1), :] = jnp.where(
        low, late_ref[:per, :], late_ref[per * (blocks - 1) :, :]
    )


def came_from(per, refs):
    lanes = per * len(refs)
    tiles, groups = lanes // LANES, LANES // per
    at = pl.ds(per * (PTS // LANES + 1), NP)
    group = lax.broadcasted_iota(jnp.int32, (NP, LANES), 1) // per
    spot = lax.broadcasted_iota(jnp.int32, (LANES, lanes), 1).astype(jnp.float32)
    row = lax.broadcasted_iota(jnp.int32, (LANES, lanes), 0)
    came = jnp.zeros((1, lanes), jnp.float32)
    for t in range(tiles):
        new = refs[groups * t][at, :]
        for g in range(1, groups):
            new = jnp.where(group == g, refs[groups * t + g][at, :], new)
        new = jnp.transpose(jnp.concatenate([new] * (LANES // NP), axis=0))
        new = jnp.concatenate([new] * tiles, axis=1)
        old = (row + t * LANES).astype(jnp.float32)
        came = came + jnp.sum(jnp.where(new == spot, old, 0.0), axis=0, keepdims=True)
    return jnp.broadcast_to(came.astype(jnp.int32), (NP, lanes))


def turned(per, refs, start, came):
    tiles, groups = per * len(refs) // LANES, LANES // per
    old = [
        jnp.transpose(
            jnp.concatenate([refs[groups * t + g][pl.ds(start, per), :] for g in range(groups)], axis=0)
        )
        for t in range(tiles)
    ]
    for r in range(LANES // NP):
        for t in range(tiles):
            cols = slice(t * LANES, (t + 1) * LANES)
            home, lane = came[:, cols] // LANES, came[:, cols] % LANES
            value = None
            for h in range(tiles):
                pick = jnp.take_along_axis(old[h][NP * r : NP * (r + 1), :], lane, axis=1)
                value = pick if value is None else jnp.where(home == h, pick, value)
            yield r, cols, value


def first_kernel(per, narrow, wide, *refs):
    got, (rhs_ref, came_ref, msg_a_ref, msg_b_ref, ends_ref) = refs[:narrow], refs[narrow:]
    grid = Grid(per * narrow, wide)
    blocks = PTS // LANES
    came = came_from(per, got)
    came_ref[...] = came
    for q in range(blocks):
        for r, cols, value in turned(per, got, per * q, came):
            at = q * LANES + NP * r
            a, b = at // PLANE, (at % PLANE) // NP
            mass = float(WEIGHTS[a]) * float(WEIGHTS[b])
            rhs_ref[pl.ds(at, NP), cols] = value * (mass * grid.w[:, cols])
    for r, cols, value in turned(per, got, per * blocks, came):
        ends_ref[pl.ds(NP * r, NP), cols] = value
    grid.assemble(rhs_ref)

    def write(part):
        def put(b, first, second):
            msg_a_ref[pl.ds(part * HALF + NP * b, NP), :] = first
            msg_b_ref[pl.ds(part * HALF + NP * b, NP), :] = second

        return put

    last = NP - 1
    pack_face(
        grid,
        [jnp.where(grid.lower, rhs_ref[rows(0, b), :], rhs_ref[rows(last, b), :]) for b in range(NP)],
        write(0),
    )
    part = []
    for b in range(NP):
        f = [rhs_ref[rows(a, b), :] for a in range(NP)]
        low = sum_of([float(STIFF[0, a]) * f[a] for a in range(1, NP)])
        high = sum_of([float(STIFF[last, a]) * f[a] for a in range(last)])
        part.append((float(WEIGHTS[b]) * grid.w) * jnp.where(grid.lower, low, high))
    pack_face(grid, part, write(1))
    pack_face(
        grid,
        [
            jnp.where(
                grid.lower, ends_ref[pl.ds(NP * b, NP), :], ends_ref[pl.ds(PLANE + NP * b, NP), :]
            )
            for b in range(NP)
        ],
        write(2),
    )


def reaction_kernel(per, narrow, wide, *refs):
    got, (came_ref, massed_ref) = refs[:narrow], refs[narrow:]
    grid = Grid(per * narrow, wide)
    came = came_ref[...]
    for q in range(PTS // LANES):
        for r, cols, value in turned(per, got, per * q, came):
            at = q * LANES + NP * r
            a, b = at // PLANE, (at % PLANE) // NP
            mass = float(WEIGHTS[a]) * float(WEIGHTS[b])
            massed_ref[pl.ds(at, NP), cols] = value * (mass * grid.w[:, cols])


def middle_kernel(wide, rhs_ref, part_ref, flat_ref, tmp_ref):
    grid = Grid(rhs_ref.shape[1], wide)
    grid.local(rhs_ref, None, part_ref, tmp_ref)
    for b in range(NP):
        low, high = rhs_ref[rows(0, b), :], rhs_ref[rows(NP - 1, b), :]
        flat_ref[pl.ds(NP * b, NP), :] = jnp.where(grid.lower, low, high)
    flat = grid.plane_product(flat_ref, 0, tmp_ref)
    for b in range(NP):
        flat_ref[pl.ds(NP * b, NP), :] = flat[b]


def second_kernel(
    wide,
    rhs_ref,
    massed_ref,
    part_ref,
    flat0_ref,
    got_a_ref,
    got_b_ref,
    v0_ref,
    v1_ref,
    v2_ref,
    msg_a_ref,
    msg_b_ref,
    face_ref,
    tmp_ref,
):
    lanes = rhs_ref.shape[1]
    grid = Grid(lanes, wide)
    nb = grid.has_neighbour()
    last = NP - 1

    def reader(part):
        def first(b):
            return got_a_ref[pl.ds(part * HALF + NP * b, NP), :]

        def second(b):
            return got_b_ref[pl.ds(part * HALF + NP * b, NP), :]

        return first, second

    extra = unpack_face(grid, *reader(0), nb)
    slopes = unpack_face(grid, *reader(1), nb)
    reactions = unpack_face(grid, *reader(2), nb)
    for b in range(NP):
        face_ref[pl.ds(NP * b, NP), :] = extra[b]
    flat = grid.plane_product(face_ref, 0, tmp_ref)
    pull = [jnp.where(grid.lower, float(STIFF[a, 0]), float(STIFF[a, last])) for a in range(NP)]
    w0 = float(WEIGHTS[0])
    for b in range(NP):
        wb = float(WEIGHTS[b]) * grid.w
        more = wb * extra[b]
        for a in range(1, last):
            r = rows(a, b)
            value = rhs_ref[r, :]
            v0_ref[r, :] = value
            v1_ref[r, :] = part_ref[r, :] + pull[a] * more + massed_ref[r, :] * value
        r_low, r_high = rows(0, b), rows(last, b)
        low = rhs_ref[r_low, :] + jnp.where(grid.lower, extra[b], 0.0)
        high = rhs_ref[r_high, :] + jnp.where(grid.lower, 0.0, extra[b])
        v0_ref[r_low, :] = low
        v0_ref[r_high, :] = high
        face = jnp.where(grid.lower, low, high)
        theirs = slopes[b] + w0 * (flat0_ref[pl.ds(NP * b, NP), :] + flat[b])
        theirs = theirs + wb * ((float(STIFF[0, 0]) + w0 * reactions[b]) * face)
        end = w0 * flat[b] + jnp.where(nb, theirs, 0.0)
        v1_low = part_ref[r_low, :] + pull[0] * more + massed_ref[r_low, :] * low
        v1_high = part_ref[r_high, :] + pull[last] * more + massed_ref[r_high, :] * high
        v1_ref[r_low, :] = v1_low + jnp.where(grid.lower, end, 0.0)
        v1_ref[r_high, :] = v1_high + jnp.where(grid.lower, 0.0, end)
    grid.assemble(v1_ref)
    grid.local(v1_ref, massed_ref, v2_ref, tmp_ref)
    weight = grid.count_weights()
    parts = [[], [], [], []]
    kinds = {}
    for a in range(NP):
        for b in range(NP):
            kinds.setdefault((place(a), place(b)), []).append(rows(a, b))
    for (i, j), where_in in kinds.items():
        terms = [[], [], [], []]
        for r in where_in:
            v0, v1, v2 = v0_ref[r, :], v1_ref[r, :], v2_ref[r, :]
            for t, value in zip(terms, (v0 * v0, v1 * v0, v1 * v1, v1 * v2)):
                t.append(value)
        for k, t in enumerate(terms):
            total = sum_of(t)
            parts[k].append(total if k == 3 else weight[i][j] * total)
    row = grid.row
    out = jnp.zeros((NP, lanes), jnp.float32)
    for k, p in enumerate(parts):
        total = jnp.sum(sum_of(p), axis=0, keepdims=True)
        out = jnp.where(row == k, jnp.broadcast_to(total, (NP, lanes)), out)
    msg_a_ref[HALF : HALF + NP, :] = out
    msg_b_ref[HALF : HALF + NP, :] = out
    grid.assemble(v2_ref)

    def write(b, first, second):
        msg_a_ref[pl.ds(NP * b, NP), :] = first
        msg_b_ref[pl.ds(NP * b, NP), :] = second

    pack_face(
        grid,
        [jnp.where(grid.lower, v2_ref[rows(0, b), :], v2_ref[rows(last, b), :]) for b in range(NP)],
        write,
    )


def own_kernel(per, wide, *refs):
    *in_refs, scratch_ref = refs
    vector_refs, out_refs = in_refs[:3], in_refs[3:]
    lanes = vector_refs[0].shape[1]
    grid = Grid(lanes, wide)
    mine = pl.ds(pl.multiple_of(lax.axis_index("narrow") * per, per), per)
    weight = grid.count_weights()
    inverse = 1.0 / grid.w
    weight = [[w * inverse for w in line] for line in weight]
    for q in range(PTS // LANES):
        lines = []
        for r in range(LANES // NP):
            at = q * LANES + NP * r
            a, b = at // PLANE, (at % PLANE) // NP
            lines.append(float(1.0 / (WEIGHTS[a] * WEIGHTS[b])) * weight[place(a)][place(b)])
        scale = jnp.concatenate(lines, axis=0)
        fields = [ref[q * LANES : (q + 1) * LANES, :] for ref in vector_refs] + [scale]
        for k, (field, ref) in enumerate(zip(fields, out_refs)):
            for t in range(lanes // LANES):
                scratch_ref[k, t * LANES : (t + 1) * LANES, :] = jnp.transpose(
                    field[:, t * LANES : (t + 1) * LANES]
                )
            ref[:, q * LANES : (q + 1) * LANES] = scratch_ref[k, mine, :]


def last_kernel(
    wide,
    v0_ref,
    v1_ref,
    v2_ref,
    scale_ref,
    got_a_ref,
    got_b_ref,
    twin_b_ref,
    sums_ref,
    solution_ref,
    strong_ref,
    face_ref,
    turned_ref,
):
    per = v0_ref.shape[0]
    lanes = got_a_ref.shape[1]
    grid = Grid(lanes, wide)
    nb = grid.has_neighbour()
    v = lax.axis_index("narrow")
    core = v % 2
    extra = unpack_face(
        grid,
        lambda b: got_a_ref[pl.ds(NP * b, NP), :],
        lambda b: jnp.where(
            core == 0, twin_b_ref[pl.ds(NP * b, NP), :], got_b_ref[pl.ds(NP * b, NP), :]
        ),
        nb,
    )
    for b in range(NP):
        face_ref[pl.ds(NP * b, NP), :] = extra[b]
        face_ref[pl.ds(PLANE + NP * b, NP), :] = extra[b]
    for t in range(lanes // LANES):
        turned_ref[t * LANES : (t + 1) * LANES, :] = jnp.transpose(
            face_ref[:, t * LANES : (t + 1) * LANES]
        )
    face = turned_ref[pl.ds(pl.multiple_of(v * per, per), per), :]
    spot = lax.broadcasted_iota(jnp.int32, (per, LANES), 1)
    layer = lax.broadcasted_iota(jnp.int32, (per, LANES), 0) // XSTEP
    ends = {
        0: jnp.where((spot < PLANE) & (layer == 0), face, 0.0),
        PTS // LANES - 1: jnp.where((spot >= PLANE) & (layer == BX - 1), face, 0.0),
    }
    g = [jnp.sum(sums_ref[k : k + 1, :], axis=1, keepdims=True) for k in range(4)]
    alpha = g[0] / g[1]
    norm = g[0] - 2.0 * alpha * g[1] + (alpha * alpha) * g[2]
    beta = norm / g[0]
    one = 1.0 + beta
    curve = one * one * g[1] - 2.0 * one * alpha * g[2] + (alpha * alpha) * g[3]
    step = norm / curve
    first = jnp.broadcast_to(alpha + step * one, (per, LANES))
    second = jnp.broadcast_to(alpha * step, (per, LANES))
    for q in range(PTS // LANES):
        at = (slice(None), slice(q * LANES, (q + 1) * LANES))
        v0, v1, v2 = v0_ref[at], v1_ref[at], v2_ref[at]
        if q in ends:
            v2 = v2 + ends[q]
        solution_ref[at] = first * v0 - second * v1
        strong_ref[at] = (v0 - first * v1 + second * v2) * scale_ref[at]


VM = pl.BlockSpec(memory_space=pltpu.VMEM)


def call(kernel, out_shapes, in_specs, scratch=()):
    return pl.pallas_call(
        kernel,
        out_shape=[
            jax.ShapeDtypeStruct(*(s if isinstance(s[0], tuple) else (s, jnp.float32)))
            for s in out_shapes
        ],
        in_specs=in_specs,
        out_specs=[VM] * len(out_shapes),
        scratch_shapes=list(scratch),
        compiler_params=pltpu.CompilerParams(vmem_limit_bytes=16 * 1024 * 1024),
    )


def in_hbm(*arrays):
    return [pltpu.with_memory_space_constraint(x, pltpu.HBM) for x in arrays]


def swap(x, wide, narrow, *partner_of):
    pairs = []
    for u in range(wide):
        to = [partner(u) for partner in partner_of]
        idle = [not 0 <= t < wide for t in to]
        for v in range(narrow):
            k = v % len(to)
            away = v ^ 1 if all(idle) else v ^ 2
            target = u * narrow + away if idle[k] else to[k] * narrow + v
            pairs.append((u * narrow + v, target))
    return lax.ppermute(x, ("wide", "narrow"), pairs)


def same_pair(u):
    return u ^ 1


def next_pair(u):
    return u + 1 if u % 2 else u - 1


def far_copy(x, narrow):
    if narrow != 4:
        return list(lax.all_gather(x, "narrow"))
    return [x, lax.ppermute(x, "narrow", [(v, v ^ 2) for v in range(narrow)])]


def near_copies(blocks, narrow):
    if narrow != 4:
        return blocks
    return blocks + [twin(x, narrow) for x in blocks]


def twin(x, narrow):
    return lax.ppermute(x, "narrow", [(v, v ^ 1) for v in range(narrow)])


def finish(msg_a, msg_b, wide, narrow):
    sums = msg_a[HALF:]
    if wide == 8:
        got_b = swap(msg_b, wide, narrow, lambda u: u ^ 4, next_pair)
        more = swap(sums, wide, narrow, lambda u: u ^ 2, lambda u: u ^ 6)
        twin_b = twin(got_b[:HALF], narrow)
        even = lax.axis_index("narrow") % 2 == 0
        part = more + jnp.where(even, sums + got_b[HALF:], 0.0)
        got_a = swap(jnp.concatenate([msg_a[:HALF], part], axis=0), wide, narrow, same_pair)
        cross = [
            (u * narrow + v, (u ^ 1) * narrow + (v ^ 1)) for u in range(wide) for v in range(narrow)
        ]
        theirs = got_a[HALF:] + lax.ppermute(part, ("wide", "narrow"), cross)
        total = (part + twin(part, narrow)) + theirs
        return got_a[:HALF], got_b[:HALF], twin_b, total
    got_a = swap(msg_a, wide, narrow, same_pair)
    got_b = swap(msg_b, wide, narrow, next_pair)[:HALF]
    return got_a[:HALF], got_b, got_b, lax.psum(sums, "wide")


def local(wide, narrow, source_old, reaction_old, new_place):
    per = source_old.shape[1]
    lanes = per * narrow
    blocks = PTS // LANES
    early, late = call(
        pack_kernel,
        [(per * (blocks + 1) + NP, LANES), (per * blocks, LANES)],
        [pl.BlockSpec(memory_space=pltpu.HBM)] * 3,
        [pltpu.VMEM((1, per), jnp.int32), pltpu.SemaphoreType.DMA((2 * blocks + 1,))],
    )(*in_hbm(source_old.T, reaction_old.T, new_place.reshape(1, per)))
    full = (PTS, lanes)
    late = far_copy(late, narrow)
    early = near_copies(far_copy(early, narrow), narrow)
    rhs, came, msg_a, msg_b = call(
        functools.partial(first_kernel, per, narrow, wide),
        [full, ((NP, lanes), jnp.int32), (3 * HALF, lanes), (3 * HALF, lanes)],
        [VM] * narrow,
        [pltpu.VMEM((2 * PLANE, lanes), jnp.float32)],
    )(*early)
    got_a = swap(msg_a, wide, narrow, same_pair)
    got_b = swap(msg_b, wide, narrow, next_pair)
    part, flat = call(
        functools.partial(middle_kernel, wide),
        [full, (PLANE, lanes)],
        [VM],
        [pltpu.VMEM((PLANE, lanes), jnp.float32)],
    )(rhs)
    late, came = lax.optimization_barrier((late, came))
    late = near_copies(late, narrow)
    massed = call(
        functools.partial(reaction_kernel, per, narrow, wide), [full], [VM] * (narrow + 1)
    )(*late, came)[0]
    v0, v1, v2, msg_a, msg_b = call(
        functools.partial(second_kernel, wide),
        [full, full, full, (HALF + NP, lanes), (HALF + NP, lanes)],
        [VM] * 6,
        [pltpu.VMEM((PLANE, lanes), jnp.float32), pltpu.VMEM((PLANE, lanes), jnp.float32)],
    )(rhs, massed, part, flat, got_a, got_b)
    arrived = finish(msg_a, msg_b, wide, narrow)
    own = call(
        functools.partial(own_kernel, per, wide),
        [(per, PTS)] * 4,
        [VM] * 3,
        [pltpu.VMEM((4, lanes, LANES), jnp.float32)],
    )(v0, v1, v2)
    out = call(
        functools.partial(last_kernel, wide),
        [(per, PTS), (per, PTS)],
        [VM] * 8,
        [pltpu.VMEM((LANES, lanes), jnp.float32), pltpu.VMEM((lanes, LANES), jnp.float32)],
    )(*own, *arrived)
    return tuple(x.T for x in out)


def solution(mesh):
    placed = (P(None, ("wide", "narrow")), P(None, ("wide", "narrow")), P(("wide", "narrow")))
    return jax.shard_map(
        functools.partial(local, mesh.shape["wide"], mesh.shape["narrow"]),
        mesh=mesh,
        in_specs=placed,
        out_specs=(P(None, ("wide", "narrow")), P(None, ("wide", "narrow"))),
        check_vma=False,
    )
```

```python
import functools

import jax
import jax.numpy as jnp
import numpy as np
from jax import lax
from jax.experimental import pallas as pl
from jax.experimental.pallas import tpu as pltpu
from jax.sharding import PartitionSpec as P


NP = 8
BX = 2
BY = 4
EZ = 4
PTS = NP**3
PLANE = NP * NP
LANES = 128
HALF = PLANE // 2
XSTEP = BY * EZ

DIFFUSION = 0.05


def legendre_values(abscissa, num_points):
    columns = [np.ones(abscissa.shape), abscissa]
    for degree in range(2, num_points):
        columns.append(
            ((2 * degree - 1) * abscissa * columns[degree - 1] - (degree - 1) * columns[degree - 2])
            / degree
        )
    return np.stack(columns, 1)


def gll_tables(num_points):
    poly_order = num_points - 1
    abscissa = np.cos(np.pi * np.arange(num_points) / poly_order)
    for _ in range(60):
        legendre = legendre_values(abscissa, num_points)
        abscissa = abscissa - (abscissa * legendre[:, poly_order] - legendre[:, poly_order - 1]) / (
            num_points * legendre[:, poly_order]
        )
    legendre = legendre_values(abscissa, num_points)
    top_values = legendre[:, poly_order][::-1]
    abscissa = abscissa[::-1]
    weights = 2.0 / (poly_order * num_points * top_values**2)
    identity = np.eye(num_points)
    differ = np.where(identity > 0, 1.0, abscissa[:, None] - abscissa[None, :])
    deriv_table = np.where(identity > 0, 0.0, top_values[:, None] / (top_values[None, :] * differ))
    quarter = poly_order * num_points / 4.0
    edge_fix = np.concatenate([np.array([-quarter]), np.zeros(num_points - 2), np.array([quarter])])
    deriv_table = deriv_table + identity * edge_fix[:, None]
    return (weights, deriv_table)


def stiffness():
    weights, deriv = gll_tables(NP)
    stiff = DIFFUSION * deriv.T @ np.diag(weights) @ deriv
    return weights, 0.5 * (stiff + stiff.T)


WEIGHTS, STIFF = stiffness()
EVEN = 0.5 * (STIFF[:4, :4] + STIFF[:4, 7:3:-1])
ODD = 0.5 * (STIFF[:4, :4] - STIFF[:4, 7:3:-1])
EVEN = 0.5 * (EVEN + EVEN.T)
ODD = 0.5 * (ODD + ODD.T)


def apply_stiff(f):
    even = [f[j] + f[7 - j] for j in range(4)]
    odd = [f[j] - f[7 - j] for j in range(4)]
    flux = {(i, j): float(EVEN[i, j]) * (even[j] - even[i]) for i in range(4) for j in range(i + 1, 4)}
    e = [
        (flux[0, 1] + flux[0, 2]) + flux[0, 3],
        (flux[1, 2] + flux[1, 3]) - flux[0, 1],
        (flux[2, 3] - flux[0, 2]) - flux[1, 2],
        None,
    ]
    e[3] = -((flux[0, 3] + flux[1, 3]) + flux[2, 3])
    out = [None] * NP
    for i in range(4):
        o = sum_of([float(ODD[min(i, j), max(i, j)]) * odd[j] for j in range(4)])
        out[i] = e[i] + o
        out[7 - i] = e[i] - o
    return out


def sum_of(terms):
    while len(terms) > 1:
        terms = [
            terms[k] + terms[k + 1] if k + 1 < len(terms) else terms[k]
            for k in range(0, len(terms), 2)
        ]
    return terms[0]


class Grid:
    def __init__(self, lanes, wide):
        self.lanes = lanes
        self.wide = wide
        self.lane = lax.broadcasted_iota(jnp.int32, (NP, lanes), 1)
        self.row = lax.broadcasted_iota(jnp.int32, (NP, lanes), 0)
        self.s = self.lane & (EZ - 1)
        self.j = (self.lane // EZ) & (BY - 1)
        self.i = (self.lane // XSTEP) & (BX - 1)
        self.lower = self.i == 0
        w = jnp.full((NP, lanes), float(WEIGHTS[0]), jnp.float32)
        for c in range(1, NP):
            w = jnp.where(self.row == c, float(WEIGHTS[c]), w)
        self.w = w

    def has_neighbour(self):
        u = lax.axis_index("wide")
        low = jnp.where(u > 0, 1, 0)
        high = jnp.where(u < self.wide - 1, 1, 0)
        return jnp.where(self.lower, low, high) > 0

    def roll(self, x, shift):
        return pltpu.roll(x, shift % self.lanes, axis=x.ndim - 1)

    def share(self, lo, hi, axis):
        if axis == "x":
            new_lo = lo + jnp.where(self.lower, 0.0, self.roll(hi, XSTEP))
            new_hi = hi + jnp.where(self.lower, self.roll(lo, -XSTEP), 0.0)
        elif axis == "y":
            block = BX * XSTEP
            jump = block - (BY - 1) * EZ
            from_hi = jnp.where(self.j > 0, self.roll(hi, EZ), self.roll(hi, jump))
            from_lo = jnp.where(self.j < BY - 1, self.roll(lo, -EZ), self.roll(lo, -jump))
            first = (self.j == 0) & (self.lane < block)
            last = (self.j == BY - 1) & (self.lane >= self.lanes - block)
            new_lo = lo + jnp.where(first, 0.0, from_hi)
            new_hi = hi + jnp.where(last, 0.0, from_lo)
        else:
            new_lo = lo + jnp.where(self.s > 0, self.roll(hi, 1), 0.0)
            new_hi = hi + jnp.where(self.s < EZ - 1, self.roll(lo, -1), 0.0)
        return new_lo, new_hi

    def assemble(self, ref):
        for b in range(NP):
            lo, hi = rows(0, b), rows(NP - 1, b)
            ref[lo, :], ref[hi, :] = self.share(ref[lo, :], ref[hi, :], "x")
        for a in range(NP):
            lo, hi = rows(a, 0), rows(a, NP - 1)
            ref[lo, :], ref[hi, :] = self.share(ref[lo, :], ref[hi, :], "y")
        for a in range(NP):
            lo, hi = self.share(column(ref, PLANE * a), column(ref, PLANE * a + NP - 1), "z")
            put_column(ref, PLANE * a, lo)
            put_column(ref, PLANE * a + NP - 1, hi)

    def plane_product(self, f_ref, base, out_ref, wa=1.0):
        scale = wa * self.w
        z = apply_stiff([column(f_ref, base + c) for c in range(NP)])
        for c in range(NP):
            put_column(out_ref, c, scale * z[c])
        y = apply_stiff([f_ref[pl.ds(base + NP * b, NP), :] for b in range(NP)])
        return [scale * y[b] + out_ref[pl.ds(NP * b, NP), :] for b in range(NP)]

    def local(self, f_ref, massed_ref, out_ref, tmp_ref):
        for a in range(NP):
            flat = self.plane_product(f_ref, PLANE * a, tmp_ref, float(WEIGHTS[a]))
            for b in range(NP):
                r = rows(a, b)
                value = flat[b]
                if massed_ref is not None:
                    value = value + massed_ref[r, :] * f_ref[r, :]
                out_ref[r, :] = value
        for b in range(NP):
            x = apply_stiff([f_ref[rows(a, b), :] for a in range(NP)])
            wb = float(WEIGHTS[b]) * self.w
            for a in range(NP):
                r = rows(a, b)
                out_ref[r, :] = out_ref[r, :] + wb * x[a]

    def count_weights(self):
        nb = self.has_neighbour()
        one = jnp.ones((NP, self.lanes), jnp.float32)
        x0 = jnp.where(~self.lower | nb, 0.5, one)
        x7 = jnp.where(self.lower | nb, 0.5, one)
        block = BX * XSTEP
        first = (self.j == 0) & (self.lane < block)
        last = (self.j == BY - 1) & (self.lane >= self.lanes - block)
        y0 = jnp.where(first, one, 0.5)
        y7 = jnp.where(last, one, 0.5)
        z = jnp.where((self.row == 0) & (self.s > 0), 0.5, one)
        z = jnp.where((self.row == NP - 1) & (self.s < EZ - 1), 0.5, z)
        zx = [z * x0, z, z * x7]
        return [[m * y0, m, m * y7] for m in zx]


def place(a):
    return 0 if a == 0 else (2 if a == NP - 1 else 1)


def rows(a, b):
    return pl.ds(PLANE * a + NP * b, NP)


def column(ref, start):
    if ref.shape[1] == LANES:
        return ref[pl.ds(start, NP, stride=NP), :]
    return jnp.concatenate([ref[pl.ds(start + NP * b, 1), :] for b in range(NP)], axis=0)


def put_column(ref, start, value):
    if ref.shape[1] == LANES:
        ref[pl.ds(start, NP, stride=NP), :] = value
    else:
        for b in range(NP):
            ref[pl.ds(start + NP * b, 1), :] = value[b : b + 1, :]


def pack_face(grid, face, write):
    u = lax.axis_index("wide")
    even = (u % 2) == 0
    for b in range(NP // 2):
        top, bottom = face[b], face[b + NP // 2]
        up = jnp.where(grid.lower, grid.roll(bottom, -XSTEP), top)
        down = jnp.where(grid.lower, top, grid.roll(bottom, XSTEP))
        write(b, jnp.where(even, up, down), jnp.where(even, down, up))


def unpack_face(grid, read_a, read_b, nb):
    u = lax.axis_index("wide")
    even = (u % 2) == 0
    tops, bottoms = [], []
    for b in range(NP // 2):
        first, second = read_a(b), read_b(b)
        from_up = jnp.where(even, first, second)
        from_down = jnp.where(even, second, first)
        top = jnp.where(grid.lower, grid.roll(from_down, -XSTEP), grid.roll(from_up, XSTEP))
        bottom = jnp.where(grid.lower, from_down, from_up)
        tops.append(jnp.where(nb, top, 0.0))
        bottoms.append(jnp.where(nb, bottom, 0.0))
    return tops + bottoms


def pack_kernel(source_ref, reaction_ref, place_ref, early_ref, late_ref, near_ref, sems):
    per = source_ref.shape[0]
    blocks = PTS // LANES
    places = pltpu.make_async_copy(place_ref, near_ref, sems.at[2 * blocks])
    places.start()
    copies = []
    for ref, out_ref in ((reaction_ref, late_ref), (source_ref, early_ref)):
        for q in range(blocks):
            copy = pltpu.make_async_copy(
                ref.at[:, pl.ds(q * LANES, LANES)],
                out_ref.at[pl.ds(per * q, per), :],
                sems.at[len(copies)],
            )
            copy.start()
            copies.append(copy)
    places.wait()
    near = jnp.concatenate([near_ref[...].astype(jnp.float32)] * (LANES // per), axis=1)
    early_ref[per * (blocks + 1) :, :] = jnp.broadcast_to(near, (NP, LANES))
    for copy in copies:
        copy.wait()
    low = lax.broadcasted_iota(jnp.int32, (per, LANES), 1) < PLANE
    early_ref[per * blocks : per * (blocks + 1), :] = jnp.where(
        low, late_ref[:per, :], late_ref[per * (blocks - 1) :, :]
    )


def came_from(per, refs):
    lanes = per * len(refs)
    tiles, groups = lanes // LANES, LANES // per
    at = pl.ds(per * (PTS // LANES + 1), NP)
    group = lax.broadcasted_iota(jnp.int32, (NP, LANES), 1) // per
    spot = lax.broadcasted_iota(jnp.int32, (LANES, lanes), 1).astype(jnp.float32)
    row = lax.broadcasted_iota(jnp.int32, (LANES, lanes), 0)
    came = jnp.zeros((1, lanes), jnp.float32)
    for t in range(tiles):
        new = refs[groups * t][at, :]
        for g in range(1, groups):
            new = jnp.where(group == g, refs[groups * t + g][at, :], new)
        new = jnp.transpose(jnp.concatenate([new] * (LANES // NP), axis=0))
        new = jnp.concatenate([new] * tiles, axis=1)
        old = (row + t * LANES).astype(jnp.float32)
        came = came + jnp.sum(jnp.where(new == spot, old, 0.0), axis=0, keepdims=True)
    return jnp.broadcast_to(came.astype(jnp.int32), (NP, lanes))


def turned(per, refs, start, came):
    tiles, groups = per * len(refs) // LANES, LANES // per
    old = [
        jnp.transpose(
            jnp.concatenate([refs[groups * t + g][pl.ds(start, per), :] for g in range(groups)], axis=0)
        )
        for t in range(tiles)
    ]
    for r in range(LANES // NP):
        for t in range(tiles):
            cols = slice(t * LANES, (t + 1) * LANES)
            home, lane = came[:, cols] // LANES, came[:, cols] % LANES
            value = None
            for h in range(tiles):
                pick = jnp.take_along_axis(old[h][NP * r : NP * (r + 1), :], lane, axis=1)
                value = pick if value is None else jnp.where(home == h, pick, value)
            yield r, cols, value


def first_kernel(per, narrow, wide, *refs):
    got, (rhs_ref, came_ref, msg_ref, ends_ref) = refs[:narrow], refs[narrow:]
    grid = Grid(per * narrow, wide)
    blocks = PTS // LANES
    came = came_from(per, got)
    came_ref[...] = came
    for q in range(blocks):
        for r, cols, value in turned(per, got, per * q, came):
            at = q * LANES + NP * r
            a, b = at // PLANE, (at % PLANE) // NP
            mass = float(WEIGHTS[a]) * float(WEIGHTS[b])
            rhs_ref[pl.ds(at, NP), cols] = value * (mass * grid.w[:, cols])
    for r, cols, value in turned(per, got, per * blocks, came):
        ends_ref[pl.ds(NP * r, NP), cols] = value
    grid.assemble(rhs_ref)

    even = lax.axis_index("narrow") % 2 == 0

    def write(part):
        def put(b, first, second):
            msg_ref[pl.ds(part * HALF + NP * b, NP), :] = jnp.where(even, first, second)

        return put

    last = NP - 1
    pack_face(
        grid,
        [jnp.where(grid.lower, rhs_ref[rows(0, b), :], rhs_ref[rows(last, b), :]) for b in range(NP)],
        write(0),
    )
    part = []
    for b in range(NP):
        f = [rhs_ref[rows(a, b), :] for a in range(NP)]
        low = sum_of([float(STIFF[0, a]) * f[a] for a in range(1, NP)])
        high = sum_of([float(STIFF[last, a]) * f[a] for a in range(last)])
        part.append((float(WEIGHTS[b]) * grid.w) * jnp.where(grid.lower, low, high))
    pack_face(grid, part, write(1))
    pack_face(
        grid,
        [
            jnp.where(
                grid.lower, ends_ref[pl.ds(NP * b, NP), :], ends_ref[pl.ds(PLANE + NP * b, NP), :]
            )
            for b in range(NP)
        ],
        write(2),
    )


def reaction_kernel(per, narrow, wide, *refs):
    got, (came_ref, massed_ref) = refs[:narrow], refs[narrow:]
    grid = Grid(per * narrow, wide)
    came = came_ref[...]
    for q in range(PTS // LANES):
        for r, cols, value in turned(per, got, per * q, came):
            at = q * LANES + NP * r
            a, b = at // PLANE, (at % PLANE) // NP
            mass = float(WEIGHTS[a]) * float(WEIGHTS[b])
            massed_ref[pl.ds(at, NP), cols] = value * (mass * grid.w[:, cols])


def middle_kernel(wide, rhs_ref, part_ref, flat_ref, tmp_ref):
    grid = Grid(rhs_ref.shape[1], wide)
    grid.local(rhs_ref, None, part_ref, tmp_ref)
    for b in range(NP):
        low, high = rhs_ref[rows(0, b), :], rhs_ref[rows(NP - 1, b), :]
        flat_ref[pl.ds(NP * b, NP), :] = jnp.where(grid.lower, low, high)
    flat = grid.plane_product(flat_ref, 0, tmp_ref)
    for b in range(NP):
        flat_ref[pl.ds(NP * b, NP), :] = flat[b]


def second_kernel(
    wide,
    rhs_ref,
    massed_ref,
    part_ref,
    flat0_ref,
    mine_ref,
    other_ref,
    v0_ref,
    v1_ref,
    v2_ref,
    msg_a_ref,
    msg_b_ref,
    face_ref,
    tmp_ref,
):
    lanes = rhs_ref.shape[1]
    grid = Grid(lanes, wide)
    nb = grid.has_neighbour()
    last = NP - 1

    even = lax.axis_index("narrow") % 2 == 0

    def reader(part):
        def first(b):
            r = pl.ds(part * HALF + NP * b, NP)
            return jnp.where(even, mine_ref[r, :], other_ref[r, :])

        def second(b):
            r = pl.ds(part * HALF + NP * b, NP)
            return jnp.where(even, other_ref[r, :], mine_ref[r, :])

        return first, second

    extra = unpack_face(grid, *reader(0), nb)
    slopes = unpack_face(grid, *reader(1), nb)
    reactions = unpack_face(grid, *reader(2), nb)
    for b in range(NP):
        face_ref[pl.ds(NP * b, NP), :] = extra[b]
    flat = grid.plane_product(face_ref, 0, tmp_ref)
    pull = [jnp.where(grid.lower, float(STIFF[a, 0]), float(STIFF[a, last])) for a in range(NP)]
    w0 = float(WEIGHTS[0])
    for b in range(NP):
        wb = float(WEIGHTS[b]) * grid.w
        more = wb * extra[b]
        for a in range(1, last):
            r = rows(a, b)
            value = rhs_ref[r, :]
            v0_ref[r, :] = value
            v1_ref[r, :] = part_ref[r, :] + pull[a] * more + massed_ref[r, :] * value
        r_low, r_high = rows(0, b), rows(last, b)
        low = rhs_ref[r_low, :] + jnp.where(grid.lower, extra[b], 0.0)
        high = rhs_ref[r_high, :] + jnp.where(grid.lower, 0.0, extra[b])
        v0_ref[r_low, :] = low
        v0_ref[r_high, :] = high
        face = jnp.where(grid.lower, low, high)
        theirs = slopes[b] + w0 * (flat0_ref[pl.ds(NP * b, NP), :] + flat[b])
        theirs = theirs + wb * ((float(STIFF[0, 0]) + w0 * reactions[b]) * face)
        end = w0 * flat[b] + jnp.where(nb, theirs, 0.0)
        v1_low = part_ref[r_low, :] + pull[0] * more + massed_ref[r_low, :] * low
        v1_high = part_ref[r_high, :] + pull[last] * more + massed_ref[r_high, :] * high
        v1_ref[r_low, :] = v1_low + jnp.where(grid.lower, end, 0.0)
        v1_ref[r_high, :] = v1_high + jnp.where(grid.lower, 0.0, end)
    grid.assemble(v1_ref)
    grid.local(v1_ref, massed_ref, v2_ref, tmp_ref)
    weight = grid.count_weights()
    parts = [[], [], [], []]
    kinds = {}
    for a in range(NP):
        for b in range(NP):
            kinds.setdefault((place(a), place(b)), []).append(rows(a, b))
    for (i, j), where_in in kinds.items():
        terms = [[], [], [], []]
        for r in where_in:
            v0, v1, v2 = v0_ref[r, :], v1_ref[r, :], v2_ref[r, :]
            for t, value in zip(terms, (v0 * v0, v1 * v0, v1 * v1, v1 * v2)):
                t.append(value)
        for k, t in enumerate(terms):
            total = sum_of(t)
            parts[k].append(total if k == 3 else weight[i][j] * total)
    row = grid.row
    out = jnp.zeros((NP, lanes), jnp.float32)
    for k, p in enumerate(parts):
        total = jnp.sum(sum_of(p), axis=0, keepdims=True)
        out = jnp.where(row == k, jnp.broadcast_to(total, (NP, lanes)), out)
    msg_a_ref[HALF : HALF + NP, :] = out
    msg_b_ref[HALF : HALF + NP, :] = out
    grid.assemble(v2_ref)

    def write(b, first, second):
        msg_a_ref[pl.ds(NP * b, NP), :] = first
        msg_b_ref[pl.ds(NP * b, NP), :] = second

    pack_face(
        grid,
        [jnp.where(grid.lower, v2_ref[rows(0, b), :], v2_ref[rows(last, b), :]) for b in range(NP)],
        write,
    )


def own_kernel(per, wide, *refs):
    *in_refs, scratch_ref = refs
    vector_refs, out_refs = in_refs[:3], in_refs[3:]
    lanes = vector_refs[0].shape[1]
    grid = Grid(lanes, wide)
    mine = pl.ds(pl.multiple_of(lax.axis_index("narrow") * per, per), per)
    weight = grid.count_weights()
    inverse = 1.0 / grid.w
    weight = [[w * inverse for w in line] for line in weight]
    for q in range(PTS // LANES):
        lines = []
        for r in range(LANES // NP):
            at = q * LANES + NP * r
            a, b = at // PLANE, (at % PLANE) // NP
            lines.append(float(1.0 / (WEIGHTS[a] * WEIGHTS[b])) * weight[place(a)][place(b)])
        scale = jnp.concatenate(lines, axis=0)
        fields = [ref[q * LANES : (q + 1) * LANES, :] for ref in vector_refs] + [scale]
        for k, (field, ref) in enumerate(zip(fields, out_refs)):
            for t in range(lanes // LANES):
                scratch_ref[k, t * LANES : (t + 1) * LANES, :] = jnp.transpose(
                    field[:, t * LANES : (t + 1) * LANES]
                )
            ref[:, q * LANES : (q + 1) * LANES] = scratch_ref[k, mine, :]


def last_kernel(
    wide,
    v0_ref,
    v1_ref,
    v2_ref,
    scale_ref,
    got_a_ref,
    got_b_ref,
    twin_b_ref,
    sums_ref,
    solution_ref,
    strong_ref,
    face_ref,
    turned_ref,
):
    per = v0_ref.shape[0]
    lanes = got_a_ref.shape[1]
    grid = Grid(lanes, wide)
    nb = grid.has_neighbour()
    v = lax.axis_index("narrow")
    core = v % 2
    extra = unpack_face(
        grid,
        lambda b: got_a_ref[pl.ds(NP * b, NP), :],
        lambda b: jnp.where(
            core == 0, twin_b_ref[pl.ds(NP * b, NP), :], got_b_ref[pl.ds(NP * b, NP), :]
        ),
        nb,
    )
    for b in range(NP):
        face_ref[pl.ds(NP * b, NP), :] = extra[b]
        face_ref[pl.ds(PLANE + NP * b, NP), :] = extra[b]
    for t in range(lanes // LANES):
        turned_ref[t * LANES : (t + 1) * LANES, :] = jnp.transpose(
            face_ref[:, t * LANES : (t + 1) * LANES]
        )
    face = turned_ref[pl.ds(pl.multiple_of(v * per, per), per), :]
    spot = lax.broadcasted_iota(jnp.int32, (per, LANES), 1)
    layer = lax.broadcasted_iota(jnp.int32, (per, LANES), 0) // XSTEP
    ends = {
        0: jnp.where((spot < PLANE) & (layer == 0), face, 0.0),
        PTS // LANES - 1: jnp.where((spot >= PLANE) & (layer == BX - 1), face, 0.0),
    }
    g = [jnp.sum(sums_ref[k : k + 1, :], axis=1, keepdims=True) for k in range(4)]
    alpha = g[0] / g[1]
    norm = g[0] - 2.0 * alpha * g[1] + (alpha * alpha) * g[2]
    beta = norm / g[0]
    one = 1.0 + beta
    curve = one * one * g[1] - 2.0 * one * alpha * g[2] + (alpha * alpha) * g[3]
    step = norm / curve
    first = jnp.broadcast_to(alpha + step * one, (per, LANES))
    second = jnp.broadcast_to(alpha * step, (per, LANES))
    for q in range(PTS // LANES):
        at = (slice(None), slice(q * LANES, (q + 1) * LANES))
        v0, v1, v2 = v0_ref[at], v1_ref[at], v2_ref[at]
        if q in ends:
            v2 = v2 + ends[q]
        solution_ref[at] = first * v0 - second * v1
        strong_ref[at] = (v0 - first * v1 + second * v2) * scale_ref[at]


VM = pl.BlockSpec(memory_space=pltpu.VMEM)


def call(kernel, out_shapes, in_specs, scratch=()):
    return pl.pallas_call(
        kernel,
        out_shape=[
            jax.ShapeDtypeStruct(*(s if isinstance(s[0], tuple) else (s, jnp.float32)))
            for s in out_shapes
        ],
        in_specs=in_specs,
        out_specs=[VM] * len(out_shapes),
        scratch_shapes=list(scratch),
        compiler_params=pltpu.CompilerParams(vmem_limit_bytes=16 * 1024 * 1024),
    )


def in_hbm(*arrays):
    return [pltpu.with_memory_space_constraint(x, pltpu.HBM) for x in arrays]


def swap(x, wide, narrow, *partner_of):
    pairs = []
    for u in range(wide):
        to = [partner(u) for partner in partner_of]
        idle = [not 0 <= t < wide for t in to]
        for v in range(narrow):
            k = v % len(to)
            away = v ^ 1 if all(idle) else v ^ 2
            target = u * narrow + away if idle[k] else to[k] * narrow + v
            pairs.append((u * narrow + v, target))
    return lax.ppermute(x, ("wide", "narrow"), pairs)


def same_pair(u):
    return u ^ 1


def next_pair(u):
    return u + 1 if u % 2 else u - 1


def far_copy(x, narrow):
    if narrow != 4:
        return list(lax.all_gather(x, "narrow"))
    return [x, lax.ppermute(x, "narrow", [(v, v ^ 2) for v in range(narrow)])]


def near_copies(blocks, narrow):
    if narrow != 4:
        return blocks
    return blocks + [twin(x, narrow) for x in blocks]


def twin(x, narrow):
    return lax.ppermute(x, "narrow", [(v, v ^ 1) for v in range(narrow)])


def finish(msg_a, msg_b, wide, narrow):
    sums = msg_a[HALF:]
    if wide == 8:
        got_b = swap(msg_b, wide, narrow, lambda u: u ^ 4, next_pair)
        more = swap(sums, wide, narrow, lambda u: u ^ 2, lambda u: u ^ 6)
        twin_b = twin(got_b[:HALF], narrow)
        even = lax.axis_index("narrow") % 2 == 0
        part = more + jnp.where(even, sums + got_b[HALF:], 0.0)
        got_a = swap(jnp.concatenate([msg_a[:HALF], part], axis=0), wide, narrow, same_pair)
        cross = [
            (u * narrow + v, (u ^ 1) * narrow + (v ^ 1)) for u in range(wide) for v in range(narrow)
        ]
        theirs = got_a[HALF:] + lax.ppermute(part, ("wide", "narrow"), cross)
        total = (part + twin(part, narrow)) + theirs
        return got_a[:HALF], got_b[:HALF], twin_b, total
    got_a = swap(msg_a, wide, narrow, same_pair)
    got_b = swap(msg_b, wide, narrow, next_pair)[:HALF]
    return got_a[:HALF], got_b, got_b, lax.psum(sums, "wide")


def local(wide, narrow, source_old, reaction_old, new_place):
    per = source_old.shape[1]
    lanes = per * narrow
    blocks = PTS // LANES
    early, late = call(
        pack_kernel,
        [(per * (blocks + 1) + NP, LANES), (per * blocks, LANES)],
        [pl.BlockSpec(memory_space=pltpu.HBM)] * 3,
        [pltpu.VMEM((1, per), jnp.int32), pltpu.SemaphoreType.DMA((2 * blocks + 1,))],
    )(*in_hbm(source_old.T, reaction_old.T, new_place.reshape(1, per)))
    full = (PTS, lanes)
    late = far_copy(late, narrow)
    early = near_copies(far_copy(early, narrow), narrow)
    rhs, came, msg = call(
        functools.partial(first_kernel, per, narrow, wide),
        [full, ((NP, lanes), jnp.int32), (3 * HALF, lanes)],
        [VM] * narrow,
        [pltpu.VMEM((2 * PLANE, lanes), jnp.float32)],
    )(*early)
    mine = swap(msg, wide, narrow, same_pair, next_pair)
    other = twin(mine, narrow)
    part, flat = call(
        functools.partial(middle_kernel, wide),
        [full, (PLANE, lanes)],
        [VM],
        [pltpu.VMEM((PLANE, lanes), jnp.float32)],
    )(rhs)
    late, came = lax.optimization_barrier((late, came))
    late = near_copies(late, narrow)
    massed = call(
        functools.partial(reaction_kernel, per, narrow, wide), [full], [VM] * (narrow + 1)
    )(*late, came)[0]
    v0, v1, v2, msg_a, msg_b = call(
        functools.partial(second_kernel, wide),
        [full, full, full, (HALF + NP, lanes), (HALF + NP, lanes)],
        [VM] * 6,
        [pltpu.VMEM((PLANE, lanes), jnp.float32), pltpu.VMEM((PLANE, lanes), jnp.float32)],
    )(rhs, massed, part, flat, mine, other)
    arrived = finish(msg_a, msg_b, wide, narrow)
    own = call(
        functools.partial(own_kernel, per, wide),
        [(per, PTS)] * 4,
        [VM] * 3,
        [pltpu.VMEM((4, lanes, LANES), jnp.float32)],
    )(v0, v1, v2)
    out = call(
        functools.partial(last_kernel, wide),
        [(per, PTS), (per, PTS)],
        [VM] * 8,
        [pltpu.VMEM((LANES, lanes), jnp.float32), pltpu.VMEM((lanes, LANES), jnp.float32)],
    )(*own, *arrived)
    return tuple(x.T for x in out)


def solution(mesh):
    placed = (P(None, ("wide", "narrow")), P(None, ("wide", "narrow")), P(("wide", "narrow")))
    return jax.shard_map(
        functools.partial(local, mesh.shape["wide"], mesh.shape["narrow"]),
        mesh=mesh,
        in_specs=placed,
        out_specs=(P(None, ("wide", "narrow")), P(None, ("wide", "narrow"))),
        check_vma=False,
    )
```
